32 devices in a mesh: grp: 2 (over core), rep: 16 (over z, y, x).
Axes of the slice: x: 2, y: 2, z: 4, core: 2. Of those that a mesh axis runs over, the one named last changes fastest.
Arguments:
- tokens: bfloat16 [16, 1024, 1152], P('rep', 'grp'), may hold values from -6 to 6
- cotangent: bfloat16 [16, 1024, 1152], P('rep', 'grp'), may hold values from -6 to 6
- segment_ids: int32 [16, 1024], P('rep'), may hold values from 0 to 3, never falling along the last dimension, each value on 1 to 800 neighbouring positions
- adapter_ids: int32 [16], P('rep'), may hold values from 0 to 7
- norm_gains: bfloat16 [2, 1152], P(None, 'grp'), may hold values from 0.5 to 1.5
- frozen_qkv: bfloat16 [1152, 1920], P('grp'), may hold values from -0.1875 to 0.1875
- frozen_out: bfloat16 [1152, 1152], P('grp'), may hold values from -1.5 to 1.5
- frozen_gate_up: bfloat16 [1152, 6144], P('grp'), may hold values from -0.1875 to 0.1875
- frozen_down: bfloat16 [3072, 1152], P('grp'), may hold values from -0.109375 to 0.109375
- lower_mats: bfloat16 [6, 8, 1152, 16], replicated, may hold values from -0.1875 to 0.1875
- lower_down: bfloat16 [8, 3072, 16], replicated, may hold values from -0.109375 to 0.109375
- upper_width: bfloat16 [3, 8, 16, 1152], replicated, may hold values from -1 to 1
- upper_keys: bfloat16 [2, 8, 16, 384], replicated, may hold values from -1 to 1
- upper_hidden: bfloat16 [2, 8, 16, 3072], replicated, may hold values from -1 to 1
Outputs:
- layer_out: bfloat16 [16, 1024, 1152], P('rep', 'grp')
- input_grad: bfloat16 [16, 1024, 1152], P('rep', 'grp')
- lower_grad: float32 [6, 8, 1152, 16], P(None, 'grp', 'rep')
- lower_down_grad: float32 [8, 3072, 16], P('grp', 'rep')
- upper_width_grad: float32 [3, 8, 16, 1152], P(None, 'grp', None, 'rep')
- upper_keys_grad: float32 [2, 8, 16, 384], P(None, 'grp', None, 'rep')
- upper_hidden_grad: float32 [2, 8, 16, 3072], P(None, 'grp', None, 'rep')
The draws below stay inside these ranges and needn't reach their ends.
Inputs may be any that keep to these rules, and one draw needn't show every extreme that they name: `segment_ids`: within each sequence the ids never fall, each document has 1 to 800 positions, and one has exactly 800.
All inputs are finite; a program needn't handle non-finite values.
Results may differ from the reference program's by a relative error of at most 0.018.
Values may be sent and summed in bfloat16 or wider, within the bound.
No kernel may reach another device: no remote copies, remote signals or barrier semaphores. Data moves between devices by JAX's collectives and lax.ppermute only.
A program may use at most 192 MiB of HBM per device.

```python
import math
import jax
import jax.numpy as jnp
import numpy as np
from jax import lax

D = 1152
H = 18
KVH = 6
HD = 64
FF = 3072
R = 16
NAD = 8
KV = 384
LENGTH = 1024
NSEQ = 16
DOCS = 4
DOC_MOST = 800


def place_ends(values, own_key, smallest, high):
    spot = [jax.random.randint(jax.random.fold_in(own_key, axis), (), 0, length) for axis, length in enumerate(values.shape)]
    widest = values.shape.index(max(values.shape))
    next_to = spot[:widest] + [(spot[widest] + 1) % values.shape[widest]] + spot[widest + 1:]
    return values.at[tuple(spot)].set(smallest).at[tuple(next_to)].set(high)


def level_of(stream_key, dims, pieces, least, top_value):
    loudness, own = 1.0, jax.random.fold_in(stream_key, 6)
    for dim, blocks in pieces:
        steps = jnp.exp(jax.random.uniform(jax.random.fold_in(own, dim), (blocks,), jnp.float32, least / len(pieces), top_value / len(pieces)))
        loudness = loudness * jnp.repeat(steps, dims[dim] // blocks).reshape([-1 if axis == dim else 1 for axis in range(len(dims))])
    return loudness


def length_profile(count, total, bound, slope):
    loads = [(1 << 20) // math.isqrt(rank ** slope) + 1 for rank in range(2, count + 1)]
    surplus, given = total - bound - (count - 1), [1] * (count - 1)
    while surplus > 0:
        movable = [i for i in range(count - 1) if given[i] < bound]
        pool, remaining = sum([loads[i] for i in movable]), surplus
        for i in movable:
            more = min(bound - given[i], max(1, remaining * loads[i] // pool), surplus)
            given[i] = given[i] + more
            surplus = surplus - more
    return np.array([bound] + given)


def ragged(key, count, total, most, skew):
    if count == 2:
        one = jax.random.randint(key, (), max(1, total - most), min(most, total - 1) + 1)
        return jnp.stack([one, total - one])
    sizes = jnp.asarray(length_profile(count, total, most, skew), jnp.int32)
    couples = (count - 1) // 2
    giver, receiver = sizes[1:1 + 2 * couples:2], sizes[2:2 + 2 * couples:2]
    slack = jnp.minimum(giver - 1, most - receiver)
    moved = jax.random.randint(jax.random.fold_in(key, 1), (couples,), 0, 1 << 20) % (slack + 1)
    sizes = sizes.at[1:1 + 2 * couples:2].set(giver - moved).at[2:2 + 2 * couples:2].set(receiver + moved)
    return sizes[jax.random.permutation(jax.random.fold_in(key, 2), count)]


def normal_values(stream_key, shape, deviation, most, pieces=(), kind=jnp.bfloat16):
    values = jax.random.normal(stream_key, shape, jnp.float32) * deviation
    if len(pieces) > 0:
        values = level_of(stream_key, shape, pieces, -0.22, 0.18) * values
    return jnp.clip(values, min=-most, max=most).astype(kind)


def setup_inputs(seed: int = 0) -> dict:
    arg_keys = jax.random.split(jax.random.key(seed), 15)
    return {
        "tokens": normal_values(arg_keys[0], (NSEQ, LENGTH, D), 1.0, 6.0, ((0, 16), (1, 2))),
        "cotangent": normal_values(arg_keys[1], (NSEQ, LENGTH, D), 1.0, 6.0, ((0, 16), (1, 2))),
        "segment_ids": jax.vmap(lambda own: jnp.searchsorted(jnp.cumsum(ragged(own, DOCS, LENGTH, DOC_MOST, 2)), jnp.arange(LENGTH), side="right"))(jax.random.split(arg_keys[2], NSEQ)).reshape((NSEQ, LENGTH)).astype(jnp.int32),
        "adapter_ids": place_ends(jax.random.randint(arg_keys[3], (NSEQ,), 0, NAD), jax.random.fold_in(arg_keys[3], 1), 0, NAD - 1).astype(jnp.int32),
        "norm_gains": jnp.clip(1.0 + 0.1 * jax.random.normal(arg_keys[4], (2, D), jnp.float32), 0.5, 1.5).astype(jnp.bfloat16),
        "frozen_qkv": normal_values(arg_keys[5], (D, D + 2 * KV), D ** -0.5, 0.1875, ((0, 2),)),
        "frozen_out": normal_values(arg_keys[6], (D, D), (D // 64) ** -0.5, 1.5, ((0, 2),)),
        "frozen_gate_up": normal_values(arg_keys[7], (D, 2 * FF), D ** -0.5, 0.1875, ((0, 2),)),
        "frozen_down": normal_values(arg_keys[8], (FF, D), FF ** -0.5, 0.109375, ((0, 2),)),
        "lower_mats": normal_values(arg_keys[9], (6, NAD, D, R), D ** -0.5, 0.1875),
        "lower_down": normal_values(arg_keys[10], (NAD, FF, R), FF ** -0.5, 0.109375),
        "upper_width": normal_values(arg_keys[11], (3, NAD, R, D), (2 * R) ** -0.5, 1.0),
        "upper_keys": normal_values(arg_keys[12], (2, NAD, R, KV), (2 * R) ** -0.5, 1.0),
        "upper_hidden": normal_values(arg_keys[13], (2, NAD, R, FF), (2 * R) ** -0.5, 1.0),
    }


@jax.custom_vjp
def low(v):
    return lax.optimization_barrier(v.astype(jnp.bfloat16)).astype(jnp.float32)

@jax.custom_vjp
def low_back(v):
    return v

def low_keep(v):
    return (low(v), None)

def low_pass(kept, grad):
    return (grad,)

def back_keep(v):
    return (v, None)

def back_low(kept, grad):
    return (low(grad),)
low.defvjp(low_keep, low_pass)
low_back.defvjp(back_keep, back_low)
epsilon = 1e-05
theta_base = 10000.0
highest = lax.Precision.HIGHEST
masked_value = -1e+30

def matmul(left, right):
    return jnp.dot(left, right, precision=highest, preferred_element_type=jnp.float32)

def normalize(rows, gain_row):
    return rows * lax.rsqrt(lax.optimization_barrier(jnp.mean(rows * rows, axis=-1, keepdims=True)) + epsilon) * gain_row

def positions_of(segments):
    places = jnp.arange(segments.shape[0], dtype=jnp.int32)
    change = jnp.concatenate([jnp.ones((1,), jnp.bool_), segments[1:] != segments[:-1]])
    starts = lax.cummax(jnp.where(change, places, 0), axis=0)
    return places - starts

def angles(positions, head_size):
    half_size = head_size // 2
    freqs = theta_base ** (-jnp.arange(half_size, dtype=jnp.float32) * 2.0 / head_size)
    turned = positions.astype(jnp.float32)[:, None] * freqs[None, :]
    return (jnp.cos(turned)[:, None, :], jnp.sin(turned)[:, None, :])

def rotate(rows, cosine, sine):
    half_size = rows.shape[-1] // 2
    first = rows[..., :half_size]
    second = rows[..., half_size:]
    return jnp.concatenate([first * cosine - second * sine, second * cosine + first * sine], axis=-1)

def adapted(source, frozen, lower, upper):
    inner = low(low_back(matmul(source, lower)))
    return low_back(matmul(source, frozen) + matmul(inner, upper))

def attention(queries, key_rows, value_rows, segments):
    length = queries.shape[0]
    grouped = queries.reshape(length, KVH, H // KVH, HD)
    scores = jnp.einsum('qkgd,skd->kgqs', grouped, key_rows, precision=highest) * HD ** (-0.5)
    scores = low_back(scores)
    places = jnp.arange(length)
    allowed = (places[None, :] <= places[:, None]) & (segments[None, :] == segments[:, None])
    scores = jnp.where(allowed, scores, masked_value)
    row_max = lax.optimization_barrier(jnp.max(scores, axis=-1, keepdims=True))
    weights = jnp.exp(scores - row_max)
    chances = low(weights / lax.optimization_barrier(jnp.sum(weights, axis=-1, keepdims=True)))
    blended = jnp.einsum('kgqs,skd->qkgd', chances, value_rows, precision=highest)
    return blended.reshape(length, H * HD)

def sequence_forward(hidden, frozen_set, adapter_set, segments, chosen):
    norm_gains, frozen_qkv, frozen_out, frozen_gate_up, frozen_down = frozen_set
    lower_mats, lower_down, upper_width, upper_keys, upper_hidden = adapter_set
    lower_pick = lower_mats[:, chosen]
    lower_last = lower_down[chosen]
    width_pick = upper_width[:, chosen]
    keys_pick = upper_keys[:, chosen]
    hidden_pick = upper_hidden[:, chosen]
    cosine, sine = angles(positions_of(segments), HD)
    length = hidden.shape[0]
    normed = low(normalize(hidden, norm_gains[0]))
    query_lin = adapted(normed, frozen_qkv[:, :D], lower_pick[0], width_pick[0])
    key_lin = adapted(normed, frozen_qkv[:, D:D + KV], lower_pick[1], keys_pick[0])
    value_lin = adapted(normed, frozen_qkv[:, D + KV:], lower_pick[2], keys_pick[1])
    queries = low(rotate(query_lin.reshape(length, H, HD), cosine, sine))
    key_rows = low(rotate(key_lin.reshape(length, KVH, HD), cosine, sine))
    value_rows = low(value_lin.reshape(length, KVH, HD))
    blended = low(low_back(attention(queries, key_rows, value_rows, segments)))
    branch = adapted(blended, frozen_out, lower_pick[3], width_pick[1])
    middle = hidden + branch
    normed_two = low(normalize(middle, norm_gains[1]))
    gate_lin = adapted(normed_two, frozen_gate_up[:, :FF], lower_pick[4], hidden_pick[0])
    up_lin = adapted(normed_two, frozen_gate_up[:, FF:], lower_pick[5], hidden_pick[1])
    active = low(jax.nn.silu(gate_lin) * up_lin)
    return middle + adapted(active, frozen_down, lower_last, width_pick[2])

def reference(tokens, cotangent, segment_ids, adapter_ids, norm_gains, frozen_qkv, frozen_out, frozen_gate_up, frozen_down, lower_mats, lower_down, upper_width, upper_keys, upper_hidden):
    frozen_set = tuple((item.astype(jnp.float32) for item in (norm_gains, frozen_qkv, frozen_out, frozen_gate_up, frozen_down)))
    adapter_set = tuple((item.astype(jnp.float32) for item in (lower_mats, lower_down, upper_width, upper_keys, upper_hidden)))

    def one_sequence(totals, item):
        sequence, grad_rows, segments, chosen = item

        def forward(hidden, adapters):
            return sequence_forward(hidden, frozen_set, adapters, segments, chosen)
        result, pullback = jax.vjp(forward, sequence.astype(jnp.float32), adapter_set)
        grad_hidden, grad_adapters = pullback(grad_rows.astype(jnp.float32))
        totals = jax.tree.map(lambda total, extra: total + extra, totals, grad_adapters)
        return (totals, (result.astype(jnp.bfloat16), grad_hidden.astype(jnp.bfloat16)))
    zeros = tuple((jnp.zeros(item.shape, jnp.float32) for item in adapter_set))
    totals, (layer_out, input_grad) = lax.scan(one_sequence, zeros, (tokens, cotangent, segment_ids, adapter_ids))
    return (layer_out, input_grad, totals[0], totals[1], totals[2], totals[3], totals[4])
```

```python
import jax
import jax.numpy as jnp
from jax import lax
from jax.sharding import PartitionSpec as P

D = 1152
H = 18
KVH = 6
HD = 64
FF = 3072
R = 16
NAD = 8
KV = 384


epsilon = 1e-05
theta_base = 10000.0
masked_value = -1e30


def passed_along(value, axis, by):
    size = lax.axis_size(axis)
    pairs = [(i, i + by) for i in range(size) if 0 <= i + by < size]
    return lax.ppermute(value, axis, pairs)


def contract(form, left, right):
    return jnp.einsum(form, left, right, preferred_element_type=jnp.float32)


def normalize(rows, gain_row):
    return rows * lax.rsqrt(jnp.mean(rows * rows, axis=-1, keepdims=True) + epsilon) * gain_row


def positions_of(segments):
    places = jnp.arange(segments.shape[0], dtype=jnp.int32)
    change = jnp.concatenate([jnp.ones((1,), jnp.bool_), segments[1:] != segments[:-1]])
    starts = lax.cummax(jnp.where(change, places, 0), axis=0)
    return places - starts


def angles(positions, head_size):
    half_size = head_size // 2
    freqs = theta_base ** (-jnp.arange(half_size, dtype=jnp.float32) * 2.0 / head_size)
    turned = positions.astype(jnp.float32)[:, None] * freqs[None, :]
    return (jnp.cos(turned)[:, None, :], jnp.sin(turned)[:, None, :])


def rotate(rows, cosine, sine):
    half_size = rows.shape[-1] // 2
    first = rows[..., :half_size]
    second = rows[..., half_size:]
    return jnp.concatenate(
        [first * cosine - second * sine, second * cosine + first * sine], axis=-1
    )


def per_device(
    tokens,
    cotangent,
    segment_ids,
    adapter_ids,
    norm_gains,
    frozen_qkv,
    frozen_out,
    frozen_gate_up,
    frozen_down,
    lower_mats,
    lower_down,
    upper_width,
    upper_keys,
    upper_hidden,
):
    chosen = adapter_ids[0]
    segments = segment_ids[0]
    tok_rows = tokens.shape[1]
    groups = H // KVH
    factor = HD ** (-0.5)
    offset = lax.axis_index("grp") * tok_rows
    gains_all, qkv_full, out_full, gate_up_full, down_full = (
        lax.all_gather(norm_gains, "grp", axis=1, tiled=True),
        lax.all_gather(frozen_qkv, "grp", axis=0, tiled=True),
        lax.all_gather(frozen_out, "grp", axis=0, tiled=True),
        lax.all_gather(frozen_gate_up, "grp", axis=0, tiled=True),
        lax.all_gather(frozen_down, "grp", axis=0, tiled=True),
    )
    lower_pick = lax.dynamic_index_in_dim(lower_mats, chosen, 1, keepdims=False)
    lower_last = lax.dynamic_index_in_dim(lower_down, chosen, 0, keepdims=False)
    width_pick = lax.dynamic_index_in_dim(upper_width, chosen, 1, keepdims=False)
    keys_pick = lax.dynamic_index_in_dim(upper_keys, chosen, 1, keepdims=False)
    hidden_pick = lax.dynamic_index_in_dim(upper_hidden, chosen, 1, keepdims=False)
    positions = lax.dynamic_slice_in_dim(positions_of(segments), offset, tok_rows)
    cosine, sine = angles(positions, HD)
    padded_segs = jnp.concatenate([jnp.full((tok_rows,), -1, jnp.int32), segments])
    key_segs = lax.dynamic_slice_in_dim(padded_segs, offset, 2 * tok_rows)
    query_segs = lax.dynamic_slice_in_dim(segments, offset, tok_rows)
    query_place = offset + jnp.arange(tok_rows, dtype=jnp.int32)
    key_place = offset - tok_rows + jnp.arange(2 * tok_rows, dtype=jnp.int32)
    allowed = (key_place[None, :] <= query_place[:, None]) & (
        key_segs[None, :] == query_segs[:, None]
    )
    hidden = tokens[0].astype(jnp.float32)
    gain_one = gains_all[0].astype(jnp.float32)
    gain_two = gains_all[1].astype(jnp.float32)
    normed = normalize(hidden, gain_one).astype(jnp.bfloat16)
    qkv_lower = jnp.concatenate([lower_pick[0], lower_pick[1], lower_pick[2]], axis=1)
    inner_qkv = jnp.dot(normed, qkv_lower, preferred_element_type=jnp.float32).astype(jnp.bfloat16)
    base_qkv = jnp.dot(normed, qkv_full, preferred_element_type=jnp.float32)
    query_lin = base_qkv[:, :D] + jnp.dot(
        inner_qkv[:, :R], width_pick[0], preferred_element_type=jnp.float32
    )
    key_lin = base_qkv[:, D : D + KV] + jnp.dot(
        inner_qkv[:, R : 2 * R], keys_pick[0], preferred_element_type=jnp.float32
    )
    value_lin = base_qkv[:, D + KV :] + jnp.dot(
        inner_qkv[:, 2 * R :], keys_pick[1], preferred_element_type=jnp.float32
    )
    queries = rotate(query_lin.reshape(tok_rows, H, HD), cosine, sine).astype(jnp.bfloat16)
    key_flat = (
        rotate(key_lin.reshape(tok_rows, KVH, HD), cosine, sine)
        .astype(jnp.bfloat16)
        .reshape(tok_rows, KV)
    )
    value_flat = value_lin.astype(jnp.bfloat16)
    prev_keys, prev_values = passed_along((key_flat, value_flat), "grp", 1)
    all_keys = (
        jnp.concatenate([prev_keys, key_flat], axis=0)
        .reshape(2 * tok_rows, KVH, HD)
        .transpose(1, 0, 2)
    )
    all_values = (
        jnp.concatenate([prev_values, value_flat], axis=0)
        .reshape(2 * tok_rows, KVH, HD)
        .transpose(1, 0, 2)
    )
    grouped = queries.reshape(tok_rows, KVH, groups, HD).transpose(1, 0, 2, 3)

    def head_forward(operands):
        query_block, key_block, value_block = operands
        scores = contract("tgd,sd->gts", query_block, key_block) * factor
        scores = jnp.where(allowed[None], scores, masked_value)
        row_max = jnp.max(scores, axis=-1, keepdims=True)
        weights = jnp.exp(scores - row_max)
        row_total = jnp.sum(weights, axis=-1, keepdims=True)
        chances = (weights / row_total).astype(jnp.bfloat16)
        blended = contract("gts,sd->tgd", chances, value_block)
        return (blended, row_max[..., 0] + jnp.log(row_total[..., 0]))

    blended, log_total = lax.map(head_forward, (grouped, all_keys, all_values))
    attn_mix = blended.transpose(1, 0, 2, 3).reshape(tok_rows, D).astype(jnp.bfloat16)
    inner_out = jnp.dot(attn_mix, lower_pick[3], preferred_element_type=jnp.float32).astype(
        jnp.bfloat16
    )
    branch = jnp.dot(attn_mix, out_full, preferred_element_type=jnp.float32) + jnp.dot(
        inner_out, width_pick[1], preferred_element_type=jnp.float32
    )
    middle = hidden + branch
    normed_two = normalize(middle, gain_two).astype(jnp.bfloat16)
    ff_lower = jnp.concatenate([lower_pick[4], lower_pick[5]], axis=1)
    inner_ff = jnp.dot(normed_two, ff_lower, preferred_element_type=jnp.float32).astype(
        jnp.bfloat16
    )
    base_ff = jnp.dot(normed_two, gate_up_full, preferred_element_type=jnp.float32)
    gate_lin = base_ff[:, :FF] + jnp.dot(
        inner_ff[:, :R], hidden_pick[0], preferred_element_type=jnp.float32
    )
    up_lin = base_ff[:, FF:] + jnp.dot(
        inner_ff[:, R:], hidden_pick[1], preferred_element_type=jnp.float32
    )
    active = (jax.nn.silu(gate_lin) * up_lin).astype(jnp.bfloat16)
    inner_down = jnp.dot(active, lower_last, preferred_element_type=jnp.float32).astype(
        jnp.bfloat16
    )
    result = (
        middle
        + jnp.dot(active, down_full, preferred_element_type=jnp.float32)
        + jnp.dot(inner_down, width_pick[2], preferred_element_type=jnp.float32)
    )
    layer_out = result.astype(jnp.bfloat16)[None]
    gains_all, qkv_full, out_full, gate_up_full, down_full = (
        lax.all_gather(norm_gains, "grp", axis=1, tiled=True),
        lax.all_gather(frozen_qkv, "grp", axis=0, tiled=True),
        lax.all_gather(frozen_out, "grp", axis=0, tiled=True),
        lax.all_gather(frozen_gate_up, "grp", axis=0, tiled=True),
        lax.all_gather(frozen_down, "grp", axis=0, tiled=True),
    )
    gain_one = gains_all[0].astype(jnp.float32)
    gain_two = gains_all[1].astype(jnp.float32)
    cot_rows = cotangent[0]
    grad_out = cot_rows.astype(jnp.float32)
    width_down_grad = contract("tr,td->rd", inner_down, cot_rows)
    grad_inner_down = contract("td,rd->tr", cot_rows, width_pick[2]).astype(jnp.bfloat16)
    down_lower_grad = contract("tf,tr->fr", active, grad_inner_down)
    grad_active = contract("td,fd->tf", cot_rows, down_full) + contract(
        "tr,fr->tf", grad_inner_down, lower_last
    )
    sigmoid_gate = jax.nn.sigmoid(gate_lin)
    grad_gate = (
        grad_active * up_lin * sigmoid_gate * (1.0 + gate_lin * (1.0 - sigmoid_gate))
    ).astype(jnp.bfloat16)
    grad_up = (grad_active * gate_lin * sigmoid_gate).astype(jnp.bfloat16)
    hidden_local = jnp.stack(
        [
            contract("tr,tf->rf", inner_ff[:, :R], grad_gate),
            contract("tr,tf->rf", inner_ff[:, R:], grad_up),
        ]
    )
    grad_inner_ff = jnp.concatenate(
        [
            contract("tf,rf->tr", grad_gate, hidden_pick[0]),
            contract("tf,rf->tr", grad_up, hidden_pick[1]),
        ],
        axis=1,
    ).astype(jnp.bfloat16)
    ff_lower_grad = contract("td,tr->dr", normed_two, grad_inner_ff)
    grad_ff = jnp.concatenate([grad_gate, grad_up], axis=1)
    grad_normed_two = contract("tf,df->td", grad_ff, gate_up_full) + contract(
        "tr,dr->td", grad_inner_ff, ff_lower
    )
    norm_two_back = jax.vjp(lambda rows: normalize(rows, gain_two), middle)[1]
    grad_middle = grad_out + norm_two_back(grad_normed_two)[0]
    ffn_lower_local = ff_lower_grad.reshape(D, 2, R).transpose(1, 0, 2)
    grad_branch = grad_middle.astype(jnp.bfloat16)
    width_out_grad = contract("tr,td->rd", inner_out, grad_branch)
    grad_inner_out = contract("td,rd->tr", grad_branch, width_pick[1]).astype(jnp.bfloat16)
    out_lower_grad = contract("td,tr->dr", attn_mix, grad_inner_out)
    grad_mix = (
        contract("te,de->td", grad_branch, out_full)
        + contract("tr,dr->td", grad_inner_out, lower_pick[3])
    ).astype(jnp.bfloat16)
    grad_grouped = grad_mix.reshape(tok_rows, KVH, groups, HD).transpose(1, 0, 2, 3)

    def head_backward(operands):
        query_block, key_block, value_block, grad_block, log_block = operands
        scores = contract("tgd,sd->gts", query_block, key_block) * factor
        chances = jnp.where(allowed[None], jnp.exp(scores - log_block[..., None]), 0.0)
        grad_chances = contract("tgd,sd->gts", grad_block, value_block)
        grad_scores = (
            chances * (grad_chances - jnp.sum(chances * grad_chances, axis=-1, keepdims=True))
        ).astype(jnp.bfloat16)
        grad_query = contract("gts,sd->tgd", grad_scores, key_block) * factor
        grad_key = contract("gts,tgd->sd", grad_scores, query_block) * factor
        grad_value = contract("gts,tgd->sd", chances.astype(jnp.bfloat16), grad_block)
        return (grad_query, grad_key, grad_value)

    grad_queries, grad_keys, grad_values = lax.map(
        head_backward, (grouped, all_keys, all_values, grad_grouped, log_total)
    )
    grad_queries = grad_queries.transpose(1, 0, 2, 3).reshape(tok_rows, H, HD)
    grad_keys = grad_keys.transpose(1, 0, 2).reshape(2 * tok_rows, KV)
    grad_values = grad_values.transpose(1, 0, 2).reshape(2 * tok_rows, KV)
    back_keys, back_values = (
        passed_along(grad_keys[:tok_rows].astype(jnp.bfloat16), "grp", -1).astype(jnp.float32),
        passed_along(grad_values[:tok_rows].astype(jnp.bfloat16), "grp", -1).astype(jnp.float32),
    )
    grad_key_sum = grad_keys[tok_rows:] + back_keys
    grad_value_sum = grad_values[tok_rows:] + back_values
    grad_query_lin = rotate(grad_queries, cosine, -sine).reshape(tok_rows, D).astype(jnp.bfloat16)
    grad_key_lin = (
        rotate(grad_key_sum.reshape(tok_rows, KVH, HD), cosine, -sine)
        .reshape(tok_rows, KV)
        .astype(jnp.bfloat16)
    )
    grad_value_lin = grad_value_sum.astype(jnp.bfloat16)
    width_query_grad = contract("tr,td->rd", inner_qkv[:, :R], grad_query_lin)
    keys_local = jnp.stack(
        [
            contract("tr,td->rd", inner_qkv[:, R : 2 * R], grad_key_lin),
            contract("tr,td->rd", inner_qkv[:, 2 * R :], grad_value_lin),
        ]
    )
    grad_inner_qkv = jnp.concatenate(
        [
            contract("td,rd->tr", grad_query_lin, width_pick[0]),
            contract("td,rd->tr", grad_key_lin, keys_pick[0]),
            contract("td,rd->tr", grad_value_lin, keys_pick[1]),
        ],
        axis=1,
    ).astype(jnp.bfloat16)
    qkv_lower_grad = contract("td,tr->dr", normed, grad_inner_qkv)
    grad_qkv = jnp.concatenate([grad_query_lin, grad_key_lin, grad_value_lin], axis=1)
    grad_normed = contract("te,de->td", grad_qkv, qkv_full) + contract(
        "tr,dr->td", grad_inner_qkv, qkv_lower
    )
    norm_one_back = jax.vjp(lambda rows: normalize(rows, gain_one), hidden)[1]
    grad_hidden = grad_middle + norm_one_back(grad_normed)[0]
    input_grad = grad_hidden.astype(jnp.bfloat16)[None]
    attn_lower_local = jnp.concatenate(
        [qkv_lower_grad.reshape(D, 3, R).transpose(1, 0, 2), out_lower_grad[None]], axis=0
    )
    attn_width_local = jnp.stack([width_query_grad, width_out_grad])
    lower_local = jnp.concatenate([attn_lower_local, ffn_lower_local], axis=0)
    width_local = jnp.concatenate([attn_width_local, width_down_grad[None]], axis=0)
    sums = summed_by_adapter(
        [
            lower_local.transpose(0, 2, 1),
            down_lower_grad.T[None],
            width_local,
            keys_local,
            hidden_local,
        ],
        chosen,
    )
    return (
        layer_out,
        input_grad,
        sums[0].transpose(0, 1, 3, 2),
        sums[1][0].transpose(0, 2, 1),
        sums[2],
        sums[3],
        sums[4],
    )


def summed_by_adapter(parts, chosen):
    reps = lax.axis_size("rep")
    pieces = [part.shape[-1] // reps for part in parts]
    blocks = [
        part.reshape(-1, reps, piece).transpose(1, 0, 2).reshape(reps, -1)
        for part, piece in zip(parts, pieces)
    ]
    mine = jnp.concatenate(blocks, axis=1)
    other = lax.ppermute(mine.astype(jnp.bfloat16), "grp", [(0, 1), (1, 0)])
    both = (mine + other.astype(jnp.float32)).astype(jnp.bfloat16)
    label = jnp.full((reps, 128), chosen, jnp.int32).astype(jnp.bfloat16)
    received = lax.all_to_all(
        jnp.concatenate([label, both], axis=1), "rep", 0, 0, tiled=True
    )
    quota = NAD // lax.axis_size("grp")
    wanted = lax.axis_index("grp") * quota + jnp.arange(quota, dtype=jnp.int32)
    picks = (received[:, 0].astype(jnp.int32)[None, :] == wanted[:, None]).astype(jnp.bfloat16)
    total = jnp.dot(picks, received[:, 128:], preferred_element_type=jnp.float32)
    outs = []
    start = 0
    for part, piece in zip(parts, pieces):
        count = part.shape[0] * part.shape[1] * piece
        outs.append(
            total[:, start : start + count]
            .reshape(quota, part.shape[0], part.shape[1], piece)
            .transpose(1, 0, 2, 3)
        )
        start += count
    return outs


def solution(mesh):
    return jax.shard_map(
        per_device,
        mesh=mesh,
        in_specs=(
            P("rep", "grp", None),
            P("rep", "grp", None),
            P("rep", None),
            P("rep"),
            P(None, "grp"),
            P("grp", None),
            P("grp", None),
            P("grp", None),
            P("grp", None),
            P(),
            P(),
            P(),
            P(),
            P(),
        ),
        out_specs=(
            P("rep", "grp", None),
            P("rep", "grp", None),
            P(None, "grp", "rep", None),
            P("grp", "rep", None),
            P(None, "grp", None, "rep"),
            P(None, "grp", None, "rep"),
            P(None, "grp", None, "rep"),
        ),
        check_vma=False,
    )
```

```python
import functools

import jax
import jax.numpy as jnp
from jax import lax
from jax.experimental import pallas as pl
from jax.experimental.pallas import tpu as pltpu
from jax.sharding import PartitionSpec as P

D = 1152
H = 18
KVH = 6
HD = 64
FF = 3072
R = 16
NAD = 8
KV = 384

HALF = D // 2
HEADS = H // 2
GROUP = H // KVH
QW = 640
KW = 256
SPAN = QW + 2 * KW
AUG = D + 128
TILE = 512
BLOCK = 256

epsilon = 1e-05
theta_base = 10000.0
masked_value = -1e30
f32 = jnp.float32
bf16 = jnp.bfloat16
SWAP = [(0, 1), (1, 0)]

ANY = pl.BlockSpec(memory_space=pl.ANY)
VMEM = pl.BlockSpec(memory_space=pltpu.VMEM)
SMEM = pl.BlockSpec(memory_space=pltpu.SMEM)


def nn(left, right):
    return jnp.dot(left, right, preferred_element_type=f32)


def nt(left, right):
    return lax.dot_general(left, right, (((1,), (1,)), ((), ())), preferred_element_type=f32)


def tn(left, right):
    return lax.dot_general(left, right, (((0,), (0,)), ((), ())), preferred_element_type=f32)


def lanes(shape):
    return lax.broadcasted_iota(jnp.int32, shape, len(shape) - 1)


def turned(rows, cosine, sine):
    first = lanes(rows.shape) % HD < HD // 2
    partner = jnp.where(first, pltpu.roll(rows, 128 - HD // 2, 1), pltpu.roll(rows, HD // 2, 1))
    return rows * cosine + partner * sine


def halves(pair_one, pair_two):
    low = lanes(pair_one.shape) < HD
    low_one = jnp.where(low, pair_one, 0.0)
    high_one = jnp.where(low, 0.0, pair_one)
    low_two = jnp.where(low, pair_two, 0.0)
    return (
        low_one,
        pltpu.roll(low_one, HD, 1),
        pltpu.roll(high_one, HD, 1),
        high_one,
        low_two,
        pltpu.roll(low_two, HD, 1),
    )


def attend_kernel(
    ids,
    tok_own,
    tok_oth,
    w_own,
    w_oth,
    b_win,
    at_qkv,
    gain,
    cosine,
    sine,
    starts,
    o_out,
    q_out,
    k_out,
    v_out,
    n_out,
    zt_out,
    lse_out,
    tok,
    normed,
    weight,
    query,
    keys,
    values,
    mixed,
    logs,
    sems,
    out_sems,
):
    g = ids[0]
    rows = tok_own.shape[0]
    here = pl.multiple_of(g * rows, 128)
    there = pl.multiple_of((1 - g) * rows, 128)
    w_here = pl.multiple_of(g * HALF, 64)
    w_there = pl.multiple_of((1 - g) * HALF, 64)
    loads = [
        pltpu.make_async_copy(tok_own, tok.at[pl.ds(here, rows)], sems.at[0]),
        pltpu.make_async_copy(tok_oth, tok.at[pl.ds(there, rows)], sems.at[1]),
        pltpu.make_async_copy(w_own, weight.at[pl.ds(w_here, HALF)], sems.at[2]),
        pltpu.make_async_copy(w_oth, weight.at[pl.ds(w_there, HALF)], sems.at[3]),
        pltpu.make_async_copy(b_win, weight.at[pl.ds(D, 128)], sems.at[4]),
    ]
    for load in loads:
        load.start()
    mixed[...] = jnp.zeros_like(mixed)
    logs[...] = jnp.zeros_like(logs)
    loads[0].wait()
    loads[1].wait()
    for part in range(2):
        span = pl.ds(part * rows, rows)
        wide = tok[span, :].astype(f32)
        scale = lax.rsqrt(jnp.mean(wide * wide, axis=-1, keepdims=True) + epsilon)
        normed[span, :D] = (wide * scale * gain[...]).astype(bf16)
        inner = nt(normed[span, :D], at_qkv[...])
        normed[span, D:] = inner.astype(bf16)
        zt_out[:, span] = inner.T.astype(bf16)
    for load in loads[2:]:
        load.wait()
    for part in range(2):
        span = pl.ds(part * rows, rows)
        cos_rows = cosine[span, :]
        sin_rows = sine[span, :]
        for pair in range(QW // 256 + 1):
            width = min(256, QW - pair * 256)
            made = nn(normed[span, :], weight[:, pair * 256 : pair * 256 + width])
            for unit in range(width // 128):
                at = pair * 256 + unit * 128
                query[span, at : at + 128] = (
                    turned(made[:, unit * 128 : unit * 128 + 128], cos_rows, sin_rows) * HD**-0.5
                ).astype(bf16)
        made = nn(normed[span, :], weight[:, QW : QW + KW])
        forms = halves(
            turned(made[:, :128], cos_rows, sin_rows), turned(made[:, 128:], cos_rows, sin_rows)
        )
        for index, form in enumerate(forms):
            keys[index, span, :] = form.astype(bf16)
        made = nn(normed[span, :], weight[:, QW + KW :])
        for index, form in enumerate(halves(made[:, :128], made[:, 128:])):
            values[index, span, :] = form.astype(bf16)
    stores = [
        pltpu.make_async_copy(query, q_out, out_sems.at[0]),
        pltpu.make_async_copy(keys, k_out, out_sems.at[1]),
        pltpu.make_async_copy(values, v_out, out_sems.at[2]),
        pltpu.make_async_copy(normed.at[:, pl.ds(0, D)], n_out, out_sems.at[3]),
    ]
    for store in stores:
        store.start()

    for block in range(2 * rows // BLOCK):
        low, high = block * BLOCK, (block + 1) * BLOCK
        begin = starts[low:high, :]

        def head(h, carry, low=low, high=high, begin=begin):
            pair, parity = h // 2, h % 2
            form = (h // GROUP) * 2 + parity
            at = pl.ds(pl.multiple_of(pair * 128, 128), 128)
            scores = nt(query[low:high, at], keys[form, :high, :])
            place = lanes((BLOCK, BLOCK))
            offset = lax.broadcasted_iota(jnp.int32, (BLOCK, BLOCK), 0)
            pieces = []
            for first in range(0, high, BLOCK):
                allowed = place + first >= begin
                if first == low:
                    allowed = allowed & (place <= offset)
                pieces.append(
                    jnp.where(allowed, scores[:, first : first + BLOCK], masked_value)
                )
            top = functools.reduce(jnp.maximum, pieces)
            top = jnp.max(top, axis=-1, keepdims=True)
            pieces = [jnp.exp(piece - top) for piece in pieces]
            total = jnp.sum(functools.reduce(jnp.add, pieces), axis=-1, keepdims=True)
            chances = jnp.concatenate([piece.astype(bf16) for piece in pieces], axis=1)
            blended = nn(chances, values[form, :high, :]) / total
            mixed[low:high, at] += blended
            logs[low:high, :] = jnp.where(
                lanes((BLOCK, 128)) == h, top + jnp.log(total), logs[low:high, :]
            )
            return carry

        lax.fori_loop(0, HEADS, head, 0)
        o_out[low:high, :] = mixed[low:high, :].astype(bf16)
    lse_out[...] = logs[...].T[:R, :]
    for store in stores:
        store.wait()


def attend(ids, tok_own, tok_oth, w_own, w_oth, b_win, at_qkv, gain, cosine, sine, starts):
    rows = tok_own.shape[0]
    length = 2 * rows
    shape = jax.ShapeDtypeStruct
    return pl.pallas_call(
        attend_kernel,
        out_shape=[
            shape((length, QW), bf16),
            shape((length, QW), bf16),
            shape((6, length, 128), bf16),
            shape((6, length, 128), bf16),
            shape((length, D), bf16),
            shape((128, length), bf16),
            shape((R, length), f32),
        ],
        in_specs=[SMEM] + [ANY] * 5 + [VMEM] * 5,
        out_specs=[VMEM, ANY, ANY, ANY, ANY, VMEM, VMEM],
        scratch_shapes=[
            pltpu.VMEM((length, D), bf16),
            pltpu.VMEM((length, AUG), bf16),
            pltpu.VMEM((AUG, SPAN), bf16),
            pltpu.VMEM((length, QW), bf16),
            pltpu.VMEM((6, length, 128), bf16),
            pltpu.VMEM((6, length, 128), bf16),
            pltpu.VMEM((length, QW), f32),
            pltpu.VMEM((length, 128), f32),
            pltpu.SemaphoreType.DMA((5,)),
            pltpu.SemaphoreType.DMA((4,)),
        ],
        compiler_params=pltpu.CompilerParams(vmem_limit_bytes=48 << 20),
        cost_estimate=pl.CostEstimate(
            flops=16 * 10**9, bytes_accessed=16 << 20, transcendentals=6 * 10**6
        ),
        name="attend",
    )(ids, tok_own, tok_oth, w_own, w_oth, b_win, at_qkv, gain, cosine, sine, starts)


def normed_back(rows, gain_row, grad):
    scale = lax.rsqrt(jnp.mean(rows * rows, axis=-1, keepdims=True) + epsilon)
    scaled = grad * gain_row
    inside = jnp.mean(rows * scaled, axis=-1, keepdims=True)
    return scale * (scaled - rows * (scale * scale * inside))


def feed_kernel(
    ids,
    o_own,
    o_oth,
    tok,
    cot,
    wo_own,
    wo_oth,
    wgu_own,
    wgu_oth,
    wd_own,
    wd_oth,
    a_down,
    upper_hidden,
    at_own,
    at_oth,
    at_gu,
    b_out,
    b_down,
    gain,
    layer_out,
    grad_middle,
    do_own,
    do_oth,
    ga_gu,
    gb_gate,
    gb_up,
    ga_down,
    gb_down,
    ga_own,
    ga_oth,
    gb_out,
    wout,
    wg,
    wu,
    wd,
    middle,
    normed,
    cot_aug,
    total,
    back,
    z_gu_t,
    dz_down_t,
    sems,
    o_sems,
):
    g = ids[0]
    chosen = ids[1]
    rows = tok.shape[0]
    steps = FF // TILE
    each = steps // 2
    w_here = pl.multiple_of(g * HALF, 64)
    w_there = pl.multiple_of((1 - g) * HALF, 64)

    def column(step):
        owner = jnp.where(step < each, g, 1 - g)
        return owner * (FF // 2) + (step % each) * TILE

    def copies(step, slot):
        at = pl.multiple_of(column(step), TILE)
        gate_at = pl.ds(at, TILE)
        up_at = pl.ds(pl.multiple_of(FF + at, TILE), TILE)
        local = pl.ds(pl.multiple_of((step % each) * TILE, TILE), TILE)
        sem = lambda k: sems.at[slot, k]
        main = wd.at[slot, :, pl.ds(0, D)]
        return (
            [
                pltpu.make_async_copy(wgu_own.at[:, gate_at], wg.at[slot, pl.ds(w_here, HALF)], sem(0)),
                pltpu.make_async_copy(wgu_oth.at[:, gate_at], wg.at[slot, pl.ds(w_there, HALF)], sem(1)),
                pltpu.make_async_copy(wgu_own.at[:, up_at], wu.at[slot, pl.ds(w_here, HALF)], sem(2)),
                pltpu.make_async_copy(wgu_oth.at[:, up_at], wu.at[slot, pl.ds(w_there, HALF)], sem(3)),
                pltpu.make_async_copy(upper_hidden.at[0, chosen, :, gate_at], wg.at[slot, pl.ds(D, R)], sem(4)),
                pltpu.make_async_copy(upper_hidden.at[1, chosen, :, gate_at], wu.at[slot, pl.ds(D + R, R)], sem(5)),
                pltpu.make_async_copy(a_down.at[gate_at], wd.at[slot, :, pl.ds(D, 128)], sem(6)),
            ],
            pltpu.make_async_copy(wd_own.at[local], main, sem(7)),
            pltpu.make_async_copy(wd_oth.at[local], main, sem(7)),
        )

    def start(step, slot):
        always, own, oth = copies(step, slot)
        for copy in always:
            copy.start()

        @pl.when(step < each)
        def _():
            own.start()

        @pl.when(step >= each)
        def _():
            oth.start()

    def wait(step, slot):
        always, own, _ = copies(step, slot)
        for copy in always:
            copy.wait()
        own.wait()

    out_loads = [
        pltpu.make_async_copy(wo_own, wout.at[0, pl.ds(0, HALF)], o_sems.at[0]),
        pltpu.make_async_copy(wo_oth, wout.at[1, pl.ds(0, HALF)], o_sems.at[1]),
    ]
    for load in out_loads:
        load.start()
    for slot in range(2):
        wg[slot, D:, :] = jnp.zeros((128, TILE), bf16)
        wu[slot, D:, :] = jnp.zeros((128, TILE), bf16)
        wout[slot, HALF:, :] = jnp.zeros((QW - HALF, D), bf16)
    start(0, 0)

    inner_out = (nt(o_own[...], at_own[...]) + nt(o_oth[...], at_oth[...])).astype(bf16)
    cot_aug[:, :D] = cot[...]
    dz_down = nt(cot[...], b_down[...])
    cot_aug[:, D:] = dz_down.astype(bf16)
    dz_down_t[...] = dz_down.T[:R, :].astype(bf16)
    for load in out_loads:
        load.wait()
    middle[...] = (
        tok[...].astype(f32)
        + nn(o_own[...], wout[0])
        + nn(o_oth[...], wout[1])
        + nn(inner_out, b_out[...])
    )
    scale = lax.rsqrt(jnp.mean(middle[...] * middle[...], axis=-1, keepdims=True) + epsilon)
    normed[:, :D] = (middle[...] * scale * gain[...]).astype(bf16)
    inner_gu = nt(normed[:, :D], at_gu[...])
    normed[:, D:] = inner_gu.astype(bf16)
    z_gu_t[...] = inner_gu.T[: 2 * R, :].astype(bf16)
    total[...] = jnp.zeros_like(total)
    back[...] = jnp.zeros_like(back)

    def step_body(step, carry):
        slot = step % 2

        @pl.when(step + 1 < steps)
        def _():
            start(step + 1, 1 - slot)

        wait(step, slot)
        gate_at = pl.ds(pl.multiple_of(column(step), TILE), TILE)
        gate = nn(normed[...], wg[slot])
        up = nn(normed[...], wu[slot])
        grad_active = nt(cot_aug[...], wd[slot])
        sigmoid = 1.0 / (1.0 + jnp.exp(-gate))
        silu = gate * sigmoid
        active = (silu * up).astype(bf16)
        grad_gate = (grad_active * up * (sigmoid * (1.0 + gate * (1.0 - sigmoid)))).astype(bf16)
        grad_up = (grad_active * silu).astype(bf16)
        total[...] += nn(active, wd[slot])
        back[...] += nt(grad_gate, wg[slot]) + nt(grad_up, wu[slot])
        gb_gate[:, gate_at] = nn(z_gu_t[...], grad_gate)[:R]
        gb_up[:, gate_at] = nn(z_gu_t[...], grad_up)[R:]
        ga_down[:, gate_at] = nn(dz_down_t[...], active)
        return carry

    lax.fori_loop(0, steps, step_body, 0)

    inner_down = total[:, D:].astype(bf16)
    layer_out[...] = (middle[...] + total[:, :D] + nn(inner_down, b_down[...])).astype(bf16)
    gb_down[...] = nn(total[:, D:].T[:R, :].astype(bf16), cot[...])
    dz_gu = back[:, D:].astype(bf16)
    grad_normed = back[:, :D] + nn(dz_gu, at_gu[...])
    ga_gu[...] = nn(back[:, D:].T[: 2 * R, :].astype(bf16), normed[:, :D])
    grad = cot[...].astype(f32) + normed_back(middle[...], gain[...], grad_normed)
    grad_middle[...] = grad
    branch = grad.astype(bf16)
    gb_out[...] = nn(inner_out.astype(f32).T[:R, :].astype(bf16), branch)
    dz_out = nt(branch, b_out[...])
    dz_out_low = dz_out.astype(bf16)
    dz_out_t = dz_out.T[:R, :].astype(bf16)
    ga_own[...] = nn(dz_out_t, o_own[...])
    ga_oth[...] = nn(dz_out_t, o_oth[...])
    do_own[...] = (nt(branch, wout[0]) + nn(dz_out_low, at_own[...])).astype(bf16)
    do_oth[...] = (nt(branch, wout[1]) + nn(dz_out_low, at_oth[...])).astype(bf16)


def feed(*args):
    rows = args[3].shape[0]
    shape = jax.ShapeDtypeStruct
    return pl.pallas_call(
        feed_kernel,
        out_shape=[
            shape((rows, D), bf16),
            shape((rows, D), f32),
            shape((rows, QW), bf16),
            shape((rows, QW), bf16),
            shape((2 * R, D), f32),
            shape((R, FF), f32),
            shape((R, FF), f32),
            shape((R, FF), f32),
            shape((R, D), f32),
            shape((R, QW), f32),
            shape((R, QW), f32),
            shape((R, D), f32),
        ],
        in_specs=[SMEM] + [VMEM] * 4 + [ANY] * 8 + [VMEM] * 6,
        out_specs=[VMEM] * 12,
        scratch_shapes=[
            pltpu.VMEM((2, QW, D), bf16),
            pltpu.VMEM((2, AUG, TILE), bf16),
            pltpu.VMEM((2, AUG, TILE), bf16),
            pltpu.VMEM((2, TILE, AUG), bf16),
            pltpu.VMEM((rows, D), f32),
            pltpu.VMEM((rows, AUG), bf16),
            pltpu.VMEM((rows, AUG), bf16),
            pltpu.VMEM((rows, AUG), f32),
            pltpu.VMEM((rows, AUG), f32),
            pltpu.VMEM((2 * R, rows), bf16),
            pltpu.VMEM((R, rows), bf16),
            pltpu.SemaphoreType.DMA((2, 8)),
            pltpu.SemaphoreType.DMA((2,)),
        ],
        compiler_params=pltpu.CompilerParams(vmem_limit_bytes=52 << 20),
        cost_estimate=pl.CostEstimate(
            flops=30 * 10**9, bytes_accessed=36 << 20, transcendentals=2 * 10**6
        ),
        name="feed",
    )(*args)


def attend_back_kernel(
    ids,
    do_own,
    do_oth,
    w_own,
    w_oth,
    b_win,
    normed,
    o_all,
    query,
    keys,
    values,
    at_qkv,
    zt,
    lse,
    cosine,
    sine,
    starts,
    part_own,
    part_oth,
    ga,
    gb,
    grad_o,
    weight,
    n_rows,
    delta,
    dq,
    dk,
    dv,
    dy,
    sems,
):
    g = ids[0]
    rows = do_own.shape[0]
    length = 2 * rows
    here = pl.multiple_of(g * rows, 128)
    there = pl.multiple_of((1 - g) * rows, 128)
    w_here = pl.multiple_of(g * HALF, 64)
    w_there = pl.multiple_of((1 - g) * HALF, 64)
    loads = [
        pltpu.make_async_copy(do_own, grad_o.at[pl.ds(here, rows)], sems.at[0]),
        pltpu.make_async_copy(do_oth, grad_o.at[pl.ds(there, rows)], sems.at[1]),
        pltpu.make_async_copy(w_own, weight.at[pl.ds(w_here, HALF)], sems.at[2]),
        pltpu.make_async_copy(w_oth, weight.at[pl.ds(w_there, HALF)], sems.at[3]),
        pltpu.make_async_copy(b_win, weight.at[pl.ds(D, 128)], sems.at[4]),
        pltpu.make_async_copy(normed, n_rows, sems.at[5]),
    ]
    for load in loads:
        load.start()
    dq[...] = jnp.zeros_like(dq)
    dk[...] = jnp.zeros_like(dk)
    dv[...] = jnp.zeros_like(dv)
    loads[0].wait()
    loads[1].wait()
    ones = (
        lanes((R, QW)) // HD == lax.broadcasted_iota(jnp.int32, (R, QW), 0)
    ).astype(bf16)
    product = grad_o[...].astype(f32) * o_all[...].astype(f32)
    upper = product.astype(bf16)
    lower = (product - upper.astype(f32)).astype(bf16)
    delta[...] = nt(ones, upper) + nt(ones, lower)

    for block in range(length // BLOCK):
        low, high = block * BLOCK, (block + 1) * BLOCK
        begin = starts[:, low:high]

        def head(h, carry, low=low, high=high, begin=begin):
            pair, parity = h // 2, h % 2
            form = (h // GROUP) * 2 + parity
            at = pl.ds(pl.multiple_of(pair * 128, 128), 128)
            q_rows = query[low:high, at]
            g_rows = grad_o[low:high, at]
            logs = lse[pl.ds(h, 1), low:high]
            deltas = delta[pl.ds(h, 1), low:high]
            place = lax.broadcasted_iota(jnp.int32, (BLOCK, BLOCK), 0)
            lane = lanes((BLOCK, BLOCK))
            grads = jnp.zeros((BLOCK, 128), f32)
            for first in range(0, high, BLOCK):
                span = slice(first, first + BLOCK)
                scores = nt(keys[form, span, :], q_rows)
                allowed = place + first >= begin
                if first == low:
                    allowed = allowed & (place <= lane)
                chances = jnp.where(allowed, jnp.exp(scores - logs), 0.0)
                grad_chances = nt(values[form, span, :], g_rows)
                grad_scores = (chances * (grad_chances - deltas)).astype(bf16)
                dv[form, span, :] += nn(chances.astype(bf16), g_rows)
                dk[form, span, :] += nn(grad_scores, q_rows)
                grads += tn(grad_scores, keys[form, span, :])
            dq[low:high, at] += grads
            return carry

        lax.fori_loop(0, HEADS, head, 0)

    for load in loads[2:]:
        load.wait()

    def joined(acc, span):
        low = lanes((rows, 128)) < HD
        one = jnp.where(
            low,
            acc[0, span, :] + pltpu.roll(acc[1, span, :], HD, 1),
            acc[3, span, :] + pltpu.roll(acc[2, span, :], HD, 1),
        )
        two = jnp.where(low, acc[4, span, :] + pltpu.roll(acc[5, span, :], HD, 1), 0.0)
        return one, two

    for part in range(2):
        span = pl.ds(part * rows, rows)
        cos_rows = cosine[span, :]
        sin_rows = -sine[span, :]
        for pair in range(QW // 128):
            at = slice(pair * 128, pair * 128 + 128)
            dy[span, at] = (turned(dq[span, at], cos_rows, sin_rows) * HD**-0.5).astype(bf16)
        for index, acc in enumerate(joined(dk, span)):
            dy[span, QW + index * 128 : QW + index * 128 + 128] = turned(
                acc, cos_rows, sin_rows
            ).astype(bf16)
        for index, acc in enumerate(joined(dv, span)):
            at = QW + KW + index * 128
            dy[span, at : at + 128] = acc.astype(bf16)

    gb[...] = nn(zt[: 3 * R, :], dy[...])
    ga_total = jnp.zeros((3 * R, D), f32)
    for offset, out in ((there, part_oth), (here, part_own)):
        span = pl.ds(offset, rows)
        made = nt(dy[span, :], weight[...])
        inner = made[:, D:]
        out[...] = (made[:, :D] + nn(inner.astype(bf16), at_qkv[...])).astype(out.dtype)
        ga_total += nn(inner.T[: 3 * R, :].astype(bf16), n_rows[span, :])
    ga[...] = ga_total


def attend_back(*args):
    rows = args[1].shape[0]
    length = 2 * rows
    shape = jax.ShapeDtypeStruct
    return pl.pallas_call(
        attend_back_kernel,
        out_shape=[
            shape((rows, D), f32),
            shape((rows, D), bf16),
            shape((3 * R, D), f32),
            shape((3 * R, SPAN), f32),
        ],
        in_specs=[SMEM] + [ANY] * 6 + [VMEM] * 10,
        out_specs=[VMEM] * 4,
        scratch_shapes=[
            pltpu.VMEM((length, QW), bf16),
            pltpu.VMEM((AUG, SPAN), bf16),
            pltpu.VMEM((length, D), bf16),
            pltpu.VMEM((R, length), f32),
            pltpu.VMEM((length, QW), f32),
            pltpu.VMEM((6, length, 128), f32),
            pltpu.VMEM((6, length, 128), f32),
            pltpu.VMEM((length, SPAN), bf16),
            pltpu.SemaphoreType.DMA((6,)),
        ],
        compiler_params=pltpu.CompilerParams(vmem_limit_bytes=56 << 20),
        cost_estimate=pl.CostEstimate(
            flops=24 * 10**9, bytes_accessed=20 << 20, transcendentals=6 * 10**6
        ),
        name="attend_back",
    )(*args)


def padded(value, count, axis):
    pads = [(0, 0)] * value.ndim
    pads[axis] = (0, count - value.shape[axis])
    return jnp.pad(value, pads)


def head_columns(matrix, side):
    quarter = KV // 2
    return jnp.concatenate(
        [
            padded(matrix[:, side * HALF : (side + 1) * HALF], QW, 1),
            padded(matrix[:, D + side * quarter : D + (side + 1) * quarter], KW, 1),
            padded(matrix[:, D + KV + side * quarter : D + KV + (side + 1) * quarter], KW, 1),
        ],
        axis=1,
    )


def per_device(
    tokens,
    cotangent,
    segment_ids,
    adapter_ids,
    norm_gains,
    frozen_qkv,
    frozen_out,
    frozen_gate_up,
    frozen_down,
    lower_mats,
    lower_down,
    upper_width,
    upper_keys,
    upper_hidden,
):
    chosen = adapter_ids[0]
    segments = segment_ids[0]
    rows = tokens.shape[1]
    length = segments.shape[0]
    g = lax.axis_index("grp")
    first = g == 0
    swap = lambda value: lax.ppermute(value, "grp", SWAP)

    def by_side(zero, one):
        return jnp.where(first, zero, one)

    tok_own = tokens[0]
    tok_oth = swap(tok_own)
    side_zero, side_one = head_columns(frozen_qkv, 0), head_columns(frozen_qkv, 1)
    w_own = by_side(side_zero, side_one)
    w_oth = swap(by_side(side_one, side_zero))
    gains_oth = swap(norm_gains)
    wo_oth = swap(frozen_out)
    wgu_oth = swap(frozen_gate_up)
    wd_oth = swap(frozen_down)

    gains = by_side(
        jnp.concatenate([norm_gains, gains_oth], axis=1),
        jnp.concatenate([gains_oth, norm_gains], axis=1),
    ).astype(f32)
    lower_t = lax.dynamic_index_in_dim(lower_mats, chosen, 1, keepdims=False).transpose(0, 2, 1)
    down_t = lax.dynamic_index_in_dim(lower_down, chosen, 0, keepdims=False)
    width_pick = lax.dynamic_index_in_dim(upper_width, chosen, 1, keepdims=False)
    keys_pick = lax.dynamic_index_in_dim(upper_keys, chosen, 1, keepdims=False)

    at_qkv = padded(lower_t[:3].reshape(3 * R, D), 128, 0)
    at_gu = padded(lower_t[4:].reshape(2 * R, D), 128, 0)
    at_out = padded(lower_t[3], 128, 0)
    at_zero, at_one = padded(at_out[:, :HALF], QW, 1), padded(at_out[:, HALF:], QW, 1)
    at_own, at_oth = by_side(at_zero, at_one), by_side(at_one, at_zero)
    b_out = padded(width_pick[1], 128, 0)
    b_down = padded(width_pick[2], 128, 0)
    a_down = padded(down_t, 128, 1)
    zeros = lambda columns: jnp.zeros((R, columns), bf16)
    b_all = jnp.concatenate(
        [
            jnp.concatenate([width_pick[0], zeros(2 * KV)], axis=1),
            jnp.concatenate([zeros(D), keys_pick[0], zeros(KV)], axis=1),
            jnp.concatenate([zeros(D + KV), keys_pick[1]], axis=1),
        ],
        axis=0,
    )
    b_win = padded(by_side(head_columns(b_all, 0), head_columns(b_all, 1)), 128, 0)

    counts = [jnp.sum((segments < value).astype(jnp.int32)) for value in range(4)]
    starts = functools.reduce(
        lambda acc, value: jnp.where(segments == value, counts[value], acc),
        range(1, 4),
        jnp.zeros_like(segments),
    )
    lane = jnp.arange(128, dtype=jnp.int32)
    freqs = theta_base ** (-(lane % (HD // 2)).astype(f32) * 2.0 / HD)
    angle = (jnp.arange(length, dtype=jnp.int32) - starts).astype(f32)[:, None] * freqs[None, :]
    cosine = jnp.cos(angle)
    sine = jnp.where(lane % HD < HD // 2, -1.0, 1.0)[None, :] * jnp.sin(angle)
    ids = jnp.stack([g, chosen]).astype(jnp.int32)

    o_all, query, keys, values, normed, zt, lse = attend(
        ids, tok_own, tok_oth, w_own, w_oth, b_win, at_qkv, gains[:1], cosine, sine, starts[:, None]
    )
    o_zero, o_one = o_all[:rows], o_all[rows:]
    o_own = by_side(o_zero, o_one)
    o_oth = swap(by_side(o_one, o_zero))
    (
        layer_out,
        grad_middle,
        do_own,
        do_send,
        ga_gu,
        gb_gate,
        gb_up,
        ga_down,
        gb_down,
        ga_own,
        ga_oth,
        gb_out,
    ) = feed(
        ids,
        o_own,
        o_oth,
        tok_own,
        cotangent[0],
        frozen_out,
        wo_oth,
        frozen_gate_up,
        wgu_oth,
        frozen_down,
        wd_oth,
        a_down,
        upper_hidden,
        at_own,
        at_oth,
        at_gu,
        b_out,
        b_down,
        gains[1:],
    )
    do_oth = swap(do_send)
    ga_out = by_side(
        jnp.concatenate([ga_own[:, :HALF], ga_oth[:, :HALF]], axis=1),
        jnp.concatenate([ga_oth[:, :HALF], ga_own[:, :HALF]], axis=1),
    )
    part_own, part_send, ga_qkv, gb_qkv = attend_back(
        ids,
        do_own,
        do_oth,
        w_own,
        w_oth,
        b_win,
        normed,
        o_all,
        query,
        keys,
        values,
        at_qkv,
        zt,
        lse,
        cosine,
        sine,
        starts[None, :],
    )
    grad_normed = part_own + swap(part_send).astype(f32)
    grad_hidden = grad_middle + normed_back(tok_own.astype(f32), gains[:1], grad_normed)
    input_grad = grad_hidden.astype(bf16)

    quarter = KV // 2

    def placed(value, count):
        blank = jnp.zeros((R, count), f32)
        return by_side(
            jnp.concatenate([value[:, :count], blank], axis=1),
            jnp.concatenate([blank, value[:, :count]], axis=1),
        )

    gb_q = placed(gb_qkv[:R, :QW], HALF)
    gb_k = placed(gb_qkv[R : 2 * R, QW : QW + KW], quarter)
    gb_v = placed(gb_qkv[2 * R :, QW + KW :], quarter)
    sums = summed_by_adapter(
        [
            jnp.concatenate([ga_qkv, ga_out, ga_gu], axis=0).reshape(6, R, D),
            ga_down[None],
            jnp.stack([gb_q, gb_out, gb_down]),
            jnp.stack([gb_k, gb_v]),
            jnp.stack([gb_gate, gb_up]),
        ],
        chosen,
    )
    return (
        layer_out[None],
        input_grad[None],
        sums[0].transpose(0, 1, 3, 2),
        sums[1][0].transpose(0, 2, 1),
        sums[2],
        sums[3],
        sums[4],
    )


def summed_by_adapter(parts, chosen):
    reps = lax.axis_size("rep")
    pieces = [part.shape[-1] // reps for part in parts]
    blocks = [
        part.reshape(-1, reps, piece).transpose(1, 0, 2).reshape(reps, -1)
        for part, piece in zip(parts, pieces)
    ]
    mine = jnp.concatenate(blocks, axis=1)
    other = lax.ppermute(mine.astype(bf16), "grp", SWAP)
    both = (mine + other.astype(f32)).astype(bf16)
    label = jnp.full((reps, 128), chosen, jnp.int32).astype(bf16)
    received = lax.all_to_all(
        jnp.concatenate([label, both], axis=1), "rep", 0, 0, tiled=True
    )
    quota = NAD // lax.axis_size("grp")
    wanted = lax.axis_index("grp") * quota + jnp.arange(quota, dtype=jnp.int32)
    picks = (received[:, 0].astype(jnp.int32)[None, :] == wanted[:, None]).astype(bf16)
    total = jnp.dot(picks, received[:, 128:], preferred_element_type=f32)
    outs = []
    start = 0
    for part, piece in zip(parts, pieces):
        count = part.shape[0] * part.shape[1] * piece
        outs.append(
            total[:, start : start + count]
            .reshape(quota, part.shape[0], part.shape[1], piece)
            .transpose(1, 0, 2, 3)
        )
        start += count
    return outs


def solution(mesh):
    return jax.shard_map(
        per_device,
        mesh=mesh,
        in_specs=(
            P("rep", "grp", None),
            P("rep", "grp", None),
            P("rep", None),
            P("rep"),
            P(None, "grp"),
            P("grp", None),
            P("grp", None),
            P("grp", None),
            P("grp", None),
            P(),
            P(),
            P(),
            P(),
            P(),
        ),
        out_specs=(
            P("rep", "grp", None),
            P("rep", "grp", None),
            P(None, "grp", "rep", None),
            P("grp", "rep", None),
            P(None, "grp", None, "rep"),
            P(None, "grp", None, "rep"),
            P(None, "grp", None, "rep"),
        ),
        check_vma=False,
    )
```

```python
import functools

import jax
import jax.numpy as jnp
from jax import lax
from jax.experimental import pallas as pl
from jax.experimental.pallas import tpu as pltpu
from jax.sharding import PartitionSpec as P

D = 1152
H = 18
KVH = 6
HD = 64
FF = 3072
R = 16
NAD = 8
KV = 384

HALF = D // 2
HEADS = H // 2
GROUP = H // KVH
QW = 640
KW = 256
SPAN = QW + 2 * KW
AUG = D + 128
TILE = 512
BLOCK = 256
DOCS = 4
PERIOD = 32
VMEM_BYTES = 61900 * 1024

epsilon = 1e-05
theta_base = 10000.0
masked_value = -1e30
f32 = jnp.float32
bf16 = jnp.bfloat16
SWAP = [(0, 1), (1, 0)]

HBM = pl.BlockSpec(memory_space=pltpu.MemorySpace.HBM)
ANY = pl.BlockSpec(memory_space=pl.ANY)
VMEM = pl.BlockSpec(memory_space=pltpu.VMEM)
SMEM = pl.BlockSpec(memory_space=pltpu.SMEM)


def nn(left, right):
    return jnp.dot(left, right, preferred_element_type=f32)


def nt(left, right):
    return lax.dot_general(left, right, (((1,), (1,)), ((), ())), preferred_element_type=f32)


def tn(left, right):
    return lax.dot_general(left, right, (((0,), (0,)), ((), ())), preferred_element_type=f32)


def lanes(shape):
    return lax.broadcasted_iota(jnp.int32, shape, len(shape) - 1)


def turned(rows, cosine, sine):
    first = lanes(rows.shape) % HD < HD // 2
    partner = jnp.where(first, pltpu.roll(rows, 128 - HD // 2, 1), pltpu.roll(rows, HD // 2, 1))
    return rows * cosine + partner * sine


def gain_row(g, own, other, row):
    mine = own[row : row + 1, :].astype(f32)
    theirs = other[row : row + 1, :].astype(f32)
    return jnp.where(
        g == 0,
        jnp.concatenate([mine, theirs], axis=1),
        jnp.concatenate([theirs, mine], axis=1),
    )


def by_slot(g, slot, pick):
    zero = pick(slot) if slot < HEADS else None
    one = pick(slot - 1) if slot > 0 else None
    if zero is None:
        return jnp.where(g == 0, jnp.zeros_like(one), one)
    if one is None:
        return jnp.where(g == 0, zero, jnp.zeros_like(zero))
    return jnp.where(g == 0, zero, one)


def copied(source, target, sem):
    return pltpu.make_async_copy(source, target, sem)


def forms_of(store, span, pairs):
    low = lanes(pairs[0].shape) < HD
    for index, pair in enumerate(pairs):
        swapped = pltpu.roll(pair, HD, 1)
        for slot, parity, rows in ((0, 0, pair), (0, 1, swapped), (1, 0, swapped), (1, 1, pair)):
            kept = jnp.where(low, rows, 0.0) if parity == 0 else jnp.where(low, 0.0, rows)
            store[4 * index + 2 * slot + parity, span, :] = kept.astype(bf16)


def doc_starts(segments):
    return [
        jnp.sum(jnp.where(segments < doc, 1.0, 0.0), axis=-1, keepdims=True)
        for doc in range(1, DOCS)
    ]


def start_at(place, starts):
    found = jnp.zeros_like(place)
    for start in starts:
        found = jnp.where(place >= start, start, found)
    return found


def fill_angles(freqs, starts, cosine, sine):
    def table(count, step):
        place = lax.broadcasted_iota(jnp.int32, (count, 128), 0).astype(f32) * step
        return jnp.cos(place * freqs), jnp.sin(place * freqs)

    length = cosine.shape[0]
    fine_cos, fine_sin = table(PERIOD, 1.0)
    wide_cos, wide_sin = table(length // PERIOD, float(PERIOD))
    docs = [(jnp.cos(start * freqs), jnp.sin(start * freqs)) for start in starts]
    sign = jnp.where(lanes((1, 128)) % HD < HD // 2, -1.0, 1.0)
    for index in range(length // PERIOD):
        c = wide_cos[index : index + 1]
        s = wide_sin[index : index + 1]
        cos_p = c * fine_cos - s * fine_sin
        sin_p = s * fine_cos + c * fine_sin
        place = (
            lax.broadcasted_iota(jnp.int32, (PERIOD, 128), 0) + index * PERIOD
        ).astype(f32)
        cos_d, sin_d = jnp.ones((PERIOD, 128), f32), jnp.zeros((PERIOD, 128), f32)
        for start, (cos_s, sin_s) in zip(starts, docs):
            inside = place >= start
            cos_d = jnp.where(inside, cos_s, cos_d)
            sin_d = jnp.where(inside, sin_s, sin_d)
        span = slice(index * PERIOD, (index + 1) * PERIOD)
        cosine[span, :] = cos_p * cos_d + sin_p * sin_d
        sine[span, :] = (sin_p * cos_d - cos_p * sin_d) * sign


def qkv_loads(g, chosen, own, oth, upper_width, upper_keys, weight, sems):
    w_here = pl.ds(pl.multiple_of(g * HALF, 64), HALF)
    w_there = pl.ds(pl.multiple_of((1 - g) * HALF, 64), HALF)
    windows = (
        (pl.multiple_of(g * 512, 128), QW, 0),
        (pl.multiple_of(D + g * 128, 128), KW, QW),
        (pl.multiple_of(D + KV + g * 128, 128), KW, QW + KW),
    )
    loads = []
    for index, (at, width, to) in enumerate(windows):
        for part, (source, rows) in enumerate(((own, w_here), (oth, w_there))):
            loads.append(
                copied(
                    source.at[:, pl.ds(at, width)],
                    weight.at[rows, pl.ds(to, width)],
                    sems.at[2 * index + part],
                )
            )
    if upper_width is None:
        return loads
    loads.append(
        copied(
            upper_width.at[0, chosen, :, pl.ds(pl.multiple_of(g * 512, 128), QW)],
            weight.at[pl.ds(D, R), pl.ds(0, QW)],
            sems.at[6],
        )
    )
    for index in range(2):
        loads.append(
            copied(
                upper_keys.at[index, chosen, :, pl.ds(pl.multiple_of(g * 128, 128), KW)],
                weight.at[pl.ds(D + (index + 1) * R, R), pl.ds(QW + index * KW, KW)],
                sems.at[7 + index],
            )
        )
    return loads


def attend_kernel(
    adapter,
    tok_own,
    tok_oth,
    qkv_own,
    qkv_oth,
    lower_t,
    upper_width,
    upper_keys,
    gains_own,
    gains_oth,
    segments,
    freqs,
    o_own,
    o_send,
    q_out,
    k_out,
    v_out,
    kt_out,
    n_out,
    zt_out,
    lse_out,
    cos_out,
    sin_out,
    tok,
    normed,
    weight,
    maps,
    query,
    natural,
    flipped,
    keys,
    values,
    mixed,
    mixed_low,
    logs,
    bias,
    cosine,
    sine,
    inner_t,
    lse,
    sems,
    w_sems,
    out_sems,
):
    g = lax.axis_index("grp")
    chosen = adapter[0]
    rows = tok_own.shape[0]
    here = pl.ds(pl.multiple_of(g * rows, 128), rows)
    there = pl.ds(pl.multiple_of((1 - g) * rows, 128), rows)
    maps[...] = jnp.zeros_like(maps)
    weight[D:, :] = jnp.zeros((128, SPAN), bf16)
    loads = [
        copied(tok_own, tok.at[here], sems.at[0]),
        copied(tok_oth, tok.at[there], sems.at[1]),
    ] + [
        copied(lower_t.at[index, chosen], maps.at[pl.ds(index * R, R)], sems.at[2 + index])
        for index in range(3)
    ]
    w_loads = qkv_loads(g, chosen, qkv_own, qkv_oth, upper_width, upper_keys, weight, w_sems)
    for load in loads:
        load.start()
    starts = doc_starts(segments[...])
    fill_angles(freqs[...], starts, cosine, sine)
    gain = gain_row(g, gains_own, gains_oth, 0)
    for load in loads:
        load.wait()
    for load in w_loads:
        load.start()

    def norm_part(part, carry):
        span = pl.ds(pl.multiple_of(part * rows, 128), rows)
        wide = tok[span, :].astype(f32)
        scale = lax.rsqrt(jnp.mean(wide * wide, axis=-1, keepdims=True) + epsilon)
        normed[span, :D] = (wide * scale * gain).astype(bf16)
        inner = nt(normed[span, :D], maps[...])
        normed[span, D:] = inner.astype(bf16)
        inner_t[:, span] = inner.T[: 3 * R, :].astype(bf16)
        return carry

    lax.fori_loop(0, 2, norm_part, 0)
    for load in w_loads:
        load.wait()

    def project(part, carry):
        span = pl.ds(pl.multiple_of(part * rows, 128), rows)
        cos_rows = cosine[span, :]
        sin_rows = sine[span, :]
        for pair in range(QW // 256 + 1):
            width = min(256, QW - pair * 256)
            made = nn(normed[span, :], weight[:, pair * 256 : pair * 256 + width])
            for unit in range(width // 128):
                at = pair * 256 + unit * 128
                query[span, at : at + 128] = (
                    turned(made[:, unit * 128 : unit * 128 + 128], cos_rows, sin_rows) * HD**-0.5
                ).astype(bf16)
        made = nn(normed[span, :], weight[:, QW : QW + KW])
        pairs = [turned(made[:, at : at + 128], cos_rows, sin_rows) for at in (0, 128)]
        forms_of(keys, span, pairs)
        for index, pair in enumerate(pairs):
            natural[0, span, index * 128 : index * 128 + 128] = pair.astype(bf16)
            flipped[index * 128 : index * 128 + 128, span] = pair.T.astype(bf16)
        made = nn(normed[span, :], weight[:, QW + KW :])
        forms_of(values, span, [made[:, :128], made[:, 128:]])
        natural[1, span, :] = made.astype(bf16)
        return carry

    lax.fori_loop(0, 2, project, 0)
    stores = [
        copied(query, q_out, out_sems.at[0]),
        copied(natural.at[0], k_out, out_sems.at[1]),
        copied(natural.at[1], v_out, out_sems.at[2]),
        copied(flipped, kt_out, out_sems.at[3]),
        copied(normed.at[:, pl.ds(0, D)], n_out, out_sems.at[4]),
        copied(cosine, cos_out, out_sems.at[5]),
        copied(sine, sin_out, out_sems.at[6]),
        copied(inner_t, zt_out, out_sems.at[9]),
    ]
    for store in stores:
        store.start()

    for block in range(2 * rows // BLOCK):
        low, high = block * BLOCK, (block + 1) * BLOCK
        place = lax.broadcasted_iota(jnp.int32, (BLOCK, 1), 0).astype(f32) + low
        begin = start_at(place, starts)
        for first in range(0, high, BLOCK):
            key_place = lanes((BLOCK, BLOCK)).astype(f32) + first
            allowed = key_place >= begin
            if first == low:
                allowed = allowed & (key_place <= place)
            bias[:, first : first + BLOCK] = jnp.where(allowed, 0.0, masked_value)

        def group(j, carry, low=low, high=high):
            for member in range(GROUP):
                slot = j * GROUP + member + g
                pair, parity = slot // 2, slot % 2
                form = (j + g) * 2 + parity
                at = pl.ds(pl.multiple_of(pair * 128, 128), 128)
                scores = nt(query[low:high, at], keys[form, :high, :]) + bias[:, :high]
                top = jnp.max(scores, axis=-1, keepdims=True)
                chances = jnp.exp(scores - top)
                total = jnp.sum(chances, axis=-1, keepdims=True)
                mixed[member, j] = (nn(chances.astype(bf16), values[form, :high, :]) / total).astype(bf16)
                logs[member, j] = jnp.broadcast_to(top + jnp.log(total), (BLOCK, 128))
            return carry

        lax.fori_loop(0, HEADS // GROUP, group, 0)
        for pair in range(QW // 128):
            both = [
                by_slot(g, slot, lambda head: mixed[head % GROUP, head // GROUP])
                for slot in (2 * pair, 2 * pair + 1)
            ]
            mixed_low[low:high, pair * 128 : pair * 128 + 128] = both[0] + both[1]
        lane = lanes((BLOCK, 128))
        merged = jnp.zeros((BLOCK, 128), f32)
        for head in range(HEADS):
            merged = jnp.where(lane == head, logs[head % GROUP, head // GROUP], merged)
        lse[:, low:high] = merged.T[:R, :]
    last = [
        copied(mixed_low.at[here], o_own, out_sems.at[7]),
        copied(mixed_low.at[there], o_send, out_sems.at[8]),
    ]
    for store in last:
        store.start()
    last.append(copied(lse, lse_out, out_sems.at[10]))
    last[-1].start()
    for store in stores + last:
        store.wait()


def attend(adapter, tok_own, *rest):
    rows = tok_own.shape[0]
    length = 2 * rows
    shape = jax.ShapeDtypeStruct
    return pl.pallas_call(
        attend_kernel,
        out_shape=[
            shape((rows, QW), bf16),
            shape((rows, QW), bf16),
            shape((length, QW), bf16),
            shape((length, KW), bf16),
            shape((length, KW), bf16),
            shape((KW, length), bf16),
            shape((length, D), bf16),
            shape((3 * R, length), bf16),
            shape((R, length), f32),
            shape((length, 128), f32),
            shape((length, 128), f32),
        ],
        in_specs=[SMEM, HBM, ANY, HBM, ANY] + [HBM] * 3 + [VMEM] * 4,
        out_specs=[HBM] * 11,
        scratch_shapes=[
            pltpu.VMEM((length, D), bf16),
            pltpu.VMEM((length, AUG), bf16),
            pltpu.VMEM((AUG, SPAN), bf16),
            pltpu.VMEM((128, D), bf16),
            pltpu.VMEM((length, QW), bf16),
            pltpu.VMEM((2, length, KW), bf16),
            pltpu.VMEM((KW, length), bf16),
            pltpu.VMEM((8, length, 128), bf16),
            pltpu.VMEM((8, length, 128), bf16),
            pltpu.VMEM((GROUP, HEADS // GROUP, BLOCK, 128), bf16),
            pltpu.VMEM((length, QW), bf16),
            pltpu.VMEM((GROUP, HEADS // GROUP, BLOCK, 128), f32),
            pltpu.VMEM((BLOCK, length), f32),
            pltpu.VMEM((length, 128), f32),
            pltpu.VMEM((length, 128), f32),
            pltpu.VMEM((3 * R, length), bf16),
            pltpu.VMEM((R, length), f32),
            pltpu.SemaphoreType.DMA((5,)),
            pltpu.SemaphoreType.DMA((9,)),
            pltpu.SemaphoreType.DMA((11,)),
        ],
        compiler_params=pltpu.CompilerParams(vmem_limit_bytes=VMEM_BYTES),
        cost_estimate=pl.CostEstimate(
            flops=16 * 10**9, bytes_accessed=16 << 20, transcendentals=6 * 10**6
        ),
        name="attend",
    )(adapter, tok_own, *rest)


def normed_back(rows, gain_row, grad):
    scale = lax.rsqrt(jnp.mean(rows * rows, axis=-1, keepdims=True) + epsilon)
    scaled = grad * gain_row
    inside = jnp.mean(rows * scaled, axis=-1, keepdims=True)
    return scale * (scaled - rows * (scale * scale * inside))


def rounded_up(count, unit):
    return -(-count // unit) * unit


def feed_lanes(reps):
    return rounded_up((5 * D + 3 * FF) // reps, 256)


def qkv_lanes(reps):
    return rounded_up((4 * D + 2 * KV) // reps + 1, 128)


def packed(grads, reps, target):
    for rep in range(reps):
        at = 0
        for grad in grads:
            piece = grad.shape[-1] // reps
            share = grad[:, rep * piece : (rep + 1) * piece]
            target[rep * R : (rep + 1) * R, at : at + piece] = share.astype(target.dtype)
            at += piece


def feed_kernel(
    reps,
    adapter,
    o_own_in,
    o_oth_in,
    tok_in,
    cot_in,
    wo_own,
    wo_oth,
    wgu_own,
    wgu_oth,
    wd_own,
    wd_oth,
    a_down,
    lower_t,
    upper_width,
    upper_hidden,
    gains_own,
    gains_oth,
    layer_out,
    grad_middle,
    do_own_out,
    do_oth_out,
    pack_own_out,
    pack_send_out,
    o_own,
    o_oth,
    tok,
    cot,
    do_own,
    do_oth,
    wout,
    wg,
    wu,
    wd,
    at_out,
    at_gu,
    b_out,
    b_down,
    middle,
    normed,
    cot_aug,
    total,
    back,
    result,
    z_gu_t,
    dz_down_t,
    ga_out,
    gb_gate,
    gb_up,
    ga_down,
    pack,
    sems,
    o_sems,
    out_sems,
):
    g = lax.axis_index("grp")
    chosen = adapter[0]
    gain = gain_row(g, gains_own, gains_oth, 1)
    steps = FF // TILE
    each = steps // 2
    w_here = pl.ds(pl.multiple_of(g * HALF, 64), HALF)
    w_there = pl.ds(pl.multiple_of((1 - g) * HALF, 64), HALF)

    def column(step):
        owner = jnp.where(step < each, g, 1 - g)
        return owner * (FF // 2) + (step % each) * TILE

    def copies(step, slot):
        at = pl.multiple_of(column(step), TILE)
        gate_at = pl.ds(at, TILE)
        up_at = pl.ds(pl.multiple_of(FF + at, TILE), TILE)
        sem = lambda k: sems.at[slot, k]
        return [
            copied(wgu_own.at[:, gate_at], wg.at[slot, w_here], sem(0)),
            copied(wgu_oth.at[:, gate_at], wg.at[slot, w_there], sem(1)),
            copied(wgu_own.at[:, up_at], wu.at[slot, w_here], sem(2)),
            copied(wgu_oth.at[:, up_at], wu.at[slot, w_there], sem(3)),
            copied(upper_hidden.at[0, chosen, :, gate_at], wg.at[slot, pl.ds(D, R)], sem(4)),
            copied(upper_hidden.at[1, chosen, :, gate_at], wu.at[slot, pl.ds(D + R, R)], sem(5)),
            copied(a_down.at[gate_at], wd.at[slot, :, pl.ds(D, 128)], sem(6)),
        ]

    def down_copy(source, step, slot):
        local = pl.ds(pl.multiple_of((step % each) * TILE, TILE), TILE)
        return copied(source.at[local], wd.at[slot, :, pl.ds(0, D)], sems.at[slot, 7])

    def start(step, slot):
        for copy in copies(step, slot):
            copy.start()

        @pl.when(step < each)
        def _():
            down_copy(wd_own, step, slot).start()

        @pl.when(step >= each)
        def _():
            down_copy(wd_oth, step, slot).start()

    def wait(step, slot):
        for copy in copies(step, slot):
            copy.wait()
        down_copy(wd_own, step, slot).wait()

    for slot in range(2):
        wg[slot, D:, :] = jnp.zeros((128, TILE), bf16)
        wu[slot, D:, :] = jnp.zeros((128, TILE), bf16)
        at_out[slot] = jnp.zeros((128, QW), bf16)
        wout[slot, :64, :] = jnp.zeros((64, D), bf16)
        wout[slot, HALF:, :] = jnp.zeros((64, D), bf16)
    for ref in (at_gu, b_out, b_down):
        ref[...] = jnp.zeros_like(ref)
    own_at = pl.multiple_of(g * 512, 128)
    oth_at = pl.multiple_of((1 - g) * 512, 128)
    loads = [
        copied(wo_own, wout.at[0, pl.ds(pl.multiple_of(g * HD, HD), HALF)], o_sems.at[0]),
        copied(wo_oth, wout.at[1, pl.ds(pl.multiple_of((1 - g) * HD, HD), HALF)], o_sems.at[1]),
        copied(lower_t.at[3, chosen, :, pl.ds(own_at, QW)], at_out.at[0, pl.ds(0, R)], o_sems.at[2]),
        copied(lower_t.at[3, chosen, :, pl.ds(oth_at, QW)], at_out.at[1, pl.ds(0, R)], o_sems.at[3]),
        copied(lower_t.at[4, chosen], at_gu.at[pl.ds(0, R)], o_sems.at[4]),
        copied(lower_t.at[5, chosen], at_gu.at[pl.ds(R, R)], o_sems.at[5]),
        copied(upper_width.at[1, chosen], b_out.at[pl.ds(0, R)], o_sems.at[6]),
        copied(upper_width.at[2, chosen], b_down.at[pl.ds(0, R)], o_sems.at[7]),
        copied(o_own_in, o_own, o_sems.at[8]),
        copied(o_oth_in, o_oth, o_sems.at[9]),
        copied(tok_in, tok, o_sems.at[10]),
        copied(cot_in, cot, o_sems.at[11]),
    ]
    first, second, third = loads[11:] + loads[7:8], loads[:4] + loads[8:10], loads[4:7] + loads[10:11]
    for load in first + second + third:
        load.start()
    total[...] = jnp.zeros_like(total)
    back[...] = jnp.zeros_like(back)
    for load in first:
        load.wait()
    cot_aug[:, :D] = cot[...]
    dz_down = nt(cot[...], b_down[...])
    cot_aug[:, D:] = dz_down.astype(bf16)
    dz_down_t[...] = dz_down.T[:R, :].astype(bf16)
    for load in second + third:
        load.wait()
    start(0, 0)
    inner_out = (nt(o_own[...], at_out[0]) + nt(o_oth[...], at_out[1])).astype(bf16)
    middle[...] = (
        tok[...].astype(f32)
        + nn(o_own[...], wout[0])
        + nn(o_oth[...], wout[1])
        + nn(inner_out, b_out[...])
    )
    scale = lax.rsqrt(jnp.mean(middle[...] * middle[...], axis=-1, keepdims=True) + epsilon)
    normed[:, :D] = (middle[...] * scale * gain).astype(bf16)
    inner_gu = nt(normed[:, :D], at_gu[...])
    normed[:, D:] = inner_gu.astype(bf16)
    z_gu_t[...] = inner_gu.T[: 2 * R, :].astype(bf16)

    def step_body(step, carry):
        slot = step % 2

        @pl.when(step + 1 < steps)
        def _():
            start(step + 1, 1 - slot)

        wait(step, slot)
        gate_at = pl.ds(pl.multiple_of(column(step), TILE), TILE)
        gate = nn(normed[...], wg[slot])
        up = nn(normed[...], wu[slot])
        grad_active = nt(cot_aug[...], wd[slot])
        sigmoid = 1.0 / (1.0 + jnp.exp(-gate))
        silu = gate * sigmoid
        active = (silu * up).astype(bf16)
        grad_gate = (grad_active * up * (sigmoid * (1.0 + gate * (1.0 - sigmoid)))).astype(bf16)
        grad_up = (grad_active * silu).astype(bf16)
        total[...] += nn(active, wd[slot])
        back[...] += nt(grad_gate, wg[slot]) + nt(grad_up, wu[slot])
        gb_gate[:, gate_at] = nn(z_gu_t[...], grad_gate)[:R]
        gb_up[:, gate_at] = nn(z_gu_t[...], grad_up)[R:]
        ga_down[:, gate_at] = nn(dz_down_t[...], active)
        return carry

    lax.fori_loop(0, steps, step_body, 0)

    inner_down = total[:, D:].astype(bf16)
    result[...] = (middle[...] + total[:, :D] + nn(inner_down, b_down[...])).astype(bf16)
    stores = [copied(result, layer_out, out_sems.at[0])]
    stores[0].start()
    gb_down = nn(total[:, D:].T[:R, :].astype(bf16), cot[...])
    dz_gu = back[:, D:].astype(bf16)
    grad_normed = back[:, :D] + nn(dz_gu, at_gu[...])
    ga_gu = nn(back[:, D:].T[: 2 * R, :].astype(bf16), normed[:, :D])
    grad = cot[...].astype(f32) + normed_back(middle[...], gain, grad_normed)
    total[:, :D] = grad
    stores.append(copied(total.at[:, pl.ds(0, D)], grad_middle, out_sems.at[1]))
    stores[1].start()
    branch = grad.astype(bf16)
    dz_out = nt(branch, b_out[...])
    dz_out_low = dz_out.astype(bf16)
    dz_out_t = dz_out.T[:R, :].astype(bf16)
    do_oth[...] = (nt(branch, wout[1]) + nn(dz_out_low, at_out[1])).astype(bf16)
    stores.append(copied(do_oth, do_oth_out, out_sems.at[2]))
    stores[-1].start()
    do_own[...] = (nt(branch, wout[0]) + nn(dz_out_low, at_out[0])).astype(bf16)
    stores.append(copied(do_own, do_own_out, out_sems.at[3]))
    stores[-1].start()
    gb_out = nn(inner_out.astype(f32).T[:R, :].astype(bf16), branch)
    ga_out[...] = jnp.zeros_like(ga_out)
    ga_out[:, pl.ds(own_at, QW)] += nn(dz_out_t, o_own[...])
    ga_out[:, pl.ds(oth_at, QW)] += nn(dz_out_t, o_oth[...])
    pack[...] = jnp.zeros_like(pack)
    packed(
        [ga_out[...], ga_gu[:R], ga_gu[R:], gb_out, gb_down, ga_down[...], gb_gate[...], gb_up[...]],
        reps,
        pack,
    )
    half = pack.shape[1] // 2
    for index, (side, target) in enumerate(((g, pack_own_out), (1 - g, pack_send_out))):
        source = pack.at[:, pl.ds(pl.multiple_of(side * half, 128), half)]
        stores.append(copied(source, target, out_sems.at[4 + index]))
        stores[-1].start()
    for store in stores:
        store.wait()


def feed(reps, *args):
    rows = args[3].shape[0]
    half = feed_lanes(reps) // 2
    shape = jax.ShapeDtypeStruct
    return pl.pallas_call(
        functools.partial(feed_kernel, reps),
        out_shape=[
            shape((rows, D), bf16),
            shape((rows, D), f32),
            shape((rows, QW), bf16),
            shape((rows, QW), bf16),
            shape((reps * R, half), bf16),
            shape((reps * R, half), bf16),
        ],
        in_specs=[SMEM, HBM, ANY] + [HBM] * 12 + [VMEM] * 2,
        out_specs=[HBM] * 6,
        scratch_shapes=[
            pltpu.VMEM((rows, QW), bf16),
            pltpu.VMEM((rows, QW), bf16),
            pltpu.VMEM((rows, D), bf16),
            pltpu.VMEM((rows, D), bf16),
            pltpu.VMEM((rows, QW), bf16),
            pltpu.VMEM((rows, QW), bf16),
            pltpu.VMEM((2, QW, D), bf16),
            pltpu.VMEM((2, AUG, TILE), bf16),
            pltpu.VMEM((2, AUG, TILE), bf16),
            pltpu.VMEM((2, TILE, AUG), bf16),
            pltpu.VMEM((2, 128, QW), bf16),
            pltpu.VMEM((128, D), bf16),
            pltpu.VMEM((128, D), bf16),
            pltpu.VMEM((128, D), bf16),
            pltpu.VMEM((rows, D), f32),
            pltpu.VMEM((rows, AUG), bf16),
            pltpu.VMEM((rows, AUG), bf16),
            pltpu.VMEM((rows, AUG), f32),
            pltpu.VMEM((rows, AUG), f32),
            pltpu.VMEM((rows, D), bf16),
            pltpu.VMEM((2 * R, rows), bf16),
            pltpu.VMEM((R, rows), bf16),
            pltpu.VMEM((R, D), f32),
            pltpu.VMEM((R, FF), f32),
            pltpu.VMEM((R, FF), f32),
            pltpu.VMEM((R, FF), f32),
            pltpu.VMEM((reps * R, 2 * half), bf16),
            pltpu.SemaphoreType.DMA((2, 8)),
            pltpu.SemaphoreType.DMA((12,)),
            pltpu.SemaphoreType.DMA((6,)),
        ],
        compiler_params=pltpu.CompilerParams(vmem_limit_bytes=VMEM_BYTES),
        cost_estimate=pl.CostEstimate(
            flops=30 * 10**9, bytes_accessed=36 << 20, transcendentals=2 * 10**6
        ),
        name="feed",
    )(*args)


def attend_back_kernel(
    reps,
    adapter,
    do_own,
    do_oth,
    o_own,
    o_oth,
    normed,
    qkv_own,
    qkv_oth,
    lower_t,
    upper_width,
    upper_keys,
    query_in,
    k_in,
    v_in,
    flipped_in,
    zt_in,
    lse_in,
    cos_in,
    sin_in,
    segments,
    pack_own_in,
    pack_oth_in,
    dy_out,
    dz_out,
    part_out,
    exchange_out,
    query,
    natural,
    flipped,
    zt,
    lse,
    cosine,
    sine,
    pack_own,
    pack_oth,
    inner_low,
    exchange,
    outgoing,
    maps,
    grad_o,
    mixed,
    n_rows,
    weight,
    keys,
    values,
    delta,
    dqt,
    dk,
    dv,
    dy,
    bias,
    gb_q,
    gb_kv,
    pack,
    sems,
    b_sems,
    out_sem,
):
    g = lax.axis_index("grp")
    chosen = adapter[0]
    rows = do_own.shape[0]
    length = 2 * rows
    here = pl.ds(pl.multiple_of(g * rows, 128), rows)
    there = pl.ds(pl.multiple_of((1 - g) * rows, 128), rows)
    weight[D:, :] = jnp.zeros((128, SPAN), bf16)
    maps[...] = jnp.zeros_like(maps)
    loads = [
        copied(do_own, grad_o.at[here], sems.at[0]),
        copied(do_oth, grad_o.at[there], sems.at[1]),
        copied(o_own, mixed.at[here], sems.at[2]),
        copied(o_oth, mixed.at[there], sems.at[3]),
        copied(query_in, query, sems.at[5]),
        copied(flipped_in, flipped, sems.at[6]),
        copied(lse_in, lse, sems.at[7]),
    ]
    early = [
        copied(k_in, natural.at[0], sems.at[8]),
        copied(v_in, natural.at[1], sems.at[9]),
    ]
    late = [
        copied(zt_in, zt, sems.at[10]),
        copied(pack_own_in, pack_own, sems.at[11]),
        copied(pack_oth_in, pack_oth, sems.at[12]),
        copied(normed, n_rows, sems.at[4]),
    ] + [
        copied(lower_t.at[index, chosen], maps.at[pl.ds(index * R, R)], sems.at[15 + index])
        for index in range(3)
    ] + qkv_loads(g, chosen, qkv_own, qkv_oth, upper_width, upper_keys, weight, b_sems)
    turns = [copied(cos_in, cosine, sems.at[13]), copied(sin_in, sine, sems.at[14])]
    for load in early + loads + turns + late:
        load.start()
    dk[...] = jnp.zeros_like(dk)
    dv[...] = jnp.zeros_like(dv)
    for load in early:
        load.wait()

    def rebuild(part, carry):
        span = pl.ds(pl.multiple_of(part * rows, 128), rows)
        for index, store in enumerate((keys, values)):
            forms_of(
                store, span, [natural[index, span, at : at + 128].astype(f32) for at in (0, 128)]
            )
        return carry

    lax.fori_loop(0, 2, rebuild, 0)
    starts = doc_starts(segments[...])
    ones = (
        lanes((R, QW)) // HD == lax.broadcasted_iota(jnp.int32, (R, QW), 0)
    ).astype(bf16)
    for load in loads:
        load.wait()
    for part in range(2):
        span = slice(part * rows, (part + 1) * rows)
        product = grad_o[span, :].astype(f32) * mixed[span, :].astype(f32)
        upper = product.astype(bf16)
        lower = (product - upper.astype(f32)).astype(bf16)
        delta[:, span] = nt(ones, upper) + nt(ones, lower)

    for block in range(length // BLOCK):
        low, high = block * BLOCK, (block + 1) * BLOCK
        place = lanes((1, BLOCK)).astype(f32) + low
        begin = start_at(place, starts)
        for first in range(0, high, BLOCK):
            key_place = lax.broadcasted_iota(jnp.int32, (BLOCK, BLOCK), 0).astype(f32) + first
            allowed = key_place >= begin
            if first == low:
                allowed = allowed & (key_place <= place)
            bias[first : first + BLOCK, :] = jnp.where(allowed, 0.0, masked_value)

        def group(j, carry, low=low, high=high):
            key_slot = j + g
            flip = flipped[pl.ds(pl.multiple_of(key_slot * HD, HD), HD), :high]
            value_grads, key_grads = [], []
            for member in range(GROUP):
                slot = j * GROUP + member + g
                pair, parity = slot // 2, slot % 2
                form = key_slot * 2 + parity
                at = pl.ds(pl.multiple_of(pair * 128, 128), 128)
                q_rows = query[low:high, at]
                g_rows = grad_o[low:high, at]
                logs = lse[pl.ds(j * GROUP + member, 1), low:high]
                deltas = delta[pl.ds(slot, 1), low:high]
                scores = nt(keys[form, :high, :], q_rows) + bias[:high, :]
                chances = jnp.exp(scores - logs)
                grad_chances = nt(values[form, :high, :], g_rows)
                grad_scores = (chances * (grad_chances - deltas)).astype(bf16)
                value_grads.append(nn(chances.astype(bf16), g_rows))
                key_grads.append(nn(grad_scores, q_rows))
                dqt[member, j, :, low:high] = nn(flip, grad_scores)
            dv[0, j, :high, :] += value_grads[0] + value_grads[2]
            dv[1, j, :high, :] += value_grads[1]
            dk[0, j, :high, :] += key_grads[0] + key_grads[2]
            dk[1, j, :high, :] += key_grads[1]
            return carry

        lax.fori_loop(0, HEADS // GROUP, group, 0)

    def gathered(acc, span):
        low = lanes((rows, 128)) < HD
        heads = []
        for j in range(HEADS // GROUP):
            odd = (j * GROUP + g) % 2 == 1
            even_sum = jnp.where(odd, acc[1, j, span, :], acc[0, j, span, :])
            odd_sum = jnp.where(odd, acc[0, j, span, :], acc[1, j, span, :])
            heads.append((even_sum, odd_sum))

        def place(slot):
            def pick(j):
                even_sum, odd_sum = heads[j]
                if slot % 2 == 0:
                    return jnp.where(low, even_sum + pltpu.roll(odd_sum, HD, 1), 0.0)
                return jnp.where(low, 0.0, odd_sum + pltpu.roll(even_sum, HD, 1))

            zero = pick(slot) if slot < 3 else jnp.zeros((rows, 128), f32)
            one = pick(slot - 1) if slot > 0 else jnp.zeros((rows, 128), f32)
            return jnp.where(g == 0, zero, one)

        return place(0) + place(1), place(2) + place(3)

    def unturn(part, carry):
        span = pl.ds(pl.multiple_of(part * rows, 128), rows)
        cos_rows = cosine[span, :]
        sin_rows = -sine[span, :]
        cos_t = cos_rows.T[: HD // 2, :]
        sin_t = sin_rows.T[: HD // 2, :]
        for pair in range(QW // 128):
            blocks = []
            for slot in (2 * pair, 2 * pair + 1):
                block = by_slot(g, slot, lambda head: dqt[head % GROUP, head // GROUP, :, span])
                top, bottom = block[: HD // 2], block[HD // 2 :]
                blocks.append(top * cos_t + bottom * sin_t)
                blocks.append(bottom * cos_t - top * sin_t)
            made = (jnp.concatenate(blocks, axis=0) * HD**-0.5).astype(bf16)
            dy[span, pair * 128 : pair * 128 + 128] = made.T
        for index, acc in enumerate(gathered(dk, span)):
            at = QW + index * 128
            dy[span, at : at + 128] = turned(acc, cos_rows, sin_rows).astype(bf16)
        for index, acc in enumerate(gathered(dv, span)):
            at = QW + KW + index * 128
            dy[span, at : at + 128] = acc.astype(bf16)
        return carry

    for load in turns:
        load.wait()
    lax.fori_loop(0, 2, unturn, 0)
    store = copied(dy.at[here], dy_out, out_sem.at[0])
    store.start()
    for load in late:
        load.wait()
    gb = nn(zt[...], dy[...])
    gb_q[...] = jnp.zeros_like(gb_q)
    gb_kv[...] = jnp.zeros_like(gb_kv)
    gb_q[:, pl.ds(pl.multiple_of(g * 512, 128), QW)] = gb[:R, :QW]
    for index in range(2):
        gb_kv[index, :, pl.ds(pl.multiple_of(g * 128, 128), KW)] = gb[
            (index + 1) * R : (index + 2) * R, QW + index * KW : QW + (index + 1) * KW
        ]
    made = nt(dy[there, :], weight[...])
    theirs = made[:, D:]
    outgoing[...] = (made[:, :D] + nn(theirs.astype(bf16), maps[...])).astype(bf16)
    part_store = copied(outgoing, part_out, out_sem.at[3])
    part_store.start()
    mine = nt(dy[here, :], weight[D:, :])
    inner_low[...] = mine.astype(bf16)
    inner_store = copied(inner_low, dz_out, out_sem.at[1])
    inner_store.start()
    ga = nn(theirs.T[: 3 * R, :].astype(bf16), n_rows[there, :]) + nn(
        mine.T[: 3 * R, :].astype(bf16), n_rows[here, :]
    )
    pack[...] = jnp.zeros_like(pack)
    packed(
        [ga[:R], ga[R : 2 * R], ga[2 * R :], gb_q[...], gb_kv[0], gb_kv[1]],
        reps,
        pack,
    )
    half = pack_own.shape[1]
    width = pack.shape[1]
    exchange[:, :half] = (pack_own[...].astype(f32) + pack_oth[...].astype(f32)).astype(bf16)
    exchange[:, half:] = jnp.where(
        lanes(pack.shape) == width - 1, chosen.astype(f32), pack[...].astype(f32)
    ).astype(bf16)
    last = copied(exchange, exchange_out, out_sem.at[2])
    last.start()
    for copy in (store, inner_store, part_store, last):
        copy.wait()


def attend_back(reps, *args):
    rows = args[1].shape[0]
    length = 2 * rows
    half = feed_lanes(reps) // 2
    width = qkv_lanes(reps)
    shape = jax.ShapeDtypeStruct
    return pl.pallas_call(
        functools.partial(attend_back_kernel, reps),
        out_shape=[
            shape((rows, SPAN), bf16),
            shape((rows, 128), bf16),
            shape((rows, D), bf16),
            shape((reps * R, half + width), bf16),
        ],
        in_specs=[SMEM, HBM, ANY] + [HBM] * 16 + [VMEM, HBM, ANY],
        out_specs=[HBM] * 4,
        scratch_shapes=[
            pltpu.VMEM((length, QW), bf16),
            pltpu.VMEM((2, length, KW), bf16),
            pltpu.VMEM((KW, length), bf16),
            pltpu.VMEM((3 * R, length), bf16),
            pltpu.VMEM((R, length), f32),
            pltpu.VMEM((length, 128), f32),
            pltpu.VMEM((length, 128), f32),
            pltpu.VMEM((reps * R, half), bf16),
            pltpu.VMEM((reps * R, half), bf16),
            pltpu.VMEM((rows, 128), bf16),
            pltpu.VMEM((reps * R, half + width), bf16),
            pltpu.VMEM((rows, D), bf16),
            pltpu.VMEM((128, D), bf16),
            pltpu.VMEM((length, QW), bf16),
            pltpu.VMEM((length, QW), bf16),
            pltpu.VMEM((length, D), bf16),
            pltpu.VMEM((AUG, SPAN), bf16),
            pltpu.VMEM((8, length, 128), bf16),
            pltpu.VMEM((8, length, 128), bf16),
            pltpu.VMEM((R, length), f32),
            pltpu.VMEM((GROUP, HEADS // GROUP, HD, length), f32),
            pltpu.VMEM((2, HEADS // GROUP, length, 128), f32),
            pltpu.VMEM((2, HEADS // GROUP, length, 128), f32),
            pltpu.VMEM((length, SPAN), bf16),
            pltpu.VMEM((length, BLOCK), f32),
            pltpu.VMEM((R, D), f32),
            pltpu.VMEM((2, R, KV), f32),
            pltpu.VMEM((reps * R, width), bf16),
            pltpu.SemaphoreType.DMA((18,)),
            pltpu.SemaphoreType.DMA((9,)),
            pltpu.SemaphoreType.DMA((4,)),
        ],
        compiler_params=pltpu.CompilerParams(vmem_limit_bytes=VMEM_BYTES),
        cost_estimate=pl.CostEstimate(
            flops=24 * 10**9, bytes_accessed=20 << 20, transcendentals=6 * 10**6
        ),
        name="attend_back",
    )(*args)


def finish_kernel(
    adapter,
    dy_in,
    dz_in,
    qkv_own,
    qkv_oth,
    lower_t,
    tok_in,
    gains_own,
    gains_oth,
    part_in,
    middle_in,
    out,
    dy,
    dz,
    tok,
    part,
    grad_middle,
    weight,
    maps,
    result,
    sems,
    w_sems,
    out_sem,
):
    g = lax.axis_index("grp")
    chosen = adapter[0]
    maps[...] = jnp.zeros_like(maps)
    loads = qkv_loads(g, chosen, qkv_own, qkv_oth, None, None, weight, w_sems)
    for index, (source, target) in enumerate(
        ((dy_in, dy), (dz_in, dz), (tok_in, tok), (middle_in, grad_middle), (part_in, part))
    ):
        loads.append(copied(source, target, sems.at[index]))
    for index in range(3):
        loads.append(
            copied(lower_t.at[index, chosen], maps.at[pl.ds(index * R, R)], sems.at[5 + index])
        )
    for load in loads:
        load.start()
    gain = gain_row(g, gains_own, gains_oth, 0)
    for load in loads:
        load.wait()
    grad = nt(dy[...], weight[...]) + nn(dz[...], maps[...]) + part[...].astype(f32)
    result[...] = (
        grad_middle[...] + normed_back(tok[...].astype(f32), gain, grad)
    ).astype(bf16)
    store = copied(result, out, out_sem.at[0])
    store.start()
    store.wait()


def finish(*args):
    rows = args[1].shape[0]
    return pl.pallas_call(
        finish_kernel,
        out_shape=jax.ShapeDtypeStruct((rows, D), bf16),
        in_specs=[SMEM] + [HBM] * 6 + [VMEM] * 2 + [ANY, HBM],
        out_specs=HBM,
        scratch_shapes=[
            pltpu.VMEM((rows, SPAN), bf16),
            pltpu.VMEM((rows, 128), bf16),
            pltpu.VMEM((rows, D), bf16),
            pltpu.VMEM((rows, D), bf16),
            pltpu.VMEM((rows, D), f32),
            pltpu.VMEM((D, SPAN), bf16),
            pltpu.VMEM((128, D), bf16),
            pltpu.VMEM((rows, D), bf16),
            pltpu.SemaphoreType.DMA((8,)),
            pltpu.SemaphoreType.DMA((6,)),
            pltpu.SemaphoreType.DMA((1,)),
        ],
        compiler_params=pltpu.CompilerParams(vmem_limit_bytes=VMEM_BYTES),
        cost_estimate=pl.CostEstimate(
            flops=4 * 10**9, bytes_accessed=10 << 20, transcendentals=0
        ),
        name="finish",
    )(*args)


def collect_kernel(source, keep, send, received, sem):
    load = copied(source, received, sem.at[0])
    load.start()
    load.wait()
    g = lax.axis_index("grp")
    count, width = received.shape
    quota = NAD // 2
    label = received[:, width - 1 :].astype(f32)
    lane = lanes((count, NAD * R))
    row = lax.broadcasted_iota(jnp.int32, (count, NAD * R), 0)
    picks = ((lane // R).astype(f32) == label) & (lane % R == row % R)
    sums = tn(picks.astype(f32).astype(bf16), received[...])
    first = g == 0
    for adapter in range(quota):
        low = sums[adapter * R : (adapter + 1) * R]
        high = sums[(quota + adapter) * R : (quota + adapter + 1) * R]
        keep[adapter] = jnp.where(first, low, high)
        send[adapter] = jnp.where(first, high, low)


def collect(received):
    shape = jax.ShapeDtypeStruct((NAD // 2, R, received.shape[1]), f32)
    return pl.pallas_call(
        collect_kernel,
        out_shape=[shape, shape],
        in_specs=[ANY],
        out_specs=[VMEM] * 2,
        scratch_shapes=[
            pltpu.VMEM(received.shape, bf16),
            pltpu.SemaphoreType.DMA((1,)),
        ],
        compiler_params=pltpu.CompilerParams(vmem_limit_bytes=VMEM_BYTES),
        cost_estimate=pl.CostEstimate(flops=10**8, bytes_accessed=2 << 20, transcendentals=0),
        name="collect",
    )(received)


def deliver_kernel(reps, keep, other, lower, down, width, keys, hidden, feeds, qkvs):
    g = lax.axis_index("grp")
    half = feeds.shape[-1] // 2
    feeds[:, :, pl.ds(pl.multiple_of(g * half, 128), half)] = keep[:, :, :half]
    feeds[:, :, pl.ds(pl.multiple_of((1 - g) * half, 128), half)] = other[:, :, :half]
    qkvs[...] = keep[:, :, half:] + other[:, :, half:]
    piece, tall, short = D // reps, FF // reps, KV // reps
    for index in range(3):
        lower[index] = qkvs[:, :, index * piece : (index + 1) * piece]
        lower[3 + index] = feeds[:, :, index * piece : (index + 1) * piece]
    width[0] = qkvs[:, :, 3 * piece : 4 * piece]
    width[1] = feeds[:, :, 3 * piece : 4 * piece]
    width[2] = feeds[:, :, 4 * piece : 5 * piece]
    for index in range(2):
        at = 4 * piece + index * short
        keys[index] = qkvs[:, :, at : at + short]
        at = 5 * piece + (1 + index) * tall
        hidden[index] = feeds[:, :, at : at + tall]
    down[...] = feeds[:, :, 5 * piece : 5 * piece + tall]


def deliver(reps, keep, other):
    quota = NAD // 2
    shape = lambda *dims: jax.ShapeDtypeStruct(dims, f32)
    return pl.pallas_call(
        functools.partial(deliver_kernel, reps),
        out_shape=[
            shape(6, quota, R, D // reps),
            shape(quota, R, FF // reps),
            shape(3, quota, R, D // reps),
            shape(2, quota, R, KV // reps),
            shape(2, quota, R, FF // reps),
        ],
        in_specs=[VMEM] * 2,
        out_specs=[VMEM] * 5,
        scratch_shapes=[
            pltpu.VMEM((quota, R, feed_lanes(reps)), f32),
            pltpu.VMEM((quota, R, qkv_lanes(reps)), f32),
        ],
        compiler_params=pltpu.CompilerParams(vmem_limit_bytes=VMEM_BYTES),
        cost_estimate=pl.CostEstimate(flops=10**6, bytes_accessed=1 << 20, transcendentals=0),
        name="deliver",
    )(keep, other)


def per_device(
    tokens,
    cotangent,
    segment_ids,
    adapter_ids,
    norm_gains,
    frozen_qkv,
    frozen_out,
    frozen_gate_up,
    frozen_down,
    lower_mats,
    lower_down,
    upper_width,
    upper_keys,
    upper_hidden,
):
    reps = lax.axis_size("rep")
    chosen = adapter_ids[0]
    first = lax.axis_index("grp") == 0
    swap = lambda value: lax.ppermute(value, "grp", SWAP)

    tok_own = tokens[0]
    tok_oth = swap(tok_own)
    qkv_oth = swap(frozen_qkv)
    gains_oth = swap(norm_gains)
    a_down = jnp.pad(
        lax.dynamic_index_in_dim(lower_down, chosen, 0, keepdims=False), ((0, 0), (0, 128 - R))
    )
    tok_oth, qkv_oth, gains_oth, a_down, wo, wgu, wd = lax.optimization_barrier(
        (tok_oth, qkv_oth, gains_oth, a_down, frozen_out, frozen_gate_up, frozen_down)
    )
    wo_oth = swap(wo)
    wgu_oth = swap(wgu)
    wd_oth = swap(wd)

    lower_t = lower_mats.transpose(0, 1, 3, 2)
    lane = jnp.arange(128, dtype=jnp.int32)
    freqs = theta_base ** (-(lane % (HD // 2)).astype(f32) * 2.0 / HD)
    gains = (norm_gains, gains_oth)

    (o_own, o_send, query, natural_k, natural_v, flipped, normed, zt, lse, cosine, sine) = attend(
        adapter_ids,
        tok_own,
        tok_oth,
        frozen_qkv,
        qkv_oth,
        lower_t,
        upper_width,
        upper_keys,
        *gains,
        segment_ids,
        freqs[None],
    )
    o_oth = swap(o_send)
    layer_out, grad_middle, do_own, do_send, pack_own, pack_send = feed(
        reps,
        adapter_ids,
        o_own,
        o_oth,
        tok_own,
        cotangent[0],
        frozen_out,
        wo_oth,
        frozen_gate_up,
        wgu_oth,
        frozen_down,
        wd_oth,
        a_down,
        lower_t,
        upper_width,
        upper_hidden,
        *gains,
    )
    do_oth = swap(do_send)
    pack_oth = swap(pack_send)
    dy, dz, part_send, exchange = attend_back(
        reps,
        adapter_ids,
        do_own,
        do_oth,
        o_own,
        o_send,
        normed,
        frozen_qkv,
        qkv_oth,
        lower_t,
        upper_width,
        upper_keys,
        query,
        natural_k,
        natural_v,
        flipped,
        zt,
        lse,
        cosine,
        sine,
        segment_ids,
        pack_own,
        pack_oth,
    )
    received = lax.all_to_all(exchange, "rep", 0, 0, tiled=True)
    input_grad = finish(
        adapter_ids,
        dy,
        dz,
        frozen_qkv,
        qkv_oth,
        lower_t,
        tok_own,
        *gains,
        swap(part_send),
        grad_middle,
    )
    received, input_grad = lax.optimization_barrier((received, input_grad))
    keep, send = collect(received)
    lower, down, width, keys, hidden = deliver(reps, keep, swap(send))
    return (
        layer_out[None],
        input_grad[None],
        lower.transpose(0, 1, 3, 2),
        down.transpose(0, 2, 1),
        width,
        keys,
        hidden,
    )


def solution(mesh):
    return jax.shard_map(
        per_device,
        mesh=mesh,
        in_specs=(
            P("rep", "grp", None),
            P("rep", "grp", None),
            P("rep", None),
            P("rep"),
            P(None, "grp"),
            P("grp", None),
            P("grp", None),
            P("grp", None),
            P("grp", None),
            P(),
            P(),
            P(),
            P(),
            P(),
        ),
        out_specs=(
            P("rep", "grp", None),
            P("rep", "grp", None),
            P(None, "grp", "rep", None),
            P("grp", "rep", None),
            P(None, "grp", None, "rep"),
            P(None, "grp", None, "rep"),
            P(None, "grp", None, "rep"),
        ),
        check_vma=False,
    )
```

```python
import functools

import jax
import jax.numpy as jnp
import numpy as np
from jax import lax
from jax.experimental import pallas as pl
from jax.experimental.pallas import tpu as pltpu
from jax.sharding import PartitionSpec as P

D = 1152
H = 18
KVH = 6
HD = 64
FF = 3072
R = 16
NAD = 8
KV = 384

HALF = D // 2
HEADS = H // 2
GROUP = H // KVH
QW = 640
KW = 256
SPAN = QW + 2 * KW
AUG = D + 128
TILE = 512
BLOCK = 256
DOCS = 4
KEYS = HEADS // GROUP
VMEM_BYTES = 61900 * 1024

epsilon = 1e-05
theta_base = 10000.0
masked_value = -1e30
f32 = jnp.float32
bf16 = jnp.bfloat16
SWAP = [(0, 1), (1, 0)]

HBM = pl.BlockSpec(memory_space=pltpu.MemorySpace.HBM)
ANY = pl.BlockSpec(memory_space=pl.ANY)
VMEM = pl.BlockSpec(memory_space=pltpu.VMEM)
SMEM = pl.BlockSpec(memory_space=pltpu.SMEM)


def nn(left, right):
    return jnp.dot(left, right, preferred_element_type=f32)


def nt(left, right):
    return lax.dot_general(left, right, (((1,), (1,)), ((), ())), preferred_element_type=f32)


def tn(left, right):
    return lax.dot_general(left, right, (((0,), (0,)), ((), ())), preferred_element_type=f32)


def lanes(shape):
    return lax.broadcasted_iota(jnp.int32, shape, len(shape) - 1)


def gain_row(g, own, other, row):
    mine = own[row : row + 1, :].astype(f32)
    theirs = other[row : row + 1, :].astype(f32)
    return jnp.where(
        g == 0,
        jnp.concatenate([mine, theirs], axis=1),
        jnp.concatenate([theirs, mine], axis=1),
    )


def copied(source, target, sem):
    return pltpu.make_async_copy(source, target, sem)


def doc_starts(segments):
    return [
        jnp.sum(jnp.where(segments < doc, 1.0, 0.0), axis=-1, keepdims=True)
        for doc in range(1, DOCS)
    ]


def start_at(place, starts):
    found = jnp.zeros_like(place)
    for start in starts:
        found = jnp.where(place >= start, start, found)
    return found


def fill_angles(starts, cosine, sine):
    def both(angle):
        return jnp.cos(angle), jnp.sin(angle)

    powers = np.float32(theta_base) ** (-np.arange(HD // 2, dtype=np.float32) * 2.0 / HD)
    row = lax.broadcasted_iota(jnp.int32, (HD // 2, 128), 0)
    freqs = jnp.zeros(row.shape, f32)
    for index, power in enumerate(powers):
        freqs = jnp.where(row == index, np.float32(power), freqs)

    fine_cos, fine_sin = both(lanes(freqs.shape).astype(f32) * freqs)
    docs = [both(start * freqs) for start in starts]
    for at in range(0, cosine.shape[1], 128):
        wide_cos, wide_sin = both(float(at) * freqs)
        cos_p = wide_cos * fine_cos - wide_sin * fine_sin
        sin_p = wide_sin * fine_cos + wide_cos * fine_sin
        place = (lanes(freqs.shape) + at).astype(f32)
        cos_d, sin_d = jnp.ones_like(cos_p), jnp.zeros_like(cos_p)
        for start, (cos_s, sin_s) in zip(starts, docs):
            inside = place >= start
            cos_d = jnp.where(inside, cos_s, cos_d)
            sin_d = jnp.where(inside, sin_s, sin_d)
        cosine[:, at : at + 128] = cos_p * cos_d + sin_p * sin_d
        sine[:, at : at + 128] = sin_p * cos_d - cos_p * sin_d


def turned(block, cosine, sine):
    first, second = block[: HD // 2], block[HD // 2 :]
    return jnp.concatenate(
        [first * cosine - second * sine, second * cosine + first * sine], axis=0
    )


def head_rows(slot):
    return pl.ds(pl.multiple_of(slot * HD, HD), HD)


def fill_mask(bias, starts, low, high):
    place = lanes((1, BLOCK)).astype(f32) + low
    begin = start_at(place, starts)
    for first in range(0, high, BLOCK):
        key_place = lax.broadcasted_iota(jnp.int32, (BLOCK, BLOCK), 0).astype(f32) + first
        allowed = key_place >= begin
        if first == low:
            allowed = allowed & (key_place <= place)
        bias[first : first + BLOCK, :] = jnp.where(allowed, 0.0, masked_value)


def qkv_loads(g, chosen, own, oth, upper_width, upper_keys, weight, sems):
    w_here = pl.ds(pl.multiple_of(g * HALF, 64), HALF)
    w_there = pl.ds(pl.multiple_of((1 - g) * HALF, 64), HALF)
    windows = (
        (pl.multiple_of(g * 512, 128), QW, 0),
        (pl.multiple_of(D + g * 128, 128), KW, QW),
        (pl.multiple_of(D + KV + g * 128, 128), KW, QW + KW),
    )
    loads = []
    for index, (at, width, to) in enumerate(windows):
        for part, (source, rows) in enumerate(((own, w_here), (oth, w_there))):
            loads.append(
                copied(
                    source.at[:, pl.ds(at, width)],
                    weight.at[rows, pl.ds(to, width)],
                    sems.at[2 * index + part],
                )
            )
    if upper_width is None:
        return loads
    loads.append(
        copied(
            upper_width.at[0, chosen, :, pl.ds(pl.multiple_of(g * 512, 128), QW)],
            weight.at[pl.ds(D, R), pl.ds(0, QW)],
            sems.at[6],
        )
    )
    for index in range(2):
        loads.append(
            copied(
                upper_keys.at[index, chosen, :, pl.ds(pl.multiple_of(g * 128, 128), KW)],
                weight.at[pl.ds(D + (index + 1) * R, R), pl.ds(QW + index * KW, KW)],
                sems.at[7 + index],
            )
        )
    return loads


def attend_kernel(
    adapter,
    tok_own,
    tok_oth,
    qkv_own,
    qkv_oth,
    lower_t,
    upper_width,
    upper_keys,
    gains_own,
    gains_oth,
    segments,
    o_own,
    o_send,
    q_out,
    k_out,
    v_out,
    o_out,
    n_out,
    zt_out,
    lse_out,
    cos_out,
    sin_out,
    tok,
    normed,
    weight,
    maps,
    query,
    key_t,
    value_t,
    key_rows,
    value_aug,
    mixed_t,
    mixed,
    scores,
    chances,
    bias,
    cosine,
    sine,
    inner_t,
    lse,
    sems,
    w_sems,
    out_sems,
):
    g = lax.axis_index("grp")
    chosen = adapter[0]
    rows = tok_own.shape[0]
    here = pl.ds(pl.multiple_of(g * rows, 128), rows)
    there = pl.ds(pl.multiple_of((1 - g) * rows, 128), rows)
    maps[...] = jnp.zeros_like(maps)
    weight[D:, :] = jnp.zeros((128, SPAN), bf16)
    loads = [
        copied(tok_own, tok.at[here], sems.at[0]),
        copied(tok_oth, tok.at[there], sems.at[1]),
    ] + [
        copied(lower_t.at[index, chosen], maps.at[pl.ds(index * R, R)], sems.at[2 + index])
        for index in range(3)
    ]
    w_loads = qkv_loads(g, chosen, qkv_own, qkv_oth, upper_width, upper_keys, weight, w_sems)
    for load in loads:
        load.start()
    starts = doc_starts(segments[...])
    fill_angles(starts, cosine, sine)
    gain = gain_row(g, gains_own, gains_oth, 0)
    for load in loads:
        load.wait()
    for load in w_loads:
        load.start()

    def norm_part(part, carry):
        span = pl.ds(pl.multiple_of(part * rows, 128), rows)
        wide = tok[span, :].astype(f32)
        scale = lax.rsqrt(jnp.mean(wide * wide, axis=-1, keepdims=True) + epsilon)
        normed[span, :D] = (wide * scale * gain).astype(bf16)
        inner = nt(normed[span, :D], maps[...])
        normed[span, D:] = inner.astype(bf16)
        inner_t[:, span] = inner.T[: 3 * R, :].astype(bf16)
        return carry

    lax.fori_loop(0, 2, norm_part, 0)
    for load in w_loads:
        load.wait()

    def project(part, carry):
        span = pl.ds(pl.multiple_of(part * rows, 128), rows)
        cos_cols = cosine[:, span]
        sin_cols = sine[:, span]
        for target, base, count, turn, scale in (
            (query, 0, QW, True, HD**-0.5),
            (key_t, QW, KW, True, 1.0),
            (value_t, QW + KW, KW, False, 1.0),
        ):
            for at in range(0, count, 256):
                width = min(256, count - at)
                made = nn(normed[span, :], weight[:, base + at : base + at + width]).T
                for to in range(0, width, HD):
                    block = made[to : to + HD]
                    if turn:
                        block = turned(block, cos_cols, sin_cols) * scale
                    target[at + to : at + to + HD, span] = block.astype(bf16)
        return carry

    lax.fori_loop(0, 2, project, 0)
    stores = [
        copied(query, q_out, out_sems.at[0]),
        copied(key_t, k_out, out_sems.at[1]),
        copied(value_t, v_out, out_sems.at[2]),
        copied(normed.at[:, pl.ds(0, D)], n_out, out_sems.at[3]),
        copied(cosine, cos_out, out_sems.at[4]),
        copied(sine, sin_out, out_sems.at[5]),
        copied(inner_t, zt_out, out_sems.at[6]),
    ]
    for store in stores:
        store.start()
    for j in range(KEYS):
        key_rows[j] = key_t[head_rows(j + g), :].T
        value_aug[j, :HD, :] = value_t[head_rows(j + g), :]
        value_aug[j, HD:, :] = jnp.ones((R, 2 * rows), bf16)
    mixed_t[:HD, :] = jnp.zeros((HD, 2 * rows), bf16)
    mixed_t[(HEADS + 1) * HD :, :] = jnp.zeros((HD, 2 * rows), bf16)

    for block in range(2 * rows // BLOCK):
        low, high = block * BLOCK, (block + 1) * BLOCK
        fill_mask(bias, starts, low, high)

        def score(h, side, low=low, high=high):
            top = None
            for first in range(0, high, BLOCK):
                span = slice(first, first + BLOCK)
                made = (
                    nn(key_rows[h // GROUP, span, :], query[head_rows(h + g), low:high])
                    + bias[span, :]
                )
                scores[side, span, :] = made
                best = jnp.max(made.reshape(BLOCK // 8, 8, BLOCK), axis=0)
                top = best if top is None else jnp.maximum(top, best)
            return jnp.max(top, axis=0, keepdims=True)

        def blend(h, side, top, low=low, high=high):
            for first in range(0, high, BLOCK):
                span = slice(first, first + BLOCK)
                chances[side, span, :] = jnp.exp(scores[side, span, :] - top).astype(bf16)
            made = nn(value_aug[h // GROUP, :, :high], chances[side, :high, :])
            total = made[HD : HD + 1]
            mixed_t[head_rows(h + 1), low:high] = (made[:HD] * (1.0 / total)).astype(bf16)
            lse[pl.ds(h, 1), low:high] = top + jnp.log(total)

        def group(j, top, score=score, blend=blend):
            for member in range(GROUP):
                h = j * GROUP + member
                later = score(jnp.minimum(h + 1, HEADS - 1), (member + 1) % GROUP)
                blend(h, member, top)
                top = later
            return top

        lax.fori_loop(0, KEYS, group, score(0, 0))
        for pair in range(QW // 128):
            side = pl.ds(pl.multiple_of((2 * pair + 1 - g) * HD, HD), 128)
            mixed[low:high, pair * 128 : pair * 128 + 128] = mixed_t[side, low:high].T
    stores += [
        copied(mixed.at[here], o_own, out_sems.at[7]),
        copied(mixed.at[there], o_send, out_sems.at[8]),
        copied(mixed_t, o_out, out_sems.at[9]),
        copied(lse, lse_out, out_sems.at[10]),
    ]
    for store in stores[-4:]:
        store.start()
    for store in stores:
        store.wait()


def attend(adapter, tok_own, *rest):
    rows = tok_own.shape[0]
    length = 2 * rows
    shape = jax.ShapeDtypeStruct
    return pl.pallas_call(
        attend_kernel,
        out_shape=[
            shape((rows, QW), bf16),
            shape((rows, QW), bf16),
            shape((QW, length), bf16),
            shape((KW, length), bf16),
            shape((KW, length), bf16),
            shape(((HEADS + 2) * HD, length), bf16),
            shape((length, D), bf16),
            shape((3 * R, length), bf16),
            shape((R, length), f32),
            shape((HD // 2, length), f32),
            shape((HD // 2, length), f32),
        ],
        in_specs=[SMEM, HBM, ANY, HBM, ANY] + [HBM] * 3 + [VMEM] * 3,
        out_specs=[HBM] * 11,
        scratch_shapes=[
            pltpu.VMEM((length, D), bf16),
            pltpu.VMEM((length, AUG), bf16),
            pltpu.VMEM((AUG, SPAN), bf16),
            pltpu.VMEM((128, D), bf16),
            pltpu.VMEM((QW, length), bf16),
            pltpu.VMEM((KW, length), bf16),
            pltpu.VMEM((KW, length), bf16),
            pltpu.VMEM((KEYS, length, HD), bf16),
            pltpu.VMEM((KEYS, HD + R, length), bf16),
            pltpu.VMEM(((HEADS + 2) * HD, length), bf16),
            pltpu.VMEM((length, QW), bf16),
            pltpu.VMEM((GROUP, length, BLOCK), f32),
            pltpu.VMEM((GROUP, length, BLOCK), bf16),
            pltpu.VMEM((length, BLOCK), f32),
            pltpu.VMEM((HD // 2, length), f32),
            pltpu.VMEM((HD // 2, length), f32),
            pltpu.VMEM((3 * R, length), bf16),
            pltpu.VMEM((R, length), f32),
            pltpu.SemaphoreType.DMA((5,)),
            pltpu.SemaphoreType.DMA((9,)),
            pltpu.SemaphoreType.DMA((11,)),
        ],
        compiler_params=pltpu.CompilerParams(vmem_limit_bytes=VMEM_BYTES),
        cost_estimate=pl.CostEstimate(
            flops=16 * 10**9, bytes_accessed=16 << 20, transcendentals=6 * 10**6
        ),
        name="attend",
    )(adapter, tok_own, *rest)


def normed_back(rows, gain_row, grad):
    scale = lax.rsqrt(jnp.mean(rows * rows, axis=-1, keepdims=True) + epsilon)
    scaled = grad * gain_row
    inside = jnp.mean(rows * scaled, axis=-1, keepdims=True)
    return scale * (scaled - rows * (scale * scale * inside))


def rounded_up(count, unit):
    return -(-count // unit) * unit


def feed_lanes(reps):
    return rounded_up((5 * D + 3 * FF) // reps, 256)


def qkv_lanes(reps):
    return rounded_up((4 * D + 2 * KV) // reps + 1, 128)


def packed(grads, reps, target):
    for rep in range(reps):
        at = 0
        for grad in grads:
            piece = grad.shape[-1] // reps
            share = grad[:, rep * piece : (rep + 1) * piece]
            target[rep * R : (rep + 1) * R, at : at + piece] = share.astype(target.dtype)
            at += piece


def feed_kernel(
    reps,
    adapter,
    o_own_in,
    o_oth_in,
    tok_in,
    cot_in,
    wo_own,
    wo_oth,
    wgu_own,
    wgu_oth,
    wd_own,
    wd_oth,
    a_down,
    lower_t,
    upper_width,
    upper_hidden,
    gains_own,
    gains_oth,
    layer_out,
    grad_middle,
    do_own_out,
    do_oth_out,
    pack_own_out,
    pack_send_out,
    o_own,
    o_oth,
    tok,
    cot,
    do_own,
    do_oth,
    wout,
    wg,
    wu,
    wd,
    at_out,
    at_gu,
    b_out,
    b_down,
    middle,
    normed,
    cot_aug,
    total,
    back,
    result,
    z_gu_t,
    dz_down_t,
    ga_out,
    gb_gate,
    gb_up,
    ga_down,
    pack,
    sems,
    o_sems,
    out_sems,
):
    g = lax.axis_index("grp")
    chosen = adapter[0]
    gain = gain_row(g, gains_own, gains_oth, 1)
    steps = FF // TILE
    each = steps // 2
    w_here = pl.ds(pl.multiple_of(g * HALF, 64), HALF)
    w_there = pl.ds(pl.multiple_of((1 - g) * HALF, 64), HALF)

    def column(step):
        owner = jnp.where(step < each, g, 1 - g)
        return owner * (FF // 2) + (step % each) * TILE

    def copies(step, slot):
        at = pl.multiple_of(column(step), TILE)
        gate_at = pl.ds(at, TILE)
        up_at = pl.ds(pl.multiple_of(FF + at, TILE), TILE)
        sem = lambda k: sems.at[slot, k]
        return [
            copied(wgu_own.at[:, gate_at], wg.at[slot, w_here], sem(0)),
            copied(wgu_oth.at[:, gate_at], wg.at[slot, w_there], sem(1)),
            copied(wgu_own.at[:, up_at], wu.at[slot, w_here], sem(2)),
            copied(wgu_oth.at[:, up_at], wu.at[slot, w_there], sem(3)),
            copied(upper_hidden.at[0, chosen, :, gate_at], wg.at[slot, pl.ds(D, R)], sem(4)),
            copied(upper_hidden.at[1, chosen, :, gate_at], wu.at[slot, pl.ds(D + R, R)], sem(5)),
            copied(a_down.at[gate_at], wd.at[slot, :, pl.ds(D, 128)], sem(6)),
        ]

    def down_copy(source, step, slot):
        local = pl.ds(pl.multiple_of((step % each) * TILE, TILE), TILE)
        return copied(source.at[local], wd.at[slot, :, pl.ds(0, D)], sems.at[slot, 7])

    def start(step, slot):
        for copy in copies(step, slot):
            copy.start()

        @pl.when(step < each)
        def _():
            down_copy(wd_own, step, slot).start()

        @pl.when(step >= each)
        def _():
            down_copy(wd_oth, step, slot).start()

    def wait(step, slot):
        for copy in copies(step, slot):
            copy.wait()
        down_copy(wd_own, step, slot).wait()

    for slot in range(2):
        wg[slot, D:, :] = jnp.zeros((128, TILE), bf16)
        wu[slot, D:, :] = jnp.zeros((128, TILE), bf16)
        at_out[slot] = jnp.zeros((128, QW), bf16)
        wout[slot, :HD, :D] = jnp.zeros((HD, D), bf16)
        wout[slot, HALF:, :D] = jnp.zeros((HD, D), bf16)
    for ref in (at_gu, b_out, b_down):
        ref[...] = jnp.zeros_like(ref)
    own_at = pl.multiple_of(g * 512, 128)
    oth_at = pl.multiple_of((1 - g) * 512, 128)
    loads = [
        copied(
            wo_own, wout.at[0, pl.ds(pl.multiple_of(g * HD, HD), HALF), pl.ds(0, D)], o_sems.at[0]
        ),
        copied(
            wo_oth,
            wout.at[1, pl.ds(pl.multiple_of((1 - g) * HD, HD), HALF), pl.ds(0, D)],
            o_sems.at[1],
        ),
        copied(lower_t.at[3, chosen, :, pl.ds(own_at, QW)], at_out.at[0, pl.ds(0, R)], o_sems.at[2]),
        copied(lower_t.at[3, chosen, :, pl.ds(oth_at, QW)], at_out.at[1, pl.ds(0, R)], o_sems.at[3]),
        copied(lower_t.at[4, chosen], at_gu.at[pl.ds(0, R)], o_sems.at[4]),
        copied(lower_t.at[5, chosen], at_gu.at[pl.ds(R, R)], o_sems.at[5]),
        copied(upper_width.at[1, chosen], b_out.at[pl.ds(0, R)], o_sems.at[6]),
        copied(upper_width.at[2, chosen], b_down.at[pl.ds(0, R)], o_sems.at[7]),
        copied(o_own_in, o_own, o_sems.at[8]),
        copied(o_oth_in, o_oth, o_sems.at[9]),
        copied(tok_in, tok, o_sems.at[10]),
        copied(cot_in, cot, o_sems.at[11]),
    ]
    first, second, third = loads[11:] + loads[2:4] + loads[7:8], loads[:2] + loads[8:10], loads[4:7] + loads[10:11]
    for load in first + second + third:
        load.start()
    total[...] = jnp.zeros_like(total)
    back[...] = jnp.zeros_like(back)
    for load in first:
        load.wait()
    cot_aug[:, :D] = cot[...]
    dz_down = nt(cot[...], b_down[...])
    cot_aug[:, D:] = dz_down.astype(bf16)
    dz_down_t[...] = dz_down.T[:R, :].astype(bf16)
    for slot in range(2):
        wout[slot, :, D:] = at_out[slot].T
    for load in second + third:
        load.wait()
    start(0, 0)
    made = nn(o_own[...], wout[0]) + nn(o_oth[...], wout[1])
    inner_out = made[:, D:].astype(bf16)
    middle[...] = tok[...].astype(f32) + made[:, :D] + nn(inner_out, b_out[...])
    scale = lax.rsqrt(jnp.mean(middle[...] * middle[...], axis=-1, keepdims=True) + epsilon)
    normed[:, :D] = (middle[...] * scale * gain).astype(bf16)
    inner_gu = nt(normed[:, :D], at_gu[...])
    normed[:, D:] = inner_gu.astype(bf16)
    z_gu_t[...] = inner_gu.T[: 2 * R, :].astype(bf16)

    def step_body(step, carry):
        slot = step % 2

        @pl.when(step + 1 < steps)
        def _():
            start(step + 1, 1 - slot)

        wait(step, slot)
        gate_at = pl.ds(pl.multiple_of(column(step), TILE), TILE)
        gate = nn(normed[...], wg[slot])
        up = nn(normed[...], wu[slot])
        grad_active = nt(cot_aug[...], wd[slot])
        sigmoid = 1.0 / (1.0 + jnp.exp(-gate))
        silu = gate * sigmoid
        active = (silu * up).astype(bf16)
        grad_gate = (grad_active * up * (sigmoid * (1.0 + gate * (1.0 - sigmoid)))).astype(bf16)
        grad_up = (grad_active * silu).astype(bf16)
        total[...] += nn(active, wd[slot])
        back[...] += nt(grad_gate, wg[slot]) + nt(grad_up, wu[slot])
        gb_gate[:, gate_at] = nn(z_gu_t[...], grad_gate)[:R]
        gb_up[:, gate_at] = nn(z_gu_t[...], grad_up)[R:]
        ga_down[:, gate_at] = nn(dz_down_t[...], active)
        return carry

    lax.fori_loop(0, steps, step_body, 0)

    inner_down = total[:, D:].astype(bf16)
    result[...] = (middle[...] + total[:, :D] + nn(inner_down, b_down[...])).astype(bf16)
    stores = [copied(result, layer_out, out_sems.at[0])]
    stores[0].start()
    gb_down = nn(total[:, D:].T[:R, :].astype(bf16), cot[...])
    dz_gu = back[:, D:].astype(bf16)
    grad_normed = back[:, :D] + nn(dz_gu, at_gu[...])
    grad = cot[...].astype(f32) + normed_back(middle[...], gain, grad_normed)
    total[:, :D] = grad
    stores.append(copied(total.at[:, pl.ds(0, D)], grad_middle, out_sems.at[1]))
    stores[1].start()
    branch = normed
    ga_gu = nn(back[:, D:].T[: 2 * R, :].astype(bf16), normed[:, :D])
    branch[:, :D] = grad.astype(bf16)
    dz_out = nt(branch[:, :D], b_out[...])
    branch[:, D:] = dz_out.astype(bf16)
    dz_out_t = dz_out.T[:R, :].astype(bf16)
    do_oth[...] = nt(wout[1], branch[...]).astype(bf16)
    stores.append(copied(do_oth, do_oth_out, out_sems.at[2]))
    stores[-1].start()
    do_own[...] = nt(wout[0], branch[...]).astype(bf16)
    stores.append(copied(do_own, do_own_out, out_sems.at[3]))
    stores[-1].start()
    gb_out = nn(inner_out.astype(f32).T[:R, :].astype(bf16), branch[:, :D])
    ga_out[...] = jnp.zeros_like(ga_out)
    ga_out[:, pl.ds(own_at, QW)] += nn(dz_out_t, o_own[...])
    ga_out[:, pl.ds(oth_at, QW)] += nn(dz_out_t, o_oth[...])
    pack[...] = jnp.zeros_like(pack)
    packed(
        [ga_out[...], ga_gu[:R], ga_gu[R:], gb_out, gb_down, ga_down[...], gb_gate[...], gb_up[...]],
        reps,
        pack,
    )
    half = pack.shape[1] // 2
    for index, (side, target) in enumerate(((g, pack_own_out), (1 - g, pack_send_out))):
        source = pack.at[:, pl.ds(pl.multiple_of(side * half, 128), half)]
        stores.append(copied(source, target, out_sems.at[4 + index]))
        stores[-1].start()
    for store in stores:
        store.wait()


def feed(reps, *args):
    rows = args[3].shape[0]
    half = feed_lanes(reps) // 2
    shape = jax.ShapeDtypeStruct
    return pl.pallas_call(
        functools.partial(feed_kernel, reps),
        out_shape=[
            shape((rows, D), bf16),
            shape((rows, D), f32),
            shape((QW, rows), bf16),
            shape((QW, rows), bf16),
            shape((reps * R, half), bf16),
            shape((reps * R, half), bf16),
        ],
        in_specs=[SMEM, HBM, ANY] + [HBM] * 12 + [VMEM] * 2,
        out_specs=[HBM] * 6,
        scratch_shapes=[
            pltpu.VMEM((rows, QW), bf16),
            pltpu.VMEM((rows, QW), bf16),
            pltpu.VMEM((rows, D), bf16),
            pltpu.VMEM((rows, D), bf16),
            pltpu.VMEM((QW, rows), bf16),
            pltpu.VMEM((QW, rows), bf16),
            pltpu.VMEM((2, QW, AUG), bf16),
            pltpu.VMEM((2, AUG, TILE), bf16),
            pltpu.VMEM((2, AUG, TILE), bf16),
            pltpu.VMEM((2, TILE, AUG), bf16),
            pltpu.VMEM((2, 128, QW), bf16),
            pltpu.VMEM((128, D), bf16),
            pltpu.VMEM((128, D), bf16),
            pltpu.VMEM((128, D), bf16),
            pltpu.VMEM((rows, D), f32),
            pltpu.VMEM((rows, AUG), bf16),
            pltpu.VMEM((rows, AUG), bf16),
            pltpu.VMEM((rows, AUG), f32),
            pltpu.VMEM((rows, AUG), f32),
            pltpu.VMEM((rows, D), bf16),
            pltpu.VMEM((2 * R, rows), bf16),
            pltpu.VMEM((R, rows), bf16),
            pltpu.VMEM((R, D), f32),
            pltpu.VMEM((R, FF), f32),
            pltpu.VMEM((R, FF), f32),
            pltpu.VMEM((R, FF), f32),
            pltpu.VMEM((reps * R, 2 * half), bf16),
            pltpu.SemaphoreType.DMA((2, 8)),
            pltpu.SemaphoreType.DMA((12,)),
            pltpu.SemaphoreType.DMA((6,)),
        ],
        compiler_params=pltpu.CompilerParams(vmem_limit_bytes=56 << 20),
        cost_estimate=pl.CostEstimate(
            flops=30 * 10**9, bytes_accessed=36 << 20, transcendentals=2 * 10**6
        ),
        name="feed",
    )(*args)


def attend_back_kernel(
    reps,
    adapter,
    do_own,
    do_oth,
    o_in,
    normed,
    qkv_own,
    qkv_oth,
    lower_t,
    upper_width,
    upper_keys,
    query_in,
    k_in,
    v_in,
    zt_in,
    lse_in,
    cos_in,
    sin_in,
    segments,
    pack_own_in,
    pack_oth_in,
    dy_out,
    dz_out,
    part_out,
    exchange_out,
    query,
    key_t,
    value_t,
    zt,
    lse,
    cosine,
    sine,
    pack_own,
    pack_oth,
    inner_low,
    exchange,
    outgoing,
    maps,
    grad_o,
    mixed_t,
    n_rows,
    weight,
    key_rows,
    value_rows,
    delta,
    dq,
    dk,
    dv,
    dy_t,
    dy,
    chances,
    grad_scores,
    bias,
    gb_q,
    gb_kv,
    pack,
    sems,
    b_sems,
    out_sem,
):
    g = lax.axis_index("grp")
    chosen = adapter[0]
    length = query.shape[1]
    rows = length // 2
    here = pl.ds(pl.multiple_of(g * rows, 128), rows)
    there = pl.ds(pl.multiple_of((1 - g) * rows, 128), rows)
    weight[D:, :] = jnp.zeros((128, SPAN), bf16)
    maps[...] = jnp.zeros_like(maps)
    early = [
        copied(k_in, key_t, sems.at[0]),
        copied(v_in, value_t, sems.at[1]),
    ]
    loads = [
        copied(do_own, grad_o.at[:, here], sems.at[2]),
        copied(do_oth, grad_o.at[:, there], sems.at[3]),
        copied(o_in, mixed_t, sems.at[4]),
        copied(query_in, query, sems.at[5]),
        copied(lse_in, lse, sems.at[6]),
    ]
    late = [
        copied(cos_in, cosine, sems.at[7]),
        copied(sin_in, sine, sems.at[8]),
        copied(normed, n_rows, sems.at[9]),
        copied(zt_in, zt, sems.at[10]),
        copied(pack_own_in, pack_own, sems.at[11]),
        copied(pack_oth_in, pack_oth, sems.at[12]),
    ] + [
        copied(lower_t.at[index, chosen], maps.at[pl.ds(index * R, R)], sems.at[13 + index])
        for index in range(3)
    ] + qkv_loads(g, chosen, qkv_own, qkv_oth, upper_width, upper_keys, weight, b_sems)
    for load in early + loads:
        load.start()
    dk[...] = jnp.zeros_like(dk)
    dv[...] = jnp.zeros_like(dv)
    dy_t[...] = jnp.zeros_like(dy_t)
    starts = doc_starts(segments[...])
    for load in early:
        load.wait()
    for j in range(KEYS):
        key_rows[j] = key_t[head_rows(j + g), :].T
        value_rows[j] = value_t[head_rows(j + g), :].T
    for load in loads:
        load.wait()
    for load in late:
        load.start()
    for h in range(HEADS):
        product = grad_o[head_rows(h + g), :].astype(f32) * mixed_t[
            (h + 1) * HD : (h + 2) * HD, :
        ].astype(f32)
        delta[h : h + 1, :] = jnp.sum(product, axis=0, keepdims=True)

    for block in range(length // BLOCK):
        low, high = block * BLOCK, (block + 1) * BLOCK
        fill_mask(bias, starts, low, high)

        def score(h, side, low=low, high=high):
            logs = lse[pl.ds(h, 1), low:high]
            deltas = delta[pl.ds(h, 1), low:high]
            for first in range(0, high, BLOCK):
                span = slice(first, first + BLOCK)
                made = nn(key_rows[h // GROUP, span, :], query[head_rows(h + g), low:high])
                grad = nn(value_rows[h // GROUP, span, :], grad_o[head_rows(h + g), low:high])
                chance = jnp.exp(made + bias[span, :] - logs)
                chances[side, span, :] = chance.astype(bf16)
                grad_scores[side, span, :] = (chance * (grad - deltas)).astype(bf16)

        def spread(h, side, low=low, high=high):
            dq[h, :, low:high] = nn(
                key_t[head_rows(h // GROUP + g), :high], grad_scores[side, :high, :]
            )
            return (
                nt(grad_o[head_rows(h + g), low:high], chances[side, :high, :]),
                nt(query[head_rows(h + g), low:high], grad_scores[side, :high, :]),
            )

        def group(j, carry, high=high, score=score, spread=spread):
            found = []
            for member in range(GROUP):
                h = j * GROUP + member
                score(jnp.minimum(h + 1, HEADS - 1), (member + 1) % GROUP)
                found.append(spread(h, member))
            dv[j, :, :high] += found[0][0] + found[1][0] + found[2][0]
            dk[j, :, :high] += found[0][1] + found[1][1] + found[2][1]
            return carry

        score(0, 0)
        lax.fori_loop(0, KEYS, group, 0)

    for load in late:
        load.wait()
    back_sine = -sine[...]
    for h in range(HEADS):
        dy_t[(h + 1) * HD : (h + 2) * HD, :] = (
            turned(dq[h], cosine[...], back_sine) * HD**-0.5
        ).astype(bf16)
    key_base = (HEADS + 2) * HD
    value_base = key_base + (KEYS + 2) * HD
    for j in range(KEYS):
        at = key_base + (j + 1) * HD
        dy_t[at : at + HD, :] = turned(dk[j], cosine[...], back_sine).astype(bf16)
        at = value_base + (j + 1) * HD
        dy_t[at : at + HD, :] = dv[j].astype(bf16)
    for base, count, to in ((0, QW, 0), (key_base, KW, QW), (value_base, KW, QW + KW)):
        for at in range(0, count, 128):
            side = pl.ds(pl.multiple_of(base + at + (1 - g) * HD, HD), 128)
            dy[:, to + at : to + at + 128] = dy_t[side, :].T
    store = copied(dy.at[here], dy_out, out_sem.at[0])
    store.start()
    made = nt(dy[there, :], weight[...])
    theirs = made[:, D:]
    outgoing[...] = (made[:, :D] + nn(theirs.astype(bf16), maps[...])).astype(bf16)
    part_store = copied(outgoing, part_out, out_sem.at[3])
    part_store.start()
    mine = nt(dy[here, :], weight[D:, :])
    inner_low[...] = mine.astype(bf16)
    inner_store = copied(inner_low, dz_out, out_sem.at[1])
    inner_store.start()
    gb = nn(zt[...], dy[...])
    gb_q[...] = jnp.zeros_like(gb_q)
    gb_kv[...] = jnp.zeros_like(gb_kv)
    gb_q[:, pl.ds(pl.multiple_of(g * 512, 128), QW)] = gb[:R, :QW]
    for index in range(2):
        gb_kv[index, :, pl.ds(pl.multiple_of(g * 128, 128), KW)] = gb[
            (index + 1) * R : (index + 2) * R, QW + index * KW : QW + (index + 1) * KW
        ]
    ga = nn(theirs.T[: 3 * R, :].astype(bf16), n_rows[there, :]) + nn(
        mine.T[: 3 * R, :].astype(bf16), n_rows[here, :]
    )
    pack[...] = jnp.zeros_like(pack)
    packed(
        [ga[:R], ga[R : 2 * R], ga[2 * R :], gb_q[...], gb_kv[0], gb_kv[1]],
        reps,
        pack,
    )
    half = pack_own.shape[1]
    width = pack.shape[1]
    exchange[:, :half] = (pack_own[...].astype(f32) + pack_oth[...].astype(f32)).astype(bf16)
    exchange[:, half:] = jnp.where(
        lanes(pack.shape) == width - 1, chosen.astype(f32), pack[...].astype(f32)
    ).astype(bf16)
    last = copied(exchange, exchange_out, out_sem.at[2])
    last.start()
    for copy in (store, inner_store, part_store, last):
        copy.wait()


def attend_back(reps, *args):
    rows = args[1].shape[1]
    length = 2 * rows
    half = feed_lanes(reps) // 2
    width = qkv_lanes(reps)
    shape = jax.ShapeDtypeStruct
    return pl.pallas_call(
        functools.partial(attend_back_kernel, reps),
        out_shape=[
            shape((rows, SPAN), bf16),
            shape((rows, 128), bf16),
            shape((rows, D), bf16),
            shape((reps * R, half + width), bf16),
        ],
        in_specs=[SMEM, HBM, ANY] + [HBM] * 14 + [VMEM, HBM, ANY],
        out_specs=[HBM] * 4,
        scratch_shapes=[
            pltpu.VMEM((QW, length), bf16),
            pltpu.VMEM((KW, length), bf16),
            pltpu.VMEM((KW, length), bf16),
            pltpu.VMEM((3 * R, length), bf16),
            pltpu.VMEM((R, length), f32),
            pltpu.VMEM((HD // 2, length), f32),
            pltpu.VMEM((HD // 2, length), f32),
            pltpu.VMEM((reps * R, half), bf16),
            pltpu.VMEM((reps * R, half), bf16),
            pltpu.VMEM((rows, 128), bf16),
            pltpu.VMEM((reps * R, half + width), bf16),
            pltpu.VMEM((rows, D), bf16),
            pltpu.VMEM((128, D), bf16),
            pltpu.VMEM((QW, length), bf16),
            pltpu.VMEM(((HEADS + 2) * HD, length), bf16),
            pltpu.VMEM((length, D), bf16),
            pltpu.VMEM((AUG, SPAN), bf16),
            pltpu.VMEM((KEYS, length, HD), bf16),
            pltpu.VMEM((KEYS, length, HD), bf16),
            pltpu.VMEM((R, length), f32),
            pltpu.VMEM((HEADS, HD, length), f32),
            pltpu.VMEM((KEYS, HD, length), f32),
            pltpu.VMEM((KEYS, HD, length), f32),
            pltpu.VMEM(((HEADS + 2 * KEYS + 6) * HD, length), bf16),
            pltpu.VMEM((length, SPAN), bf16),
            pltpu.VMEM((GROUP, length, BLOCK), bf16),
            pltpu.VMEM((GROUP, length, BLOCK), bf16),
            pltpu.VMEM((length, BLOCK), f32),
            pltpu.VMEM((R, D), f32),
            pltpu.VMEM((2, R, KV), f32),
            pltpu.VMEM((reps * R, width), bf16),
            pltpu.SemaphoreType.DMA((16,)),
            pltpu.SemaphoreType.DMA((9,)),
            pltpu.SemaphoreType.DMA((4,)),
        ],
        compiler_params=pltpu.CompilerParams(vmem_limit_bytes=56 << 20),
        cost_estimate=pl.CostEstimate(
            flops=24 * 10**9, bytes_accessed=20 << 20, transcendentals=6 * 10**6
        ),
        name="attend_back",
    )(*args)


def finish_kernel(
    adapter,
    dy_in,
    dz_in,
    qkv_own,
    qkv_oth,
    lower_t,
    tok_in,
    gains_own,
    gains_oth,
    part_in,
    middle_in,
    out,
    dy,
    dz,
    tok,
    part,
    grad_middle,
    weight,
    maps,
    result,
    sems,
    w_sems,
    out_sem,
):
    g = lax.axis_index("grp")
    chosen = adapter[0]
    maps[...] = jnp.zeros_like(maps)
    loads = qkv_loads(g, chosen, qkv_own, qkv_oth, None, None, weight, w_sems)
    for index, (source, target) in enumerate(
        ((dy_in, dy), (dz_in, dz), (tok_in, tok), (middle_in, grad_middle), (part_in, part))
    ):
        loads.append(copied(source, target, sems.at[index]))
    for index in range(3):
        loads.append(
            copied(lower_t.at[index, chosen], maps.at[pl.ds(index * R, R)], sems.at[5 + index])
        )
    for load in loads:
        load.start()
    gain = gain_row(g, gains_own, gains_oth, 0)
    for load in loads:
        load.wait()

    def half(index, carry):
        count = tok.shape[0] // 2
        span = pl.ds(pl.multiple_of(index * count, 128), count)
        grad = nt(dy[span, :], weight[...]) + nn(dz[span, :], maps[...]) + part[span, :].astype(f32)
        result[span, :] = (
            grad_middle[span, :] + normed_back(tok[span, :].astype(f32), gain, grad)
        ).astype(bf16)
        return carry

    lax.fori_loop(0, 2, half, 0)
    store = copied(result, out, out_sem.at[0])
    store.start()
    store.wait()


def finish(*args):
    rows = args[1].shape[0]
    return pl.pallas_call(
        finish_kernel,
        out_shape=jax.ShapeDtypeStruct((rows, D), bf16),
        in_specs=[SMEM] + [HBM] * 6 + [VMEM] * 2 + [ANY, HBM],
        out_specs=HBM,
        scratch_shapes=[
            pltpu.VMEM((rows, SPAN), bf16),
            pltpu.VMEM((rows, 128), bf16),
            pltpu.VMEM((rows, D), bf16),
            pltpu.VMEM((rows, D), bf16),
            pltpu.VMEM((rows, D), f32),
            pltpu.VMEM((D, SPAN), bf16),
            pltpu.VMEM((128, D), bf16),
            pltpu.VMEM((rows, D), bf16),
            pltpu.SemaphoreType.DMA((8,)),
            pltpu.SemaphoreType.DMA((6,)),
            pltpu.SemaphoreType.DMA((1,)),
        ],
        compiler_params=pltpu.CompilerParams(vmem_limit_bytes=VMEM_BYTES),
        cost_estimate=pl.CostEstimate(
            flops=4 * 10**9, bytes_accessed=10 << 20, transcendentals=0
        ),
        name="finish",
    )(*args)


def collect_kernel(source, keep, send, received, sem):
    load = copied(source, received, sem.at[0])
    load.start()
    load.wait()
    g = lax.axis_index("grp")
    count, width = received.shape
    quota = NAD // 2
    label = received[:, width - 1 :].astype(f32)
    lane = lanes((count, NAD * R))
    row = lax.broadcasted_iota(jnp.int32, (count, NAD * R), 0)
    picks = ((lane // R).astype(f32) == label) & (lane % R == row % R)
    sums = tn(picks.astype(f32).astype(bf16), received[...])
    first = g == 0
    for adapter in range(quota):
        low = sums[adapter * R : (adapter + 1) * R]
        high = sums[(quota + adapter) * R : (quota + adapter + 1) * R]
        keep[adapter] = jnp.where(first, low, high)
        send[adapter] = jnp.where(first, high, low)


def collect(received):
    shape = jax.ShapeDtypeStruct((NAD // 2, R, received.shape[1]), f32)
    return pl.pallas_call(
        collect_kernel,
        out_shape=[shape, shape],
        in_specs=[ANY],
        out_specs=[VMEM] * 2,
        scratch_shapes=[
            pltpu.VMEM(received.shape, bf16),
            pltpu.SemaphoreType.DMA((1,)),
        ],
        compiler_params=pltpu.CompilerParams(vmem_limit_bytes=8 << 20),
        cost_estimate=pl.CostEstimate(flops=10**8, bytes_accessed=2 << 20, transcendentals=0),
        name="collect",
    )(received)


def deliver_kernel(reps, keep, other, lower, down, width, keys, hidden, feeds, qkvs):
    g = lax.axis_index("grp")
    half = feeds.shape[-1] // 2
    feeds[:, :, pl.ds(pl.multiple_of(g * half, 128), half)] = keep[:, :, :half]
    feeds[:, :, pl.ds(pl.multiple_of((1 - g) * half, 128), half)] = other[:, :, :half]
    qkvs[...] = keep[:, :, half:] + other[:, :, half:]
    piece, tall, short = D // reps, FF // reps, KV // reps
    for index in range(3):
        lower[index] = qkvs[:, :, index * piece : (index + 1) * piece]
        lower[3 + index] = feeds[:, :, index * piece : (index + 1) * piece]
    width[0] = qkvs[:, :, 3 * piece : 4 * piece]
    width[1] = feeds[:, :, 3 * piece : 4 * piece]
    width[2] = feeds[:, :, 4 * piece : 5 * piece]
    for index in range(2):
        at = 4 * piece + index * short
        keys[index] = qkvs[:, :, at : at + short]
        at = 5 * piece + (1 + index) * tall
        hidden[index] = feeds[:, :, at : at + tall]
    down[...] = feeds[:, :, 5 * piece : 5 * piece + tall]


def deliver(reps, keep, other):
    quota = NAD // 2
    shape = lambda *dims: jax.ShapeDtypeStruct(dims, f32)
    return pl.pallas_call(
        functools.partial(deliver_kernel, reps),
        out_shape=[
            shape(6, quota, R, D // reps),
            shape(quota, R, FF // reps),
            shape(3, quota, R, D // reps),
            shape(2, quota, R, KV // reps),
            shape(2, quota, R, FF // reps),
        ],
        in_specs=[VMEM] * 2,
        out_specs=[VMEM] * 5,
        scratch_shapes=[
            pltpu.VMEM((quota, R, feed_lanes(reps)), f32),
            pltpu.VMEM((quota, R, qkv_lanes(reps)), f32),
        ],
        compiler_params=pltpu.CompilerParams(vmem_limit_bytes=8 << 20),
        cost_estimate=pl.CostEstimate(flops=10**6, bytes_accessed=1 << 20, transcendentals=0),
        name="deliver",
    )(keep, other)


def per_device(
    tokens,
    cotangent,
    segment_ids,
    adapter_ids,
    norm_gains,
    frozen_qkv,
    frozen_out,
    frozen_gate_up,
    frozen_down,
    lower_mats,
    lower_down,
    upper_width,
    upper_keys,
    upper_hidden,
):
    reps = lax.axis_size("rep")
    chosen = adapter_ids[0]
    first = lax.axis_index("grp") == 0
    swap = lambda value: lax.ppermute(value, "grp", SWAP)

    tok_own = tokens[0]
    tok_oth = swap(tok_own)
    qkv_oth = swap(frozen_qkv)
    gains_oth = swap(norm_gains)
    a_down = jnp.pad(
        lax.dynamic_index_in_dim(lower_down, chosen, 0, keepdims=False), ((0, 0), (0, 128 - R))
    )
    tok_oth, qkv_oth, gains_oth, a_down, wo, wgu, wd = lax.optimization_barrier(
        (tok_oth, qkv_oth, gains_oth, a_down, frozen_out, frozen_gate_up, frozen_down)
    )
    wo_oth = swap(wo)
    wgu_oth = swap(wgu)
    wd_oth = swap(wd)

    lower_t = lower_mats.transpose(0, 1, 3, 2)
    gains = (norm_gains, gains_oth)

    (o_own, o_send, query, key_t, value_t, mixed_t, normed, zt, lse, cosine, sine) = attend(
        adapter_ids,
        tok_own,
        tok_oth,
        frozen_qkv,
        qkv_oth,
        lower_t,
        upper_width,
        upper_keys,
        *gains,
        segment_ids,
    )
    o_oth = swap(o_send)
    layer_out, grad_middle, do_own, do_send, pack_own, pack_send = feed(
        reps,
        adapter_ids,
        o_own,
        o_oth,
        tok_own,
        cotangent[0],
        frozen_out,
        wo_oth,
        frozen_gate_up,
        wgu_oth,
        frozen_down,
        wd_oth,
        a_down,
        lower_t,
        upper_width,
        upper_hidden,
        *gains,
    )
    do_oth = swap(do_send)
    pack_oth = swap(pack_send)
    dy, dz, part_send, exchange = attend_back(
        reps,
        adapter_ids,
        do_own,
        do_oth,
        mixed_t,
        normed,
        frozen_qkv,
        qkv_oth,
        lower_t,
        upper_width,
        upper_keys,
        query,
        key_t,
        value_t,
        zt,
        lse,
        cosine,
        sine,
        segment_ids,
        pack_own,
        pack_oth,
    )
    received = lax.all_to_all(exchange, "rep", 0, 0, tiled=True)
    input_grad = finish(
        adapter_ids,
        dy,
        dz,
        frozen_qkv,
        qkv_oth,
        lower_t,
        tok_own,
        *gains,
        swap(part_send),
        grad_middle,
    )
    received, input_grad = lax.optimization_barrier((received, input_grad))
    keep, send = collect(received)
    lower, down, width, keys, hidden = deliver(reps, keep, swap(send))
    return (
        layer_out[None],
        input_grad[None],
        lower.transpose(0, 1, 3, 2),
        down.transpose(0, 2, 1),
        width,
        keys,
        hidden,
    )


def solution(mesh):
    return jax.shard_map(
        per_device,
        mesh=mesh,
        in_specs=(
            P("rep", "grp", None),
            P("rep", "grp", None),
            P("rep", None),
            P("rep"),
            P(None, "grp"),
            P("grp", None),
            P("grp", None),
            P("grp", None),
            P("grp", None),
            P(),
            P(),
            P(),
            P(),
            P(),
        ),
        out_specs=(
            P("rep", "grp", None),
            P("rep", "grp", None),
            P(None, "grp", "rep", None),
            P("grp", "rep", None),
            P(None, "grp", None, "rep"),
            P(None, "grp", None, "rep"),
            P(None, "grp", None, "rep"),
        ),
        check_vma=False,
    )
```

```python
import functools

import jax
import jax.numpy as jnp
import numpy as np
from jax import lax
from jax.experimental import pallas as pl
from jax.experimental.pallas import tpu as pltpu
from jax.sharding import PartitionSpec as P

D = 1152
H = 18
KVH = 6
HD = 64
FF = 3072
R = 16
NAD = 8
KV = 384

HALF = D // 2
HEADS = H // 2
GROUP = H // KVH
QW = 640
KW = 256
SPAN = QW + 2 * KW
AUG = D + 128
TILE = 768
BLOCK = 256
BLOCKS = 1024 // BLOCK
DOCS = 4
KEYS = HEADS // GROUP
VMEM_BYTES = 61900 * 1024

epsilon = 1e-05
theta_base = 10000.0
masked_value = -1e30
f32 = jnp.float32
bf16 = jnp.bfloat16
SWAP = [(0, 1), (1, 0)]

HBM = pl.BlockSpec(memory_space=pltpu.MemorySpace.HBM)
ANY = pl.BlockSpec(memory_space=pl.ANY)
VMEM = pl.BlockSpec(memory_space=pltpu.VMEM)
SMEM = pl.BlockSpec(memory_space=pltpu.SMEM)


def nn(left, right):
    return jnp.dot(left, right, preferred_element_type=f32)


def nt(left, right):
    return lax.dot_general(left, right, (((1,), (1,)), ((), ())), preferred_element_type=f32)


def tn(left, right):
    return lax.dot_general(left, right, (((0,), (0,)), ((), ())), preferred_element_type=f32)


def lanes(shape):
    return lax.broadcasted_iota(jnp.int32, shape, len(shape) - 1)


def gain_row(g, own, other, row):
    mine = own[row : row + 1, :].astype(f32)
    theirs = other[row : row + 1, :].astype(f32)
    return jnp.where(
        g == 0,
        jnp.concatenate([mine, theirs], axis=1),
        jnp.concatenate([theirs, mine], axis=1),
    )


def copied(source, target, sem):
    return pltpu.make_async_copy(source, target, sem)


def doc_starts(segments):
    return [
        jnp.sum(jnp.where(segments < doc, 1.0, 0.0), axis=-1, keepdims=True)
        for doc in range(1, DOCS)
    ]


def start_at(place, starts):
    found = jnp.zeros_like(place)
    for start in starts:
        found = jnp.where(place >= start, start, found)
    return found


def fill_angles(starts, cosine, sine):
    def both(angle):
        return jnp.cos(angle), jnp.sin(angle)

    powers = np.float32(theta_base) ** (-np.arange(HD // 2, dtype=np.float32) * 2.0 / HD)
    row = lax.broadcasted_iota(jnp.int32, (HD // 2, 128), 0)
    freqs = jnp.zeros(row.shape, f32)
    for index, power in enumerate(powers):
        freqs = jnp.where(row == index, np.float32(power), freqs)

    fine_cos, fine_sin = both(lanes(freqs.shape).astype(f32) * freqs)
    docs = [both(start * freqs) for start in starts]
    for at in range(0, cosine.shape[1], 128):
        wide_cos, wide_sin = both(float(at) * freqs)
        cos_p = wide_cos * fine_cos - wide_sin * fine_sin
        sin_p = wide_sin * fine_cos + wide_cos * fine_sin
        place = (lanes(freqs.shape) + at).astype(f32)
        cos_d, sin_d = jnp.ones_like(cos_p), jnp.zeros_like(cos_p)
        for start, (cos_s, sin_s) in zip(starts, docs):
            inside = place >= start
            cos_d = jnp.where(inside, cos_s, cos_d)
            sin_d = jnp.where(inside, sin_s, sin_d)
        cosine[:, at : at + 128] = cos_p * cos_d + sin_p * sin_d
        sine[:, at : at + 128] = sin_p * cos_d - cos_p * sin_d


def turned(block, cosine, sine):
    first, second = block[: HD // 2], block[HD // 2 :]
    return jnp.concatenate(
        [first * cosine - second * sine, second * cosine + first * sine], axis=0
    )


def head_rows(slot):
    return pl.ds(pl.multiple_of(slot * HD, HD), HD)


def fill_mask(bias, starts, low, high):
    place = lanes((1, BLOCK)).astype(f32) + low
    begin = start_at(place, starts)
    for first in range(0, high, BLOCK):
        key_place = lax.broadcasted_iota(jnp.int32, (BLOCK, BLOCK), 0).astype(f32) + first
        allowed = key_place >= begin
        if first == low:
            allowed = allowed & (key_place <= place)
        bias[first : first + BLOCK, :] = jnp.where(allowed, 0.0, masked_value)


def qkv_loads(g, chosen, own, oth, upper_width, upper_keys, weight, sems):
    w_here = pl.ds(pl.multiple_of(g * HALF, 64), HALF)
    w_there = pl.ds(pl.multiple_of((1 - g) * HALF, 64), HALF)
    windows = (
        (pl.multiple_of(g * 512, 128), QW, 0),
        (pl.multiple_of(D + g * 128, 128), KW, QW),
        (pl.multiple_of(D + KV + g * 128, 128), KW, QW + KW),
    )
    loads = []
    for index, (at, width, to) in enumerate(windows):
        for part, (source, rows) in enumerate(((own, w_here), (oth, w_there))):
            loads.append(
                copied(
                    source.at[:, pl.ds(at, width)],
                    weight.at[rows, pl.ds(to, width)],
                    sems.at[2 * index + part],
                )
            )
    if upper_width is None:
        return loads
    loads.append(
        copied(
            upper_width.at[0, chosen, :, pl.ds(pl.multiple_of(g * 512, 128), QW)],
            weight.at[pl.ds(D, R), pl.ds(0, QW)],
            sems.at[6],
        )
    )
    for index in range(2):
        loads.append(
            copied(
                upper_keys.at[index, chosen, :, pl.ds(pl.multiple_of(g * 128, 128), KW)],
                weight.at[pl.ds(D + (index + 1) * R, R), pl.ds(QW + index * KW, KW)],
                sems.at[7 + index],
            )
        )
    return loads


def attend_kernel(
    adapter,
    tok_own,
    tok_oth,
    qkv_own,
    qkv_oth,
    lower_t,
    upper_width,
    upper_keys,
    gains_own,
    gains_oth,
    segments,
    o_own,
    o_send,
    q_out,
    k_out,
    v_out,
    o_out,
    n_out,
    zt_out,
    scale_out,
    cos_out,
    sin_out,
    *refs,
):
    attend_body(
        adapter,
        tok_own,
        tok_oth,
        qkv_own,
        qkv_oth,
        lower_t,
        upper_width,
        upper_keys,
        gains_own,
        gains_oth,
        segments,
        o_own,
        o_send,
        q_out,
        k_out,
        v_out,
        o_out,
        n_out,
        zt_out,
        scale_out,
        cos_out,
        sin_out,
        refs[:BLOCKS],
        refs[BLOCKS : 2 * BLOCKS],
        *refs[2 * BLOCKS :],
    )


def attend_body(
    adapter,
    tok_own,
    tok_oth,
    qkv_own,
    qkv_oth,
    lower_t,
    upper_width,
    upper_keys,
    gains_own,
    gains_oth,
    segments,
    o_own,
    o_send,
    q_out,
    k_out,
    v_out,
    o_out,
    n_out,
    zt_out,
    scale_out,
    cos_out,
    sin_out,
    chances_out,
    chances,
    tok,
    normed,
    weight,
    maps,
    query,
    key_t,
    value_t,
    key_rows,
    value_aug,
    mixed_t,
    mixed,
    scores,
    bias,
    cosine,
    sine,
    inner_t,
    scales,
    sems,
    w_sems,
    out_sems,
    keep_sem,
):
    g = lax.axis_index("grp")
    chosen = adapter[0]
    rows = tok_own.shape[0]
    here = pl.ds(pl.multiple_of(g * rows, 128), rows)
    there = pl.ds(pl.multiple_of((1 - g) * rows, 128), rows)
    maps[...] = jnp.zeros_like(maps)
    weight[D:, :] = jnp.zeros((128, SPAN), bf16)
    loads = [
        copied(tok_own, tok.at[here], sems.at[0]),
        copied(tok_oth, tok.at[there], sems.at[1]),
    ] + [
        copied(lower_t.at[index, chosen], maps.at[pl.ds(index * R, R)], sems.at[2 + index])
        for index in range(3)
    ]
    w_loads = qkv_loads(g, chosen, qkv_own, qkv_oth, upper_width, upper_keys, weight, w_sems)
    for load in loads:
        load.start()
    starts = doc_starts(segments[...])
    fill_angles(starts, cosine, sine)
    gain = gain_row(g, gains_own, gains_oth, 0)
    for load in loads:
        load.wait()
    for load in w_loads:
        load.start()

    def norm_part(part, carry):
        span = pl.ds(pl.multiple_of(part * rows, 128), rows)
        wide = tok[span, :].astype(f32)
        scale = lax.rsqrt(jnp.mean(wide * wide, axis=-1, keepdims=True) + epsilon)
        normed[span, :D] = (wide * scale * gain).astype(bf16)
        inner = nt(normed[span, :D], maps[...])
        normed[span, D:] = inner.astype(bf16)
        inner_t[:, span] = inner.T[: 3 * R, :].astype(bf16)
        return carry

    lax.fori_loop(0, 2, norm_part, 0)
    for load in w_loads:
        load.wait()

    def project(part, carry):
        span = pl.ds(pl.multiple_of(part * rows, 128), rows)
        cos_cols = cosine[:, span]
        sin_cols = sine[:, span]
        for target, base, count, turn, scale in (
            (query, 0, QW, True, HD**-0.5),
            (key_t, QW, KW, True, 1.0),
            (value_t, QW + KW, KW, False, 1.0),
        ):
            for at in range(0, count, 256):
                width = min(256, count - at)
                made = nn(normed[span, :], weight[:, base + at : base + at + width]).T
                for to in range(0, width, HD):
                    block = made[to : to + HD]
                    if turn:
                        block = turned(block, cos_cols, sin_cols) * scale
                    target[at + to : at + to + HD, span] = block.astype(bf16)
        return carry

    lax.fori_loop(0, 2, project, 0)
    stores = [
        copied(query, q_out, out_sems.at[0]),
        copied(key_t, k_out, out_sems.at[1]),
        copied(value_t, v_out, out_sems.at[2]),
        copied(normed.at[:, pl.ds(0, D)], n_out, out_sems.at[3]),
        copied(cosine, cos_out, out_sems.at[4]),
        copied(sine, sin_out, out_sems.at[5]),
        copied(inner_t, zt_out, out_sems.at[6]),
    ]
    for store in stores:
        store.start()
    for j in range(KEYS):
        key_rows[j] = key_t[head_rows(j + g), :].T
        value_aug[j, :HD, :] = value_t[head_rows(j + g), :]
        value_aug[j, HD:, :] = jnp.ones((R, 2 * rows), bf16)
    mixed_t[:HD, :] = jnp.zeros((HD, 2 * rows), bf16)
    mixed_t[(HEADS + 1) * HD :, :] = jnp.zeros((HD, 2 * rows), bf16)

    for block in reversed(range(BLOCKS)):
        low, high = block * BLOCK, (block + 1) * BLOCK
        kept = chances[block]
        fill_mask(bias, starts, low, high)

        def score(h, side, low=low, high=high):
            top = None
            for first in range(0, high, BLOCK):
                span = slice(first, first + BLOCK)
                made = (
                    nn(key_rows[h // GROUP, span, :], query[head_rows(h + g), low:high])
                    + bias[span, :]
                )
                scores[side, span, :] = made
                best = jnp.max(made.reshape(BLOCK // 8, 8, BLOCK), axis=0)
                top = best if top is None else jnp.maximum(top, best)
            return jnp.max(top, axis=0, keepdims=True)

        def blend(h, side, top, low=low, high=high, kept=kept):
            for first in range(0, high, BLOCK):
                span = slice(first, first + BLOCK)
                kept[h, span, :] = jnp.exp(scores[side, span, :] - top).astype(bf16)
            made = nn(value_aug[h // GROUP, :, :high], kept[h])
            scale = 1.0 / made[HD : HD + 1]
            mixed_t[head_rows(h + 1), low:high] = (made[:HD] * scale).astype(bf16)
            scales[pl.ds(h, 1), low:high] = scale

        def group(j, top, score=score, blend=blend):
            for member in range(GROUP):
                h = j * GROUP + member
                later = score(jnp.minimum(h + 1, HEADS - 1), (member + 1) % GROUP)
                blend(h, member, top)
                top = later
            return top

        lax.fori_loop(0, KEYS, group, score(0, 0))
        stores.append(copied(kept, chances_out[block], keep_sem.at[block]))
        stores[-1].start()
        for pair in range(QW // 128):
            side = pl.ds(pl.multiple_of((2 * pair + 1 - g) * HD, HD), 128)
            mixed[low:high, pair * 128 : pair * 128 + 128] = mixed_t[side, low:high].T
    last = [
        copied(mixed.at[here], o_own, out_sems.at[7]),
        copied(mixed.at[there], o_send, out_sems.at[8]),
        copied(mixed_t, o_out, out_sems.at[9]),
        copied(scales, scale_out, out_sems.at[10]),
    ]
    for store in last:
        store.start()
    for store in stores + last:
        store.wait()


def attend(adapter, tok_own, *rest):
    rows = tok_own.shape[0]
    length = 2 * rows
    shape = jax.ShapeDtypeStruct
    return pl.pallas_call(
        attend_kernel,
        out_shape=[
            shape((rows, QW), bf16),
            shape((rows, QW), bf16),
            shape((QW, length), bf16),
            shape((KW, length), bf16),
            shape((KW, length), bf16),
            shape(((HEADS + 2) * HD, length), bf16),
            shape((length, D), bf16),
            shape((3 * R, length), bf16),
            shape((R, length), f32),
            shape((HD // 2, length), f32),
            shape((HD // 2, length), f32),
        ]
        + [shape((HEADS, (block + 1) * BLOCK, BLOCK), bf16) for block in range(BLOCKS)],
        in_specs=[SMEM, HBM, ANY, HBM, ANY] + [HBM] * 3 + [VMEM] * 3,
        out_specs=[HBM] * (11 + BLOCKS),
        scratch_shapes=[
            pltpu.VMEM((HEADS, (block + 1) * BLOCK, BLOCK), bf16) for block in range(BLOCKS)
        ]
        + [
            pltpu.VMEM((length, D), bf16),
            pltpu.VMEM((length, AUG), bf16),
            pltpu.VMEM((AUG, SPAN), bf16),
            pltpu.VMEM((128, D), bf16),
            pltpu.VMEM((QW, length), bf16),
            pltpu.VMEM((KW, length), bf16),
            pltpu.VMEM((KW, length), bf16),
            pltpu.VMEM((KEYS, length, HD), bf16),
            pltpu.VMEM((KEYS, HD + R, length), bf16),
            pltpu.VMEM(((HEADS + 2) * HD, length), bf16),
            pltpu.VMEM((length, QW), bf16),
            pltpu.VMEM((GROUP, length, BLOCK), f32),
            pltpu.VMEM((length, BLOCK), f32),
            pltpu.VMEM((HD // 2, length), f32),
            pltpu.VMEM((HD // 2, length), f32),
            pltpu.VMEM((3 * R, length), bf16),
            pltpu.VMEM((R, length), f32),
            pltpu.SemaphoreType.DMA((5,)),
            pltpu.SemaphoreType.DMA((9,)),
            pltpu.SemaphoreType.DMA((11,)),
            pltpu.SemaphoreType.DMA((BLOCKS,)),
        ],
        compiler_params=pltpu.CompilerParams(vmem_limit_bytes=50 << 20),
        cost_estimate=pl.CostEstimate(
            flops=16 * 10**9, bytes_accessed=16 << 20, transcendentals=6 * 10**6
        ),
        name="attend",
    )(adapter, tok_own, *rest)


def normed_back(rows, gain_row, grad):
    scale = lax.rsqrt(jnp.mean(rows * rows, axis=-1, keepdims=True) + epsilon)
    scaled = grad * gain_row
    inside = jnp.mean(rows * scaled, axis=-1, keepdims=True)
    return scale * (scaled - rows * (scale * scale * inside))


def rounded_up(count, unit):
    return -(-count // unit) * unit


def feed_lanes(reps):
    return rounded_up((5 * D + 3 * FF) // reps, 256)


def qkv_lanes(reps):
    return rounded_up((4 * D + 2 * KV) // reps + 1, 128)


def packed(grads, reps, target):
    for rep in range(reps):
        at = 0
        for grad in grads:
            piece = grad.shape[-1] // reps
            share = grad[:, rep * piece : (rep + 1) * piece]
            target[rep * R : (rep + 1) * R, at : at + piece] = share.astype(target.dtype)
            at += piece


def feed_kernel(
    reps,
    adapter,
    o_own_in,
    o_oth_in,
    tok_in,
    cot_in,
    wo_own,
    wo_oth,
    wgu_own,
    wgu_oth,
    wd_own,
    wd_oth,
    a_down,
    lower_t,
    upper_width,
    upper_hidden,
    gains_own,
    gains_oth,
    layer_out,
    grad_middle,
    do_own_out,
    do_oth_out,
    pack_own_out,
    pack_send_out,
    o_own,
    o_oth,
    tok,
    cot,
    do_own,
    do_oth,
    wout,
    wg,
    wu,
    wd,
    at_out,
    at_gu,
    b_out,
    b_down,
    middle,
    normed,
    cot_aug,
    total,
    back,
    result,
    z_gu_t,
    dz_down_t,
    ga_out,
    pack,
    sems,
    o_sems,
    out_sems,
):
    g = lax.axis_index("grp")
    chosen = adapter[0]
    gain = gain_row(g, gains_own, gains_oth, 1)
    steps = FF // TILE
    each = steps // 2
    w_here = pl.ds(pl.multiple_of(g * HALF, 64), HALF)
    w_there = pl.ds(pl.multiple_of((1 - g) * HALF, 64), HALF)

    def column(step):
        owner = jnp.where(step < each, g, 1 - g)
        return owner * (FF // 2) + (step % each) * TILE

    def copies(step, slot):
        at = pl.multiple_of(column(step), TILE)
        gate_at = pl.ds(at, TILE)
        up_at = pl.ds(pl.multiple_of(FF + at, TILE), TILE)
        sem = lambda k: sems.at[slot, k]
        return [
            copied(wgu_own.at[:, gate_at], wg.at[slot, w_here], sem(0)),
            copied(wgu_oth.at[:, gate_at], wg.at[slot, w_there], sem(1)),
            copied(wgu_own.at[:, up_at], wu.at[slot, w_here], sem(2)),
            copied(wgu_oth.at[:, up_at], wu.at[slot, w_there], sem(3)),
            copied(upper_hidden.at[0, chosen, :, gate_at], wg.at[slot, pl.ds(D, R)], sem(4)),
            copied(upper_hidden.at[1, chosen, :, gate_at], wu.at[slot, pl.ds(D + R, R)], sem(5)),
            copied(a_down.at[gate_at], wd.at[slot, :, pl.ds(D, 128)], sem(6)),
        ]

    def down_copy(source, step, slot):
        local = pl.ds(pl.multiple_of((step % each) * TILE, TILE), TILE)
        return copied(source.at[local], wd.at[slot, :, pl.ds(0, D)], sems.at[slot, 7])

    def start(step, slot):
        for copy in copies(step, slot):
            copy.start()

        @pl.when(step < each)
        def _():
            down_copy(wd_own, step, slot).start()

        @pl.when(step >= each)
        def _():
            down_copy(wd_oth, step, slot).start()

    def wait(step, slot):
        for copy in copies(step, slot):
            copy.wait()
        down_copy(wd_own, step, slot).wait()

    for slot in range(2):
        wg[slot, D:, :] = jnp.zeros((128, TILE), bf16)
        wu[slot, D:, :] = jnp.zeros((128, TILE), bf16)
        at_out[slot] = jnp.zeros((128, QW), bf16)
        wout[slot, :HD, :D] = jnp.zeros((HD, D), bf16)
        wout[slot, HALF:, :D] = jnp.zeros((HD, D), bf16)
    for ref in (at_gu, b_out, b_down):
        ref[...] = jnp.zeros_like(ref)
    own_at = pl.multiple_of(g * 512, 128)
    oth_at = pl.multiple_of((1 - g) * 512, 128)
    loads = [
        copied(
            wo_own, wout.at[0, pl.ds(pl.multiple_of(g * HD, HD), HALF), pl.ds(0, D)], o_sems.at[0]
        ),
        copied(
            wo_oth,
            wout.at[1, pl.ds(pl.multiple_of((1 - g) * HD, HD), HALF), pl.ds(0, D)],
            o_sems.at[1],
        ),
        copied(lower_t.at[3, chosen, :, pl.ds(own_at, QW)], at_out.at[0, pl.ds(0, R)], o_sems.at[2]),
        copied(lower_t.at[3, chosen, :, pl.ds(oth_at, QW)], at_out.at[1, pl.ds(0, R)], o_sems.at[3]),
        copied(lower_t.at[4, chosen], at_gu.at[pl.ds(0, R)], o_sems.at[4]),
        copied(lower_t.at[5, chosen], at_gu.at[pl.ds(R, R)], o_sems.at[5]),
        copied(upper_width.at[1, chosen], b_out.at[pl.ds(0, R)], o_sems.at[6]),
        copied(upper_width.at[2, chosen], b_down.at[pl.ds(0, R)], o_sems.at[7]),
        copied(o_own_in, o_own, o_sems.at[8]),
        copied(o_oth_in, o_oth, o_sems.at[9]),
        copied(tok_in, tok, o_sems.at[10]),
        copied(cot_in, cot, o_sems.at[11]),
    ]
    first, second, third = loads[11:] + loads[2:4] + loads[7:8], loads[:2] + loads[8:10], loads[4:7] + loads[10:11]
    for load in first + second + third:
        load.start()
    pack[...] = jnp.zeros_like(pack)
    total[...] = jnp.zeros_like(total)
    back[...] = jnp.zeros_like(back)
    for load in first:
        load.wait()
    cot_aug[:, :D] = cot[...]
    dz_down = nt(cot[...], b_down[...])
    cot_aug[:, D:] = dz_down.astype(bf16)
    dz_down_t[...] = dz_down.T[:R, :].astype(bf16)
    for slot in range(2):
        wout[slot, :, D:] = at_out[slot].T
    for load in second + third:
        load.wait()
    start(0, 0)
    made = nn(o_own[...], wout[0]) + nn(o_oth[...], wout[1])
    inner_out = made[:, D:].astype(bf16)
    middle[...] = tok[...].astype(f32) + made[:, :D] + nn(inner_out, b_out[...])
    scale = lax.rsqrt(jnp.mean(middle[...] * middle[...], axis=-1, keepdims=True) + epsilon)
    normed[:, :D] = (middle[...] * scale * gain).astype(bf16)
    inner_gu = nt(normed[:, :D], at_gu[...])
    normed[:, D:] = inner_gu.astype(bf16)
    z_gu_t[...] = inner_gu.T[: 2 * R, :].astype(bf16)

    def step_body(step, carry):
        slot = step % 2

        @pl.when(step + 1 < steps)
        def _():
            start(step + 1, 1 - slot)

        wait(step, slot)
        gate = nn(normed[...], wg[slot])
        up = nn(normed[...], wu[slot])
        grad_active = nt(cot_aug[...], wd[slot])
        sigmoid = 1.0 / (1.0 + jnp.exp(-gate))
        silu = gate * sigmoid
        active = (silu * up).astype(bf16)
        grad_gate = (grad_active * up * (sigmoid * (1.0 + gate * (1.0 - sigmoid)))).astype(bf16)
        grad_up = (grad_active * silu).astype(bf16)
        total[...] += nn(active, wd[slot])
        back[...] += nt(grad_gate, wg[slot]) + nt(grad_up, wu[slot])
        shares = (
            nn(dz_down_t[...], active),
            nn(z_gu_t[...], grad_gate)[:R],
            nn(z_gu_t[...], grad_up)[R:],
        )
        piece = FF // reps
        base = column(step) // piece
        for index, share in enumerate(shares):
            at = 5 * (D // reps) + index * piece
            for rep in range(TILE // piece):
                target = pl.ds(pl.multiple_of((base + rep) * R, R), R)
                pack[target, at : at + piece] = share[:, rep * piece : (rep + 1) * piece].astype(bf16)
        return carry

    lax.fori_loop(0, steps, step_body, 0)

    inner_down = total[:, D:].astype(bf16)
    result[...] = (middle[...] + total[:, :D] + nn(inner_down, b_down[...])).astype(bf16)
    stores = [copied(result, layer_out, out_sems.at[0])]
    stores[0].start()
    gb_down = nn(total[:, D:].T[:R, :].astype(bf16), cot[...])
    dz_gu = back[:, D:].astype(bf16)
    grad_normed = back[:, :D] + nn(dz_gu, at_gu[...])
    grad = cot[...].astype(f32) + normed_back(middle[...], gain, grad_normed)
    total[:, :D] = grad
    stores.append(copied(total.at[:, pl.ds(0, D)], grad_middle, out_sems.at[1]))
    stores[1].start()
    branch = normed
    ga_gu = nn(back[:, D:].T[: 2 * R, :].astype(bf16), normed[:, :D])
    branch[:, :D] = grad.astype(bf16)
    dz_out = nt(branch[:, :D], b_out[...])
    branch[:, D:] = dz_out.astype(bf16)
    dz_out_t = dz_out.T[:R, :].astype(bf16)
    do_oth[...] = nt(wout[1], branch[...]).astype(bf16)
    stores.append(copied(do_oth, do_oth_out, out_sems.at[2]))
    stores[-1].start()
    do_own[...] = nt(wout[0], branch[...]).astype(bf16)
    stores.append(copied(do_own, do_own_out, out_sems.at[3]))
    stores[-1].start()
    gb_out = nn(inner_out.astype(f32).T[:R, :].astype(bf16), branch[:, :D])
    ga_out[...] = jnp.zeros_like(ga_out)
    ga_out[:, pl.ds(own_at, QW)] += nn(dz_out_t, o_own[...])
    ga_out[:, pl.ds(oth_at, QW)] += nn(dz_out_t, o_oth[...])
    packed([ga_out[...], ga_gu[:R], ga_gu[R:], gb_out, gb_down], reps, pack)
    half = pack.shape[1] // 2
    for index, (side, target) in enumerate(((g, pack_own_out), (1 - g, pack_send_out))):
        source = pack.at[:, pl.ds(pl.multiple_of(side * half, 128), half)]
        stores.append(copied(source, target, out_sems.at[4 + index]))
        stores[-1].start()
    for store in stores:
        store.wait()


def feed(reps, *args):
    rows = args[3].shape[0]
    half = feed_lanes(reps) // 2
    shape = jax.ShapeDtypeStruct
    return pl.pallas_call(
        functools.partial(feed_kernel, reps),
        out_shape=[
            shape((rows, D), bf16),
            shape((rows, D), f32),
            shape((QW, rows), bf16),
            shape((QW, rows), bf16),
            shape((reps * R, half), bf16),
            shape((reps * R, half), bf16),
        ],
        in_specs=[SMEM, HBM, ANY] + [HBM] * 12 + [VMEM] * 2,
        out_specs=[HBM] * 6,
        scratch_shapes=[
            pltpu.VMEM((rows, QW), bf16),
            pltpu.VMEM((rows, QW), bf16),
            pltpu.VMEM((rows, D), bf16),
            pltpu.VMEM((rows, D), bf16),
            pltpu.VMEM((QW, rows), bf16),
            pltpu.VMEM((QW, rows), bf16),
            pltpu.VMEM((2, QW, AUG), bf16),
            pltpu.VMEM((2, AUG, TILE), bf16),
            pltpu.VMEM((2, AUG, TILE), bf16),
            pltpu.VMEM((2, TILE, AUG), bf16),
            pltpu.VMEM((2, 128, QW), bf16),
            pltpu.VMEM((128, D), bf16),
            pltpu.VMEM((128, D), bf16),
            pltpu.VMEM((128, D), bf16),
            pltpu.VMEM((rows, D), f32),
            pltpu.VMEM((rows, AUG), bf16),
            pltpu.VMEM((rows, AUG), bf16),
            pltpu.VMEM((rows, AUG), f32),
            pltpu.VMEM((rows, AUG), f32),
            pltpu.VMEM((rows, D), bf16),
            pltpu.VMEM((2 * R, rows), bf16),
            pltpu.VMEM((R, rows), bf16),
            pltpu.VMEM((R, D), f32),
            pltpu.VMEM((reps * R, 2 * half), bf16),
            pltpu.SemaphoreType.DMA((2, 8)),
            pltpu.SemaphoreType.DMA((12,)),
            pltpu.SemaphoreType.DMA((6,)),
        ],
        compiler_params=pltpu.CompilerParams(vmem_limit_bytes=46 << 20),
        cost_estimate=pl.CostEstimate(
            flops=30 * 10**9, bytes_accessed=36 << 20, transcendentals=2 * 10**6
        ),
        name="feed",
    )(*args)


def attend_back_kernel(
    reps,
    adapter,
    do_own,
    do_oth,
    o_in,
    normed,
    qkv_own,
    qkv_oth,
    lower_t,
    upper_width,
    upper_keys,
    query_in,
    k_in,
    v_in,
    zt_in,
    scale_in,
    cos_in,
    sin_in,
    pack_own_in,
    pack_oth_in,
    *refs,
):
    attend_back_body(
        reps,
        adapter,
        do_own,
        do_oth,
        o_in,
        normed,
        qkv_own,
        qkv_oth,
        lower_t,
        upper_width,
        upper_keys,
        query_in,
        k_in,
        v_in,
        zt_in,
        scale_in,
        cos_in,
        sin_in,
        pack_own_in,
        pack_oth_in,
        refs[:BLOCKS],
        refs[BLOCKS + 4 : 2 * BLOCKS + 4],
        *refs[BLOCKS : BLOCKS + 4],
        *refs[2 * BLOCKS + 4 :],
    )


def attend_back_body(
    reps,
    adapter,
    do_own,
    do_oth,
    o_in,
    normed,
    qkv_own,
    qkv_oth,
    lower_t,
    upper_width,
    upper_keys,
    query_in,
    k_in,
    v_in,
    zt_in,
    scale_in,
    cos_in,
    sin_in,
    pack_own_in,
    pack_oth_in,
    chances_in,
    chances,
    dy_out,
    dz_out,
    part_out,
    exchange_out,
    query,
    key_t,
    value_t,
    zt,
    scales,
    cosine,
    sine,
    pack_own,
    pack_oth,
    inner_low,
    exchange,
    outgoing,
    maps,
    grad_o,
    mixed_t,
    n_rows,
    weight,
    value_rows,
    delta,
    dq,
    dk,
    dv,
    dy_t,
    dy,
    grad_scores,
    gb_q,
    gb_kv,
    pack,
    sems,
    b_sems,
    out_sem,
    keep_sem,
):
    g = lax.axis_index("grp")
    chosen = adapter[0]
    length = query.shape[1]
    rows = length // 2
    here = pl.ds(pl.multiple_of(g * rows, 128), rows)
    there = pl.ds(pl.multiple_of((1 - g) * rows, 128), rows)
    weight[D:, :] = jnp.zeros((128, SPAN), bf16)
    maps[...] = jnp.zeros_like(maps)
    early = [
        copied(k_in, key_t, sems.at[0]),
        copied(v_in, value_t, sems.at[1]),
    ]
    loads = [
        copied(do_own, grad_o.at[:, here], sems.at[2]),
        copied(do_oth, grad_o.at[:, there], sems.at[3]),
        copied(o_in, mixed_t, sems.at[4]),
        copied(query_in, query, sems.at[5]),
        copied(scale_in, scales, sems.at[6]),
    ]
    late = [
        copied(cos_in, cosine, sems.at[7]),
        copied(sin_in, sine, sems.at[8]),
        copied(normed, n_rows, sems.at[9]),
        copied(zt_in, zt, sems.at[10]),
        copied(pack_own_in, pack_own, sems.at[11]),
        copied(pack_oth_in, pack_oth, sems.at[12]),
    ] + [
        copied(lower_t.at[index, chosen], maps.at[pl.ds(index * R, R)], sems.at[13 + index])
        for index in range(3)
    ] + qkv_loads(g, chosen, qkv_own, qkv_oth, upper_width, upper_keys, weight, b_sems)
    kept = [
        copied(chances_in[block], chances[block], keep_sem.at[block]) for block in range(BLOCKS)
    ]
    for load in early + loads:
        load.start()
    kept[0].start()
    dk[...] = jnp.zeros_like(dk)
    dv[...] = jnp.zeros_like(dv)
    dy_t[...] = jnp.zeros_like(dy_t)
    for load in early:
        load.wait()
    for j in range(KEYS):
        value_rows[j] = value_t[head_rows(j + g), :].T
    for load in loads:
        load.wait()
    for load in kept[1:] + late:
        load.start()
    for h in range(HEADS):
        scaled = grad_o[head_rows(h + g), :].astype(f32) * scales[h : h + 1, :]
        product = scaled * mixed_t[(h + 1) * HD : (h + 2) * HD, :].astype(f32)
        delta[h : h + 1, :] = jnp.sum(product, axis=0, keepdims=True)
        grad_o[head_rows(h + g), :] = scaled.astype(bf16)

    for block in range(length // BLOCK):
        low, high = block * BLOCK, (block + 1) * BLOCK
        found = chances[block]
        kept[block].wait()

        def score(h, side, low=low, high=high, found=found):
            deltas = delta[pl.ds(h, 1), low:high]
            for first in range(0, high, BLOCK):
                span = slice(first, first + BLOCK)
                grad = nn(value_rows[h // GROUP, span, :], grad_o[head_rows(h + g), low:high])
                chance = found[h, span, :].astype(f32)
                grad_scores[side, span, :] = (chance * (grad - deltas)).astype(bf16)

        def spread(h, side, low=low, high=high, found=found):
            dq[h, :, low:high] = nn(
                key_t[head_rows(h // GROUP + g), :high], grad_scores[side, :high, :]
            )
            return (
                nt(grad_o[head_rows(h + g), low:high], found[h]),
                nt(query[head_rows(h + g), low:high], grad_scores[side, :high, :]),
            )

        def group(j, carry, high=high, score=score, spread=spread):
            sums = []
            for member in range(GROUP):
                h = j * GROUP + member
                score(jnp.minimum(h + 1, HEADS - 1), (member + 1) % GROUP)
                sums.append(spread(h, member))
            dv[j, :, :high] += sums[0][0] + sums[1][0] + sums[2][0]
            dk[j, :, :high] += sums[0][1] + sums[1][1] + sums[2][1]
            return carry

        score(0, 0)
        lax.fori_loop(0, KEYS, group, 0)

    for load in late:
        load.wait()
    back_sine = -sine[...]
    for h in range(HEADS):
        dy_t[(h + 1) * HD : (h + 2) * HD, :] = (
            turned(dq[h], cosine[...], back_sine) * HD**-0.5
        ).astype(bf16)
    key_base = (HEADS + 2) * HD
    value_base = key_base + (KEYS + 2) * HD
    for j in range(KEYS):
        at = key_base + (j + 1) * HD
        dy_t[at : at + HD, :] = turned(dk[j], cosine[...], back_sine).astype(bf16)
        at = value_base + (j + 1) * HD
        dy_t[at : at + HD, :] = dv[j].astype(bf16)
    for base, count, to in ((0, QW, 0), (key_base, KW, QW), (value_base, KW, QW + KW)):
        for at in range(0, count, 128):
            side = pl.ds(pl.multiple_of(base + at + (1 - g) * HD, HD), 128)
            dy[:, to + at : to + at + 128] = dy_t[side, :].T
    store = copied(dy.at[here], dy_out, out_sem.at[0])
    store.start()
    made = nt(dy[there, :], weight[...])
    theirs = made[:, D:]
    outgoing[...] = (made[:, :D] + nn(theirs.astype(bf16), maps[...])).astype(bf16)
    part_store = copied(outgoing, part_out, out_sem.at[3])
    part_store.start()
    mine = nt(dy[here, :], weight[D:, :])
    inner_low[...] = mine.astype(bf16)
    inner_store = copied(inner_low, dz_out, out_sem.at[1])
    inner_store.start()
    gb = nn(zt[...], dy[...])
    gb_q[...] = jnp.zeros_like(gb_q)
    gb_kv[...] = jnp.zeros_like(gb_kv)
    gb_q[:, pl.ds(pl.multiple_of(g * 512, 128), QW)] = gb[:R, :QW]
    for index in range(2):
        gb_kv[index, :, pl.ds(pl.multiple_of(g * 128, 128), KW)] = gb[
            (index + 1) * R : (index + 2) * R, QW + index * KW : QW + (index + 1) * KW
        ]
    ga = nn(theirs.T[: 3 * R, :].astype(bf16), n_rows[there, :]) + nn(
        mine.T[: 3 * R, :].astype(bf16), n_rows[here, :]
    )
    pack[...] = jnp.zeros_like(pack)
    packed(
        [ga[:R], ga[R : 2 * R], ga[2 * R :], gb_q[...], gb_kv[0], gb_kv[1]],
        reps,
        pack,
    )
    half = pack_own.shape[1]
    width = pack.shape[1]
    exchange[:, :half] = (pack_own[...].astype(f32) + pack_oth[...].astype(f32)).astype(bf16)
    exchange[:, half:] = jnp.where(
        lanes(pack.shape) == width - 1, chosen.astype(f32), pack[...].astype(f32)
    ).astype(bf16)
    last = copied(exchange, exchange_out, out_sem.at[2])
    last.start()
    for copy in (store, inner_store, part_store, last):
        copy.wait()


def attend_back(reps, *args):
    rows = args[1].shape[1]
    length = 2 * rows
    half = feed_lanes(reps) // 2
    width = qkv_lanes(reps)
    shape = jax.ShapeDtypeStruct
    return pl.pallas_call(
        functools.partial(attend_back_kernel, reps),
        out_shape=[
            shape((rows, SPAN), bf16),
            shape((rows, 128), bf16),
            shape((rows, D), bf16),
            shape((reps * R, half + width), bf16),
        ],
        in_specs=[SMEM, HBM, ANY] + [HBM] * 15 + [ANY] + [HBM] * BLOCKS,
        out_specs=[HBM] * 4,
        scratch_shapes=[
            pltpu.VMEM((HEADS, (block + 1) * BLOCK, BLOCK), bf16) for block in range(BLOCKS)
        ]
        + [
            pltpu.VMEM((QW, length), bf16),
            pltpu.VMEM((KW, length), bf16),
            pltpu.VMEM((KW, length), bf16),
            pltpu.VMEM((3 * R, length), bf16),
            pltpu.VMEM((R, length), f32),
            pltpu.VMEM((HD // 2, length), f32),
            pltpu.VMEM((HD // 2, length), f32),
            pltpu.VMEM((reps * R, half), bf16),
            pltpu.VMEM((reps * R, half), bf16),
            pltpu.VMEM((rows, 128), bf16),
            pltpu.VMEM((reps * R, half + width), bf16),
            pltpu.VMEM((rows, D), bf16),
            pltpu.VMEM((128, D), bf16),
            pltpu.VMEM((QW, length), bf16),
            pltpu.VMEM(((HEADS + 2) * HD, length), bf16),
            pltpu.VMEM((length, D), bf16),
            pltpu.VMEM((AUG, SPAN), bf16),
            pltpu.VMEM((KEYS, length, HD), bf16),
            pltpu.VMEM((R, length), f32),
            pltpu.VMEM((HEADS, HD, length), f32),
            pltpu.VMEM((KEYS, HD, length), f32),
            pltpu.VMEM((KEYS, HD, length), f32),
            pltpu.VMEM(((HEADS + 2 * KEYS + 6) * HD, length), bf16),
            pltpu.VMEM((length, SPAN), bf16),
            pltpu.VMEM((GROUP, length, BLOCK), bf16),
            pltpu.VMEM((R, D), f32),
            pltpu.VMEM((2, R, KV), f32),
            pltpu.VMEM((reps * R, width), bf16),
            pltpu.SemaphoreType.DMA((16,)),
            pltpu.SemaphoreType.DMA((9,)),
            pltpu.SemaphoreType.DMA((4,)),
            pltpu.SemaphoreType.DMA((BLOCKS,)),
        ],
        compiler_params=pltpu.CompilerParams(vmem_limit_bytes=50 << 20),
        cost_estimate=pl.CostEstimate(
            flops=24 * 10**9, bytes_accessed=20 << 20, transcendentals=6 * 10**6
        ),
        name="attend_back",
    )(*args)


def finish_kernel(
    adapter,
    dy_in,
    dz_in,
    qkv_own,
    qkv_oth,
    lower_t,
    tok_in,
    gains_own,
    gains_oth,
    part_in,
    middle_in,
    out,
    dy,
    dz,
    tok,
    part,
    grad_middle,
    weight,
    maps,
    result,
    sems,
    w_sems,
    out_sem,
):
    g = lax.axis_index("grp")
    chosen = adapter[0]
    maps[...] = jnp.zeros_like(maps)
    loads = qkv_loads(g, chosen, qkv_own, qkv_oth, None, None, weight, w_sems)
    for index, (source, target) in enumerate(
        ((dy_in, dy), (dz_in, dz), (tok_in, tok), (middle_in, grad_middle), (part_in, part))
    ):
        loads.append(copied(source, target, sems.at[index]))
    for index in range(3):
        loads.append(
            copied(lower_t.at[index, chosen], maps.at[pl.ds(index * R, R)], sems.at[5 + index])
        )
    for load in loads:
        load.start()
    gain = gain_row(g, gains_own, gains_oth, 0)
    for load in loads:
        load.wait()

    def half(index, carry):
        count = tok.shape[0] // 2
        span = pl.ds(pl.multiple_of(index * count, 128), count)
        grad = nt(dy[span, :], weight[...]) + nn(dz[span, :], maps[...]) + part[span, :].astype(f32)
        result[span, :] = (
            grad_middle[span, :] + normed_back(tok[span, :].astype(f32), gain, grad)
        ).astype(bf16)
        return carry

    lax.fori_loop(0, 2, half, 0)
    store = copied(result, out, out_sem.at[0])
    store.start()
    store.wait()


def finish(*args):
    rows = args[1].shape[0]
    return pl.pallas_call(
        finish_kernel,
        out_shape=jax.ShapeDtypeStruct((rows, D), bf16),
        in_specs=[SMEM] + [HBM] * 6 + [VMEM] * 2 + [ANY, HBM],
        out_specs=HBM,
        scratch_shapes=[
            pltpu.VMEM((rows, SPAN), bf16),
            pltpu.VMEM((rows, 128), bf16),
            pltpu.VMEM((rows, D), bf16),
            pltpu.VMEM((rows, D), bf16),
            pltpu.VMEM((rows, D), f32),
            pltpu.VMEM((D, SPAN), bf16),
            pltpu.VMEM((128, D), bf16),
            pltpu.VMEM((rows, D), bf16),
            pltpu.SemaphoreType.DMA((8,)),
            pltpu.SemaphoreType.DMA((6,)),
            pltpu.SemaphoreType.DMA((1,)),
        ],
        compiler_params=pltpu.CompilerParams(vmem_limit_bytes=VMEM_BYTES),
        cost_estimate=pl.CostEstimate(
            flops=4 * 10**9, bytes_accessed=10 << 20, transcendentals=0
        ),
        name="finish",
    )(*args)


def collect_kernel(source, keep, send, received, sem):
    load = copied(source, received, sem.at[0])
    load.start()
    load.wait()
    g = lax.axis_index("grp")
    count, width = received.shape
    quota = NAD // 2
    label = received[:, width - 1 :].astype(f32)
    lane = lanes((count, NAD * R))
    row = lax.broadcasted_iota(jnp.int32, (count, NAD * R), 0)
    picks = ((lane // R).astype(f32) == label) & (lane % R == row % R)
    sums = tn(picks.astype(f32).astype(bf16), received[...])
    first = g == 0
    for adapter in range(quota):
        low = sums[adapter * R : (adapter + 1) * R]
        high = sums[(quota + adapter) * R : (quota + adapter + 1) * R]
        keep[adapter] = jnp.where(first, low, high)
        send[adapter] = jnp.where(first, high, low)


def collect(received):
    shape = jax.ShapeDtypeStruct((NAD // 2, R, received.shape[1]), f32)
    return pl.pallas_call(
        collect_kernel,
        out_shape=[shape, shape],
        in_specs=[ANY],
        out_specs=[VMEM] * 2,
        scratch_shapes=[
            pltpu.VMEM(received.shape, bf16),
            pltpu.SemaphoreType.DMA((1,)),
        ],
        compiler_params=pltpu.CompilerParams(vmem_limit_bytes=8 << 20),
        cost_estimate=pl.CostEstimate(flops=10**8, bytes_accessed=2 << 20, transcendentals=0),
        name="collect",
    )(received)


def deliver_kernel(reps, keep, other, lower, down, width, keys, hidden, feeds, qkvs):
    g = lax.axis_index("grp")
    half = feeds.shape[-1] // 2
    feeds[:, :, pl.ds(pl.multiple_of(g * half, 128), half)] = keep[:, :, :half]
    feeds[:, :, pl.ds(pl.multiple_of((1 - g) * half, 128), half)] = other[:, :, :half]
    qkvs[...] = keep[:, :, half:] + other[:, :, half:]
    piece, tall, short = D // reps, FF // reps, KV // reps
    for index in range(3):
        lower[index] = qkvs[:, :, index * piece : (index + 1) * piece]
        lower[3 + index] = feeds[:, :, index * piece : (index + 1) * piece]
    width[0] = qkvs[:, :, 3 * piece : 4 * piece]
    width[1] = feeds[:, :, 3 * piece : 4 * piece]
    width[2] = feeds[:, :, 4 * piece : 5 * piece]
    for index in range(2):
        at = 4 * piece + index * short
        keys[index] = qkvs[:, :, at : at + short]
        at = 5 * piece + (1 + index) * tall
        hidden[index] = feeds[:, :, at : at + tall]
    down[...] = feeds[:, :, 5 * piece : 5 * piece + tall]


def deliver(reps, keep, other):
    quota = NAD // 2
    shape = lambda *dims: jax.ShapeDtypeStruct(dims, f32)
    return pl.pallas_call(
        functools.partial(deliver_kernel, reps),
        out_shape=[
            shape(6, quota, R, D // reps),
            shape(quota, R, FF // reps),
            shape(3, quota, R, D // reps),
            shape(2, quota, R, KV // reps),
            shape(2, quota, R, FF // reps),
        ],
        in_specs=[VMEM] * 2,
        out_specs=[VMEM] * 5,
        scratch_shapes=[
            pltpu.VMEM((quota, R, feed_lanes(reps)), f32),
            pltpu.VMEM((quota, R, qkv_lanes(reps)), f32),
        ],
        compiler_params=pltpu.CompilerParams(vmem_limit_bytes=8 << 20),
        cost_estimate=pl.CostEstimate(flops=10**6, bytes_accessed=1 << 20, transcendentals=0),
        name="deliver",
    )(keep, other)


def per_device(
    tokens,
    cotangent,
    segment_ids,
    adapter_ids,
    norm_gains,
    frozen_qkv,
    frozen_out,
    frozen_gate_up,
    frozen_down,
    lower_mats,
    lower_down,
    upper_width,
    upper_keys,
    upper_hidden,
):
    reps = lax.axis_size("rep")
    chosen = adapter_ids[0]
    first = lax.axis_index("grp") == 0
    swap = lambda value: lax.ppermute(value, "grp", SWAP)

    tok_own = tokens[0]
    tok_oth = swap(tok_own)
    qkv_oth = swap(frozen_qkv)
    gains_oth = swap(norm_gains)
    a_down = jnp.pad(
        lax.dynamic_index_in_dim(lower_down, chosen, 0, keepdims=False), ((0, 0), (0, 128 - R))
    )
    tok_oth, qkv_oth, gains_oth, a_down, wo, wgu, wd = lax.optimization_barrier(
        (tok_oth, qkv_oth, gains_oth, a_down, frozen_out, frozen_gate_up, frozen_down)
    )
    wo_oth = swap(wo)
    wgu_oth = swap(wgu)
    wd_oth = swap(wd)

    lower_t = lower_mats.transpose(0, 1, 3, 2)
    gains = (norm_gains, gains_oth)

    (o_own, o_send, query, key_t, value_t, mixed_t, normed, zt, scales, cosine, sine, *chances) = (
        attend(
            adapter_ids,
            tok_own,
            tok_oth,
            frozen_qkv,
            qkv_oth,
            lower_t,
            upper_width,
            upper_keys,
            *gains,
            segment_ids,
        )
    )
    o_oth = swap(o_send)
    layer_out, grad_middle, do_own, do_send, pack_own, pack_send = feed(
        reps,
        adapter_ids,
        o_own,
        o_oth,
        tok_own,
        cotangent[0],
        frozen_out,
        wo_oth,
        frozen_gate_up,
        wgu_oth,
        frozen_down,
        wd_oth,
        a_down,
        lower_t,
        upper_width,
        upper_hidden,
        *gains,
    )
    do_oth = swap(do_send)
    pack_oth = swap(pack_send)
    dy, dz, part_send, exchange = attend_back(
        reps,
        adapter_ids,
        do_own,
        do_oth,
        mixed_t,
        normed,
        frozen_qkv,
        qkv_oth,
        lower_t,
        upper_width,
        upper_keys,
        query,
        key_t,
        value_t,
        zt,
        scales,
        cosine,
        sine,
        pack_own,
        pack_oth,
        *chances,
    )
    received = lax.all_to_all(exchange, "rep", 0, 0, tiled=True)
    input_grad = finish(
        adapter_ids,
        dy,
        dz,
        frozen_qkv,
        qkv_oth,
        lower_t,
        tok_own,
        *gains,
        swap(part_send),
        grad_middle,
    )
    received, input_grad = lax.optimization_barrier((received, input_grad))
    keep, send = collect(received)
    lower, down, width, keys, hidden = deliver(reps, keep, swap(send))
    return (
        layer_out[None],
        input_grad[None],
        lower.transpose(0, 1, 3, 2),
        down.transpose(0, 2, 1),
        width,
        keys,
        hidden,
    )


def solution(mesh):
    return jax.shard_map(
        per_device,
        mesh=mesh,
        in_specs=(
            P("rep", "grp", None),
            P("rep", "grp", None),
            P("rep", None),
            P("rep"),
            P(None, "grp"),
            P("grp", None),
            P("grp", None),
            P("grp", None),
            P("grp", None),
            P(),
            P(),
            P(),
            P(),
            P(),
        ),
        out_specs=(
            P("rep", "grp", None),
            P("rep", "grp", None),
            P(None, "grp", "rep", None),
            P("grp", "rep", None),
            P(None, "grp", None, "rep"),
            P(None, "grp", None, "rep"),
            P(None, "grp", None, "rep"),
        ),
        check_vma=False,
    )
```

```python
import functools

import jax
import jax.numpy as jnp
import numpy as np
from jax import lax
from jax.experimental import pallas as pl
from jax.experimental.pallas import tpu as pltpu
from jax.sharding import PartitionSpec as P

D = 1152
H = 18
KVH = 6
HD = 64
FF = 3072
R = 16
NAD = 8
KV = 384

HALF = D // 2
HEADS = H // 2
GROUP = H // KVH
QW = 640
KW = 256
SPAN = QW + 2 * KW
AUG = D + 128
TILE = 768
BLOCK = 256
BLOCKS = 1024 // BLOCK
DOCS = 4
KEYS = HEADS // GROUP
VMEM_BYTES = 61900 * 1024

epsilon = 1e-05
theta_base = 10000.0
masked_value = -1e30
f32 = jnp.float32
bf16 = jnp.bfloat16
SWAP = [(0, 1), (1, 0)]

HBM = pl.BlockSpec(memory_space=pltpu.MemorySpace.HBM)
ANY = pl.BlockSpec(memory_space=pl.ANY)
VMEM = pl.BlockSpec(memory_space=pltpu.VMEM)
SMEM = pl.BlockSpec(memory_space=pltpu.SMEM)


def nn(left, right):
    return jnp.dot(left, right, preferred_element_type=f32)


def nt(left, right):
    return lax.dot_general(left, right, (((1,), (1,)), ((), ())), preferred_element_type=f32)


def tn(left, right):
    return lax.dot_general(left, right, (((0,), (0,)), ((), ())), preferred_element_type=f32)


def lanes(shape):
    return lax.broadcasted_iota(jnp.int32, shape, len(shape) - 1)


def gain_row(g, own, other, row):
    mine = own[row : row + 1, :].astype(f32)
    theirs = other[row : row + 1, :].astype(f32)
    return jnp.where(
        g == 0,
        jnp.concatenate([mine, theirs], axis=1),
        jnp.concatenate([theirs, mine], axis=1),
    )


def copied(source, target, sem):
    return pltpu.make_async_copy(source, target, sem)


def doc_starts(segments):
    return [
        jnp.sum(jnp.where(segments < doc, 1.0, 0.0), axis=-1, keepdims=True)
        for doc in range(1, DOCS)
    ]


def start_at(place, starts):
    found = jnp.zeros_like(place)
    for start in starts:
        found = jnp.where(place >= start, start, found)
    return found


def fill_angles(starts, cosine, sine):
    def both(angle):
        return jnp.cos(angle), jnp.sin(angle)

    powers = np.float32(theta_base) ** (-np.arange(HD // 2, dtype=np.float32) * 2.0 / HD)
    row = lax.broadcasted_iota(jnp.int32, (HD // 2, 128), 0)
    freqs = jnp.zeros(row.shape, f32)
    for index, power in enumerate(powers):
        freqs = jnp.where(row == index, np.float32(power), freqs)

    fine_cos, fine_sin = both(lanes(freqs.shape).astype(f32) * freqs)
    docs = [both(start * freqs) for start in starts]
    for at in range(0, cosine.shape[1], 128):
        wide_cos, wide_sin = both(float(at) * freqs)
        cos_p = wide_cos * fine_cos - wide_sin * fine_sin
        sin_p = wide_sin * fine_cos + wide_cos * fine_sin
        place = (lanes(freqs.shape) + at).astype(f32)
        cos_d, sin_d = jnp.ones_like(cos_p), jnp.zeros_like(cos_p)
        for start, (cos_s, sin_s) in zip(starts, docs):
            inside = place >= start
            cos_d = jnp.where(inside, cos_s, cos_d)
            sin_d = jnp.where(inside, sin_s, sin_d)
        cosine[:, at : at + 128] = cos_p * cos_d + sin_p * sin_d
        sine[:, at : at + 128] = sin_p * cos_d - cos_p * sin_d


def turned(block, cosine, sine):
    first, second = block[: HD // 2], block[HD // 2 :]
    return jnp.concatenate(
        [first * cosine - second * sine, second * cosine + first * sine], axis=0
    )


def head_rows(slot):
    return pl.ds(pl.multiple_of(slot * HD, HD), HD)


def fill_mask(bias, starts, low, high):
    place = lanes((1, BLOCK)).astype(f32) + low
    begin = start_at(place, starts)
    for first in range(0, high, BLOCK):
        key_place = lax.broadcasted_iota(jnp.int32, (BLOCK, BLOCK), 0).astype(f32) + first
        allowed = key_place >= begin
        if first == low:
            allowed = allowed & (key_place <= place)
        bias[first : first + BLOCK, :] = jnp.where(allowed, 0.0, masked_value)


def qkv_loads(g, side, own, oth, weight, sems):
    w_here = pl.ds(pl.multiple_of(g * HALF, 64), HALF)
    w_there = pl.ds(pl.multiple_of((1 - g) * HALF, 64), HALF)
    windows = (
        (pl.multiple_of(side * 512, 128), QW, 0),
        (pl.multiple_of(D + side * 128, 128), KW, QW),
        (pl.multiple_of(D + KV + side * 128, 128), KW, QW + KW),
    )
    loads = []
    for index, (at, width, to) in enumerate(windows):
        for part, (source, rows) in enumerate(((own, w_here), (oth, w_there))):
            loads.append(
                copied(
                    source.at[:, pl.ds(at, width)],
                    weight.at[rows, pl.ds(to, width)],
                    sems.at[2 * index + part],
                )
            )
    return loads


def upper_loads(g, chosen, upper_width, upper_keys, weight, base, sems):
    loads = []
    loads.append(
        copied(
            upper_width.at[0, chosen, :, pl.ds(pl.multiple_of(g * 512, 128), QW)],
            weight.at[pl.ds(base, R), pl.ds(0, QW)],
            sems.at[6],
        )
    )
    for index in range(2):
        loads.append(
            copied(
                upper_keys.at[index, chosen, :, pl.ds(pl.multiple_of(g * 128, 128), KW)],
                weight.at[pl.ds(base + (index + 1) * R, R), pl.ds(QW + index * KW, KW)],
                sems.at[7 + index],
            )
        )
    return loads


def attend_kernel(
    adapter,
    tok_own,
    tok_oth,
    qkv_own,
    qkv_oth,
    lower_t,
    upper_width,
    upper_keys,
    gains_own,
    gains_oth,
    segments,
    o_own,
    o_send,
    q_out,
    k_out,
    v_out,
    o_out,
    n_out,
    zt_out,
    scale_out,
    cos_out,
    sin_out,
    *refs,
):
    attend_body(
        adapter,
        tok_own,
        tok_oth,
        qkv_own,
        qkv_oth,
        lower_t,
        upper_width,
        upper_keys,
        gains_own,
        gains_oth,
        segments,
        o_own,
        o_send,
        q_out,
        k_out,
        v_out,
        o_out,
        n_out,
        zt_out,
        scale_out,
        cos_out,
        sin_out,
        refs[:BLOCKS],
        refs[BLOCKS : 2 * BLOCKS],
        *refs[2 * BLOCKS :],
    )


def attend_body(
    adapter,
    tok_own,
    tok_oth,
    qkv_own,
    qkv_oth,
    lower_t,
    upper_width,
    upper_keys,
    gains_own,
    gains_oth,
    segments,
    o_own,
    o_send,
    q_out,
    k_out,
    v_out,
    o_out,
    n_out,
    zt_out,
    scale_out,
    cos_out,
    sin_out,
    chances_out,
    chances,
    tok,
    normed,
    weight,
    maps,
    query,
    key_t,
    value_t,
    key_rows,
    value_aug,
    mixed_t,
    mixed,
    scores,
    bias,
    cosine,
    sine,
    inner_t,
    scales,
    sems,
    w_sems,
    out_sems,
    keep_sem,
):
    g = lax.axis_index("grp")
    chosen = adapter[0]
    rows = tok_own.shape[0]
    here = pl.ds(pl.multiple_of(g * rows, 128), rows)
    there = pl.ds(pl.multiple_of((1 - g) * rows, 128), rows)
    maps[...] = jnp.zeros_like(maps)
    weight[D:, :] = jnp.zeros((128, SPAN), bf16)
    loads = [
        copied(tok_own, tok.at[here], sems.at[0]),
        copied(tok_oth, tok.at[there], sems.at[1]),
    ] + [
        copied(lower_t.at[index, chosen], maps.at[pl.ds(index * R, R)], sems.at[2 + index])
        for index in range(3)
    ]
    w_loads = qkv_loads(g, g, qkv_own, qkv_oth, weight, w_sems)
    w_loads += upper_loads(g, chosen, upper_width, upper_keys, weight, D, w_sems)
    for load in loads:
        load.start()
    starts = doc_starts(segments[...])
    fill_angles(starts, cosine, sine)
    gain = gain_row(g, gains_own, gains_oth, 0)
    for load in loads:
        load.wait()
    for load in w_loads:
        load.start()

    def norm_part(part, carry):
        span = pl.ds(pl.multiple_of(part * rows, 128), rows)
        wide = tok[span, :].astype(f32)
        scale = lax.rsqrt(jnp.mean(wide * wide, axis=-1, keepdims=True) + epsilon)
        normed[span, :D] = (wide * scale * gain).astype(bf16)
        inner = nt(normed[span, :D], maps[...])
        normed[span, D:] = inner.astype(bf16)
        inner_t[:, span] = inner.T[: 3 * R, :].astype(bf16)
        return carry

    lax.fori_loop(0, 2, norm_part, 0)
    for load in w_loads:
        load.wait()

    def project(part, carry):
        span = pl.ds(pl.multiple_of(part * rows, 128), rows)
        cos_cols = cosine[:, span]
        sin_cols = sine[:, span]
        for target, base, count, turn, scale in (
            (query, 0, QW, True, HD**-0.5),
            (key_t, QW, KW, True, 1.0),
            (value_t, QW + KW, KW, False, 1.0),
        ):
            for at in range(0, count, 256):
                width = min(256, count - at)
                made = nn(normed[span, :], weight[:, base + at : base + at + width]).T
                for to in range(0, width, HD):
                    block = made[to : to + HD]
                    if turn:
                        block = turned(block, cos_cols, sin_cols) * scale
                    target[at + to : at + to + HD, span] = block.astype(bf16)
        return carry

    lax.fori_loop(0, 2, project, 0)
    stores = [
        copied(query, q_out, out_sems.at[0]),
        copied(key_t, k_out, out_sems.at[1]),
        copied(value_t, v_out, out_sems.at[2]),
        copied(normed.at[:, pl.ds(0, D)], n_out, out_sems.at[3]),
        copied(cosine, cos_out, out_sems.at[4]),
        copied(sine, sin_out, out_sems.at[5]),
        copied(inner_t, zt_out, out_sems.at[6]),
    ]
    for store in stores:
        store.start()
    for j in range(KEYS):
        key_rows[j] = key_t[head_rows(j + g), :].T
        value_aug[j, :HD, :] = value_t[head_rows(j + g), :]
        value_aug[j, HD:, :] = jnp.ones((R, 2 * rows), bf16)
    mixed_t[:HD, :] = jnp.zeros((HD, 2 * rows), bf16)
    mixed_t[(HEADS + 1) * HD :, :] = jnp.zeros((HD, 2 * rows), bf16)

    for block in reversed(range(BLOCKS)):
        low, high = block * BLOCK, (block + 1) * BLOCK
        kept = chances[block]
        fill_mask(bias, starts, low, high)

        def score(h, side, low=low, high=high):
            top = None
            for first in range(0, high, BLOCK):
                span = slice(first, first + BLOCK)
                made = (
                    nn(key_rows[h // GROUP, span, :], query[head_rows(h + g), low:high])
                    + bias[span, :]
                )
                scores[side, span, :] = made
                best = jnp.max(made.reshape(BLOCK // 8, 8, BLOCK), axis=0)
                top = best if top is None else jnp.maximum(top, best)
            return jnp.max(top, axis=0, keepdims=True)

        def blend(h, side, top, low=low, high=high, kept=kept):
            for first in range(0, high, BLOCK):
                span = slice(first, first + BLOCK)
                kept[h, span, :] = jnp.exp(scores[side, span, :] - top).astype(bf16)
            made = nn(value_aug[h // GROUP, :, :high], kept[h])
            scale = 1.0 / made[HD : HD + 1]
            mixed_t[head_rows(h + 1), low:high] = (made[:HD] * scale).astype(bf16)
            scales[pl.ds(h, 1), low:high] = scale

        def group(j, top, score=score, blend=blend):
            for member in range(GROUP):
                h = j * GROUP + member
                later = score(jnp.minimum(h + 1, HEADS - 1), (member + 1) % GROUP)
                blend(h, member, top)
                top = later
            return top

        lax.fori_loop(0, KEYS, group, score(0, 0))
        stores.append(copied(kept, chances_out[block], keep_sem.at[block]))
        stores[-1].start()
        for pair in range(QW // 128):
            side = pl.ds(pl.multiple_of((2 * pair + 1 - g) * HD, HD), 128)
            mixed[low:high, pair * 128 : pair * 128 + 128] = mixed_t[side, low:high].T
    last = [
        copied(mixed.at[here], o_own, out_sems.at[7]),
        copied(mixed.at[there], o_send, out_sems.at[8]),
        copied(mixed_t, o_out, out_sems.at[9]),
        copied(scales, scale_out, out_sems.at[10]),
    ]
    for store in last:
        store.start()
    for store in stores + last:
        store.wait()


def attend(adapter, tok_own, *rest):
    rows = tok_own.shape[0]
    length = 2 * rows
    shape = jax.ShapeDtypeStruct
    return pl.pallas_call(
        attend_kernel,
        out_shape=[
            shape((rows, QW), bf16),
            shape((rows, QW), bf16),
            shape((QW, length), bf16),
            shape((KW, length), bf16),
            shape((KW, length), bf16),
            shape(((HEADS + 2) * HD, length), bf16),
            shape((length, D), bf16),
            shape((3 * R, length), bf16),
            shape((R, length), f32),
            shape((HD // 2, length), f32),
            shape((HD // 2, length), f32),
        ]
        + [shape((HEADS, (block + 1) * BLOCK, BLOCK), bf16) for block in range(BLOCKS)],
        in_specs=[SMEM, HBM, ANY, HBM, ANY] + [HBM] * 3 + [VMEM] * 3,
        out_specs=[HBM] * (11 + BLOCKS),
        scratch_shapes=[
            pltpu.VMEM((HEADS, (block + 1) * BLOCK, BLOCK), bf16) for block in range(BLOCKS)
        ]
        + [
            pltpu.VMEM((length, D), bf16),
            pltpu.VMEM((length, AUG), bf16),
            pltpu.VMEM((AUG, SPAN), bf16),
            pltpu.VMEM((128, D), bf16),
            pltpu.VMEM((QW, length), bf16),
            pltpu.VMEM((KW, length), bf16),
            pltpu.VMEM((KW, length), bf16),
            pltpu.VMEM((KEYS, length, HD), bf16),
            pltpu.VMEM((KEYS, HD + R, length), bf16),
            pltpu.VMEM(((HEADS + 2) * HD, length), bf16),
            pltpu.VMEM((length, QW), bf16),
            pltpu.VMEM((GROUP, length, BLOCK), f32),
            pltpu.VMEM((length, BLOCK), f32),
            pltpu.VMEM((HD // 2, length), f32),
            pltpu.VMEM((HD // 2, length), f32),
            pltpu.VMEM((3 * R, length), bf16),
            pltpu.VMEM((R, length), f32),
            pltpu.SemaphoreType.DMA((5,)),
            pltpu.SemaphoreType.DMA((9,)),
            pltpu.SemaphoreType.DMA((11,)),
            pltpu.SemaphoreType.DMA((BLOCKS,)),
        ],
        compiler_params=pltpu.CompilerParams(vmem_limit_bytes=50 << 20),
        cost_estimate=pl.CostEstimate(
            flops=16 * 10**9, bytes_accessed=16 << 20, transcendentals=6 * 10**6
        ),
        name="attend",
    )(adapter, tok_own, *rest)


def normed_back(rows, gain_row, grad):
    scale = lax.rsqrt(jnp.mean(rows * rows, axis=-1, keepdims=True) + epsilon)
    scaled = grad * gain_row
    inside = jnp.mean(rows * scaled, axis=-1, keepdims=True)
    return scale * (scaled - rows * (scale * scale * inside))


def rounded_up(count, unit):
    return -(-count // unit) * unit


def feed_lanes(reps):
    return rounded_up((5 * D + 3 * FF) // reps, 256)


def qkv_lanes(reps):
    return rounded_up((4 * D + 2 * KV) // reps + 1, 128)


def packed(grads, reps, target):
    for rep in range(reps):
        at = 0
        for grad in grads:
            piece = grad.shape[-1] // reps
            share = grad[:, rep * piece : (rep + 1) * piece]
            target[rep * R : (rep + 1) * R, at : at + piece] = share.astype(target.dtype)
            at += piece


def feed_kernel(
    reps,
    adapter,
    o_own_in,
    o_oth_in,
    tok_in,
    cot_in,
    wo_own,
    wo_oth,
    wgu_own,
    wgu_oth,
    wd_own,
    wd_oth,
    a_down,
    lower_t,
    upper_width,
    upper_hidden,
    gains_own,
    gains_oth,
    layer_out,
    grad_middle,
    do_own_out,
    do_oth_out,
    pack_own_out,
    pack_send_out,
    o_own,
    o_oth,
    tok,
    cot,
    do_own,
    do_oth,
    wout,
    wg,
    wu,
    wd,
    at_out,
    at_gu,
    b_out,
    b_down,
    middle,
    normed,
    cot_aug,
    total,
    back,
    result,
    z_gu_t,
    dz_down_t,
    ga_out,
    pack,
    sems,
    o_sems,
    out_sems,
):
    g = lax.axis_index("grp")
    chosen = adapter[0]
    gain = gain_row(g, gains_own, gains_oth, 1)
    steps = FF // TILE
    each = steps // 2
    w_here = pl.ds(pl.multiple_of(g * HALF, 64), HALF)
    w_there = pl.ds(pl.multiple_of((1 - g) * HALF, 64), HALF)

    def column(step):
        owner = jnp.where(step < each, g, 1 - g)
        return owner * (FF // 2) + (step % each) * TILE

    def copies(step, slot):
        at = pl.multiple_of(column(step), TILE)
        gate_at = pl.ds(at, TILE)
        up_at = pl.ds(pl.multiple_of(FF + at, TILE), TILE)
        sem = lambda k: sems.at[slot, k]
        return [
            copied(wgu_own.at[:, gate_at], wg.at[slot, w_here], sem(0)),
            copied(wgu_oth.at[:, gate_at], wg.at[slot, w_there], sem(1)),
            copied(wgu_own.at[:, up_at], wu.at[slot, w_here], sem(2)),
            copied(wgu_oth.at[:, up_at], wu.at[slot, w_there], sem(3)),
            copied(upper_hidden.at[0, chosen, :, gate_at], wg.at[slot, pl.ds(D, R)], sem(4)),
            copied(upper_hidden.at[1, chosen, :, gate_at], wu.at[slot, pl.ds(D + R, R)], sem(5)),
            copied(a_down.at[gate_at], wd.at[slot, :, pl.ds(D, 128)], sem(6)),
        ]

    def down_copy(source, step, slot):
        local = pl.ds(pl.multiple_of((step % each) * TILE, TILE), TILE)
        return copied(source.at[local], wd.at[slot, :, pl.ds(0, D)], sems.at[slot, 7])

    def start(step, slot):
        for copy in copies(step, slot):
            copy.start()

        @pl.when(step < each)
        def _():
            down_copy(wd_own, step, slot).start()

        @pl.when(step >= each)
        def _():
            down_copy(wd_oth, step, slot).start()

    def wait(step, slot):
        for copy in copies(step, slot):
            copy.wait()
        down_copy(wd_own, step, slot).wait()

    for slot in range(2):
        wg[slot, D:, :] = jnp.zeros((128, TILE), bf16)
        wu[slot, D:, :] = jnp.zeros((128, TILE), bf16)
        at_out[slot] = jnp.zeros((128, QW), bf16)
        wout[slot, :HD, :D] = jnp.zeros((HD, D), bf16)
        wout[slot, HALF:, :D] = jnp.zeros((HD, D), bf16)
    for ref in (at_gu, b_out, b_down):
        ref[...] = jnp.zeros_like(ref)
    own_at = pl.multiple_of(g * 512, 128)
    oth_at = pl.multiple_of((1 - g) * 512, 128)
    loads = [
        copied(
            wo_own, wout.at[0, pl.ds(pl.multiple_of(g * HD, HD), HALF), pl.ds(0, D)], o_sems.at[0]
        ),
        copied(
            wo_oth,
            wout.at[1, pl.ds(pl.multiple_of((1 - g) * HD, HD), HALF), pl.ds(0, D)],
            o_sems.at[1],
        ),
        copied(lower_t.at[3, chosen, :, pl.ds(own_at, QW)], at_out.at[0, pl.ds(0, R)], o_sems.at[2]),
        copied(lower_t.at[3, chosen, :, pl.ds(oth_at, QW)], at_out.at[1, pl.ds(0, R)], o_sems.at[3]),
        copied(lower_t.at[4, chosen], at_gu.at[pl.ds(0, R)], o_sems.at[4]),
        copied(lower_t.at[5, chosen], at_gu.at[pl.ds(R, R)], o_sems.at[5]),
        copied(upper_width.at[1, chosen], b_out.at[pl.ds(0, R)], o_sems.at[6]),
        copied(upper_width.at[2, chosen], b_down.at[pl.ds(0, R)], o_sems.at[7]),
        copied(o_own_in, o_own, o_sems.at[8]),
        copied(o_oth_in, o_oth, o_sems.at[9]),
        copied(tok_in, tok, o_sems.at[10]),
        copied(cot_in, cot, o_sems.at[11]),
    ]
    first, second, third = loads[11:] + loads[2:4] + loads[7:8], loads[:2] + loads[8:10], loads[4:7] + loads[10:11]
    for load in first + second + third:
        load.start()
    pack[...] = jnp.zeros_like(pack)
    total[...] = jnp.zeros_like(total)
    back[...] = jnp.zeros_like(back)
    for load in first:
        load.wait()
    cot_aug[:, :D] = cot[...]
    dz_down = nt(cot[...], b_down[...])
    cot_aug[:, D:] = dz_down.astype(bf16)
    dz_down_t[...] = dz_down.T[:R, :].astype(bf16)
    for slot in range(2):
        wout[slot, :, D:] = at_out[slot].T
    for load in second + third:
        load.wait()
    start(0, 0)
    made = nn(o_own[...], wout[0]) + nn(o_oth[...], wout[1])
    inner_out = made[:, D:].astype(bf16)
    middle[...] = tok[...].astype(f32) + made[:, :D] + nn(inner_out, b_out[...])
    scale = lax.rsqrt(jnp.mean(middle[...] * middle[...], axis=-1, keepdims=True) + epsilon)
    normed[:, :D] = (middle[...] * scale * gain).astype(bf16)
    inner_gu = nt(normed[:, :D], at_gu[...])
    normed[:, D:] = inner_gu.astype(bf16)
    z_gu_t[...] = inner_gu.T[: 2 * R, :].astype(bf16)

    def step_body(step, carry):
        slot = step % 2

        @pl.when(step + 1 < steps)
        def _():
            start(step + 1, 1 - slot)

        wait(step, slot)
        gate = nn(normed[...], wg[slot])
        up = nn(normed[...], wu[slot])
        grad_active = nt(cot_aug[...], wd[slot])
        sigmoid = 1.0 / (1.0 + jnp.exp(-gate))
        silu = gate * sigmoid
        active = (silu * up).astype(bf16)
        grad_gate = (grad_active * up * (sigmoid * (1.0 + gate * (1.0 - sigmoid)))).astype(bf16)
        grad_up = (grad_active * silu).astype(bf16)
        total[...] += nn(active, wd[slot])
        back[...] += nt(grad_gate, wg[slot]) + nt(grad_up, wu[slot])
        shares = (
            nn(dz_down_t[...], active),
            nn(z_gu_t[...], grad_gate)[:R],
            nn(z_gu_t[...], grad_up)[R:],
        )
        piece = FF // reps
        base = column(step) // piece
        for index, share in enumerate(shares):
            at = 5 * (D // reps) + index * piece
            for rep in range(TILE // piece):
                target = pl.ds(pl.multiple_of((base + rep) * R, R), R)
                pack[target, at : at + piece] = share[:, rep * piece : (rep + 1) * piece].astype(bf16)
        return carry

    lax.fori_loop(0, steps, step_body, 0)

    inner_down = total[:, D:].astype(bf16)
    result[...] = (middle[...] + total[:, :D] + nn(inner_down, b_down[...])).astype(bf16)
    stores = [copied(result, layer_out, out_sems.at[0])]
    stores[0].start()
    gb_down = nn(total[:, D:].T[:R, :].astype(bf16), cot[...])
    dz_gu = back[:, D:].astype(bf16)
    grad_normed = back[:, :D] + nn(dz_gu, at_gu[...])
    grad = cot[...].astype(f32) + normed_back(middle[...], gain, grad_normed)
    total[:, :D] = grad
    stores.append(copied(total.at[:, pl.ds(0, D)], grad_middle, out_sems.at[1]))
    stores[1].start()
    branch = normed
    ga_gu = nn(back[:, D:].T[: 2 * R, :].astype(bf16), normed[:, :D])
    branch[:, :D] = grad.astype(bf16)
    dz_out = nt(branch[:, :D], b_out[...])
    branch[:, D:] = dz_out.astype(bf16)
    dz_out_t = dz_out.T[:R, :].astype(bf16)
    do_oth[...] = nt(wout[1], branch[...]).astype(bf16)
    stores.append(copied(do_oth, do_oth_out, out_sems.at[2]))
    stores[-1].start()
    do_own[...] = nt(wout[0], branch[...]).astype(bf16)
    stores.append(copied(do_own, do_own_out, out_sems.at[3]))
    stores[-1].start()
    gb_out = nn(inner_out.astype(f32).T[:R, :].astype(bf16), branch[:, :D])
    ga_out[...] = jnp.zeros_like(ga_out)
    ga_out[:, pl.ds(own_at, QW)] += nn(dz_out_t, o_own[...])
    ga_out[:, pl.ds(oth_at, QW)] += nn(dz_out_t, o_oth[...])
    packed([ga_out[...], ga_gu[:R], ga_gu[R:], gb_out, gb_down], reps, pack)
    half = pack.shape[1] // 2
    for index, (side, target) in enumerate(((g, pack_own_out), (1 - g, pack_send_out))):
        source = pack.at[:, pl.ds(pl.multiple_of(side * half, 128), half)]
        stores.append(copied(source, target, out_sems.at[4 + index]))
        stores[-1].start()
    for store in stores:
        store.wait()


def feed(reps, *args):
    rows = args[3].shape[0]
    half = feed_lanes(reps) // 2
    shape = jax.ShapeDtypeStruct
    return pl.pallas_call(
        functools.partial(feed_kernel, reps),
        out_shape=[
            shape((rows, D), bf16),
            shape((rows, D), f32),
            shape((QW, rows), bf16),
            shape((QW, rows), bf16),
            shape((reps * R, half), bf16),
            shape((reps * R, half), bf16),
        ],
        in_specs=[SMEM, HBM, ANY] + [HBM] * 12 + [VMEM] * 2,
        out_specs=[HBM] * 6,
        scratch_shapes=[
            pltpu.VMEM((rows, QW), bf16),
            pltpu.VMEM((rows, QW), bf16),
            pltpu.VMEM((rows, D), bf16),
            pltpu.VMEM((rows, D), bf16),
            pltpu.VMEM((QW, rows), bf16),
            pltpu.VMEM((QW, rows), bf16),
            pltpu.VMEM((2, QW, AUG), bf16),
            pltpu.VMEM((2, AUG, TILE), bf16),
            pltpu.VMEM((2, AUG, TILE), bf16),
            pltpu.VMEM((2, TILE, AUG), bf16),
            pltpu.VMEM((2, 128, QW), bf16),
            pltpu.VMEM((128, D), bf16),
            pltpu.VMEM((128, D), bf16),
            pltpu.VMEM((128, D), bf16),
            pltpu.VMEM((rows, D), f32),
            pltpu.VMEM((rows, AUG), bf16),
            pltpu.VMEM((rows, AUG), bf16),
            pltpu.VMEM((rows, AUG), f32),
            pltpu.VMEM((rows, AUG), f32),
            pltpu.VMEM((rows, D), bf16),
            pltpu.VMEM((2 * R, rows), bf16),
            pltpu.VMEM((R, rows), bf16),
            pltpu.VMEM((R, D), f32),
            pltpu.VMEM((reps * R, 2 * half), bf16),
            pltpu.SemaphoreType.DMA((2, 8)),
            pltpu.SemaphoreType.DMA((12,)),
            pltpu.SemaphoreType.DMA((6,)),
        ],
        compiler_params=pltpu.CompilerParams(vmem_limit_bytes=44 << 20),
        cost_estimate=pl.CostEstimate(
            flops=30 * 10**9, bytes_accessed=36 << 20, transcendentals=2 * 10**6
        ),
        name="feed",
    )(*args)


def attend_back_kernel(
    reps,
    adapter,
    do_own,
    do_oth,
    o_in,
    normed,
    upper_width,
    upper_keys,
    query_in,
    k_in,
    v_in,
    zt_in,
    scale_in,
    cos_in,
    sin_in,
    pack_own_in,
    pack_oth_in,
    *refs,
):
    attend_back_body(
        reps,
        adapter,
        do_own,
        do_oth,
        o_in,
        normed,
        upper_width,
        upper_keys,
        query_in,
        k_in,
        v_in,
        zt_in,
        scale_in,
        cos_in,
        sin_in,
        pack_own_in,
        pack_oth_in,
        refs[:BLOCKS],
        refs[BLOCKS + 3 : 2 * BLOCKS + 3],
        *refs[BLOCKS : BLOCKS + 3],
        *refs[2 * BLOCKS + 3 :],
    )


def attend_back_body(
    reps,
    adapter,
    do_own,
    do_oth,
    o_in,
    normed,
    upper_width,
    upper_keys,
    query_in,
    k_in,
    v_in,
    zt_in,
    scale_in,
    cos_in,
    sin_in,
    pack_own_in,
    pack_oth_in,
    chances_in,
    chances,
    dy_out,
    part_out,
    exchange_out,
    query,
    key_t,
    value_t,
    zt,
    scales,
    cosine,
    sine,
    pack_own,
    pack_oth,
    exchange,
    grad_o,
    mixed_t,
    n_rows,
    weight,
    value_rows,
    delta,
    dq,
    dk,
    dv,
    dy_t,
    dy,
    grad_scores,
    gb_q,
    gb_kv,
    pack,
    sems,
    b_sems,
    out_sem,
    keep_sem,
):
    g = lax.axis_index("grp")
    chosen = adapter[0]
    length = query.shape[1]
    rows = length // 2
    here = pl.ds(pl.multiple_of(g * rows, 128), rows)
    there = pl.ds(pl.multiple_of((1 - g) * rows, 128), rows)
    weight[...] = jnp.zeros_like(weight)
    early = [
        copied(k_in, key_t, sems.at[0]),
        copied(v_in, value_t, sems.at[1]),
    ]
    loads = [
        copied(do_own, grad_o.at[:, here], sems.at[2]),
        copied(do_oth, grad_o.at[:, there], sems.at[3]),
        copied(o_in, mixed_t, sems.at[4]),
        copied(query_in, query, sems.at[5]),
        copied(scale_in, scales, sems.at[6]),
    ]
    late = [
        copied(cos_in, cosine, sems.at[7]),
        copied(sin_in, sine, sems.at[8]),
        copied(normed, n_rows, sems.at[9]),
        copied(zt_in, zt, sems.at[10]),
        copied(pack_own_in, pack_own, sems.at[11]),
        copied(pack_oth_in, pack_oth, sems.at[12]),
    ] + upper_loads(g, chosen, upper_width, upper_keys, weight, 0, b_sems)
    kept = [
        copied(chances_in[block], chances[block], keep_sem.at[block]) for block in range(BLOCKS)
    ]
    for load in early + loads:
        load.start()
    kept[0].start()
    dk[...] = jnp.zeros_like(dk)
    dv[...] = jnp.zeros_like(dv)
    dy_t[...] = jnp.zeros_like(dy_t)
    for load in early:
        load.wait()
    for j in range(KEYS):
        value_rows[j] = value_t[head_rows(j + g), :].T
    for load in loads:
        load.wait()
    for load in kept[1:] + late:
        load.start()
    for h in range(HEADS):
        scaled = grad_o[head_rows(h + g), :].astype(f32) * scales[h : h + 1, :]
        product = scaled * mixed_t[(h + 1) * HD : (h + 2) * HD, :].astype(f32)
        delta[h : h + 1, :] = jnp.sum(product, axis=0, keepdims=True)
        grad_o[head_rows(h + g), :] = scaled.astype(bf16)

    for block in range(length // BLOCK):
        low, high = block * BLOCK, (block + 1) * BLOCK
        found = chances[block]
        kept[block].wait()

        def score(h, side, low=low, high=high, found=found):
            deltas = delta[pl.ds(h, 1), low:high]
            for first in range(0, high, BLOCK):
                span = slice(first, first + BLOCK)
                grad = nn(value_rows[h // GROUP, span, :], grad_o[head_rows(h + g), low:high])
                chance = found[h, span, :].astype(f32)
                grad_scores[side, span, :] = (chance * (grad - deltas)).astype(bf16)

        def spread(h, side, low=low, high=high, found=found):
            dq[h, :, low:high] = nn(
                key_t[head_rows(h // GROUP + g), :high], grad_scores[side, :high, :]
            )
            return (
                nt(grad_o[head_rows(h + g), low:high], found[h]),
                nt(query[head_rows(h + g), low:high], grad_scores[side, :high, :]),
            )

        def group(j, carry, high=high, score=score, spread=spread):
            sums = []
            for member in range(GROUP):
                h = j * GROUP + member
                score(jnp.minimum(h + 1, HEADS - 1), (member + 1) % GROUP)
                sums.append(spread(h, member))
            dv[j, :, :high] += sums[0][0] + sums[1][0] + sums[2][0]
            dk[j, :, :high] += sums[0][1] + sums[1][1] + sums[2][1]
            return carry

        score(0, 0)
        lax.fori_loop(0, KEYS, group, 0)

    for load in late:
        load.wait()
    back_sine = -sine[...]
    for h in range(HEADS):
        dy_t[(h + 1) * HD : (h + 2) * HD, :] = (
            turned(dq[h], cosine[...], back_sine) * HD**-0.5
        ).astype(bf16)
    key_base = (HEADS + 2) * HD
    value_base = key_base + (KEYS + 2) * HD
    for j in range(KEYS):
        at = key_base + (j + 1) * HD
        dy_t[at : at + HD, :] = turned(dk[j], cosine[...], back_sine).astype(bf16)
        at = value_base + (j + 1) * HD
        dy_t[at : at + HD, :] = dv[j].astype(bf16)
    for base, count, to in ((0, QW, 0), (key_base, KW, QW), (value_base, KW, QW + KW)):
        for at in range(0, count, 128):
            side = pl.ds(pl.multiple_of(base + at + (1 - g) * HD, HD), 128)
            dy[:, to + at : to + at + 128] = dy_t[side, :].T
    inner = nt(dy[:, :SPAN], weight[...])
    dy[:, SPAN:] = inner.astype(bf16)
    dy_stores = [
        copied(dy.at[place], target, out_sem.at[index])
        for place, target, index in ((there, part_out, 0), (here, dy_out, 1))
    ]
    for copy in dy_stores:
        copy.start()
    gb = nn(zt[...], dy[:, :SPAN])
    gb_q[...] = jnp.zeros_like(gb_q)
    gb_kv[...] = jnp.zeros_like(gb_kv)
    gb_q[:, pl.ds(pl.multiple_of(g * 512, 128), QW)] = gb[:R, :QW]
    for index in range(2):
        gb_kv[index, :, pl.ds(pl.multiple_of(g * 128, 128), KW)] = gb[
            (index + 1) * R : (index + 2) * R, QW + index * KW : QW + (index + 1) * KW
        ]
    ga = nn(inner.T[: 3 * R, :].astype(bf16), n_rows[...])
    pack[...] = jnp.zeros_like(pack)
    packed(
        [ga[:R], ga[R : 2 * R], ga[2 * R :], gb_q[...], gb_kv[0], gb_kv[1]],
        reps,
        pack,
    )
    half = pack_own.shape[1]
    width = pack.shape[1]
    exchange[:, :half] = (pack_own[...].astype(f32) + pack_oth[...].astype(f32)).astype(bf16)
    exchange[:, half:] = jnp.where(
        lanes(pack.shape) == width - 1, chosen.astype(f32), pack[...].astype(f32)
    ).astype(bf16)
    last = copied(exchange, exchange_out, out_sem.at[2])
    last.start()
    for copy in (*dy_stores, last):
        copy.wait()


def attend_back(reps, *args):
    rows = args[1].shape[1]
    length = 2 * rows
    half = feed_lanes(reps) // 2
    width = qkv_lanes(reps)
    shape = jax.ShapeDtypeStruct
    return pl.pallas_call(
        functools.partial(attend_back_kernel, reps),
        out_shape=[
            shape((rows, AUG), bf16),
            shape((rows, AUG), bf16),
            shape((reps * R, half + width), bf16),
        ],
        in_specs=[SMEM, HBM, ANY] + [HBM] * 12 + [ANY] + [HBM] * BLOCKS,
        out_specs=[HBM] * 3,
        scratch_shapes=[
            pltpu.VMEM((HEADS, (block + 1) * BLOCK, BLOCK), bf16) for block in range(BLOCKS)
        ]
        + [
            pltpu.VMEM((QW, length), bf16),
            pltpu.VMEM((KW, length), bf16),
            pltpu.VMEM((KW, length), bf16),
            pltpu.VMEM((3 * R, length), bf16),
            pltpu.VMEM((R, length), f32),
            pltpu.VMEM((HD // 2, length), f32),
            pltpu.VMEM((HD // 2, length), f32),
            pltpu.VMEM((reps * R, half), bf16),
            pltpu.VMEM((reps * R, half), bf16),
            pltpu.VMEM((reps * R, half + width), bf16),
            pltpu.VMEM((QW, length), bf16),
            pltpu.VMEM(((HEADS + 2) * HD, length), bf16),
            pltpu.VMEM((length, D), bf16),
            pltpu.VMEM((128, SPAN), bf16),
            pltpu.VMEM((KEYS, length, HD), bf16),
            pltpu.VMEM((R, length), f32),
            pltpu.VMEM((HEADS, HD, length), f32),
            pltpu.VMEM((KEYS, HD, length), f32),
            pltpu.VMEM((KEYS, HD, length), f32),
            pltpu.VMEM(((HEADS + 2 * KEYS + 6) * HD, length), bf16),
            pltpu.VMEM((length, AUG), bf16),
            pltpu.VMEM((GROUP, length, BLOCK), bf16),
            pltpu.VMEM((R, D), f32),
            pltpu.VMEM((2, R, KV), f32),
            pltpu.VMEM((reps * R, width), bf16),
            pltpu.SemaphoreType.DMA((16,)),
            pltpu.SemaphoreType.DMA((9,)),
            pltpu.SemaphoreType.DMA((4,)),
            pltpu.SemaphoreType.DMA((BLOCKS,)),
        ],
        compiler_params=pltpu.CompilerParams(vmem_limit_bytes=50 << 20),
        cost_estimate=pl.CostEstimate(
            flops=24 * 10**9, bytes_accessed=20 << 20, transcendentals=6 * 10**6
        ),
        name="attend_back",
    )(*args)


def finish_kernel(
    adapter,
    dy_in,
    qkv_own,
    qkv_oth,
    lower_t,
    tok_in,
    gains_own,
    gains_oth,
    part_in,
    middle_in,
    out,
    dy,
    part,
    tok,
    grad_middle,
    weight,
    weight_oth,
    maps,
    result,
    sems,
    w_sems,
    out_sem,
):
    g = lax.axis_index("grp")
    chosen = adapter[0]
    maps[...] = jnp.zeros_like(maps)
    loads = qkv_loads(g, g, qkv_own, qkv_oth, weight, w_sems.at[0])
    loads += qkv_loads(g, 1 - g, qkv_own, qkv_oth, weight_oth, w_sems.at[1])
    for index, (source, target) in enumerate(
        ((dy_in, dy), (part_in, part), (tok_in, tok), (middle_in, grad_middle))
    ):
        loads.append(copied(source, target, sems.at[index]))
    for index in range(3):
        loads.append(
            copied(lower_t.at[index, chosen], maps.at[pl.ds(index * R, R)], sems.at[5 + index])
        )
    for load in loads:
        load.start()
    gain = gain_row(g, gains_own, gains_oth, 0)
    for load in loads:
        load.wait()

    def half(index, carry):
        count = tok.shape[0] // 2
        span = pl.ds(pl.multiple_of(index * count, 128), count)
        inner = dy[span, SPAN:].astype(f32) + part[span, SPAN:].astype(f32)
        grad = (
            nt(dy[span, :SPAN], weight[...])
            + nt(part[span, :SPAN], weight_oth[...])
            + nn(inner.astype(bf16), maps[...])
        )
        result[span, :] = (
            grad_middle[span, :] + normed_back(tok[span, :].astype(f32), gain, grad)
        ).astype(bf16)
        return carry

    lax.fori_loop(0, 2, half, 0)
    store = copied(result, out, out_sem.at[0])
    store.start()
    store.wait()


def finish(*args):
    rows = args[1].shape[0]
    return pl.pallas_call(
        finish_kernel,
        out_shape=jax.ShapeDtypeStruct((rows, D), bf16),
        in_specs=[SMEM] + [HBM] * 5 + [VMEM] * 2 + [ANY, HBM],
        out_specs=HBM,
        scratch_shapes=[
            pltpu.VMEM((rows, AUG), bf16),
            pltpu.VMEM((rows, AUG), bf16),
            pltpu.VMEM((rows, D), bf16),
            pltpu.VMEM((rows, D), f32),
            pltpu.VMEM((D, SPAN), bf16),
            pltpu.VMEM((D, SPAN), bf16),
            pltpu.VMEM((128, D), bf16),
            pltpu.VMEM((rows, D), bf16),
            pltpu.SemaphoreType.DMA((8,)),
            pltpu.SemaphoreType.DMA((2, 6)),
            pltpu.SemaphoreType.DMA((1,)),
        ],
        compiler_params=pltpu.CompilerParams(vmem_limit_bytes=50 << 20),
        cost_estimate=pl.CostEstimate(
            flops=4 * 10**9, bytes_accessed=10 << 20, transcendentals=0
        ),
        name="finish",
    )(*args)


def collect_kernel(source, keep, send, received, sem):
    load = copied(source, received, sem.at[0])
    load.start()
    load.wait()
    g = lax.axis_index("grp")
    count, width = received.shape
    quota = NAD // 2
    label = received[:, width - 1 :].astype(f32)
    lane = lanes((count, NAD * R))
    row = lax.broadcasted_iota(jnp.int32, (count, NAD * R), 0)
    picks = ((lane // R).astype(f32) == label) & (lane % R == row % R)
    sums = tn(picks.astype(f32).astype(bf16), received[...])
    first = g == 0
    for adapter in range(quota):
        low = sums[adapter * R : (adapter + 1) * R]
        high = sums[(quota + adapter) * R : (quota + adapter + 1) * R]
        keep[adapter] = jnp.where(first, low, high)
        send[adapter] = jnp.where(first, high, low)


def collect(received):
    shape = jax.ShapeDtypeStruct((NAD // 2, R, received.shape[1]), f32)
    return pl.pallas_call(
        collect_kernel,
        out_shape=[shape, shape],
        in_specs=[ANY],
        out_specs=[VMEM] * 2,
        scratch_shapes=[
            pltpu.VMEM(received.shape, bf16),
            pltpu.SemaphoreType.DMA((1,)),
        ],
        compiler_params=pltpu.CompilerParams(vmem_limit_bytes=8 << 20),
        cost_estimate=pl.CostEstimate(flops=10**8, bytes_accessed=2 << 20, transcendentals=0),
        name="collect",
    )(received)


def deliver_kernel(reps, keep, other, lower, down, width, keys, hidden, feeds, qkvs):
    g = lax.axis_index("grp")
    half = feeds.shape[-1] // 2
    feeds[:, :, pl.ds(pl.multiple_of(g * half, 128), half)] = keep[:, :, :half]
    feeds[:, :, pl.ds(pl.multiple_of((1 - g) * half, 128), half)] = other[:, :, :half]
    qkvs[...] = keep[:, :, half:] + other[:, :, half:]
    piece, tall, short = D // reps, FF // reps, KV // reps
    for index in range(3):
        lower[index] = qkvs[:, :, index * piece : (index + 1) * piece]
        lower[3 + index] = feeds[:, :, index * piece : (index + 1) * piece]
    width[0] = qkvs[:, :, 3 * piece : 4 * piece]
    width[1] = feeds[:, :, 3 * piece : 4 * piece]
    width[2] = feeds[:, :, 4 * piece : 5 * piece]
    for index in range(2):
        at = 4 * piece + index * short
        keys[index] = qkvs[:, :, at : at + short]
        at = 5 * piece + (1 + index) * tall
        hidden[index] = feeds[:, :, at : at + tall]
    down[...] = feeds[:, :, 5 * piece : 5 * piece + tall]


def deliver(reps, keep, other):
    quota = NAD // 2
    shape = lambda *dims: jax.ShapeDtypeStruct(dims, f32)
    return pl.pallas_call(
        functools.partial(deliver_kernel, reps),
        out_shape=[
            shape(6, quota, R, D // reps),
            shape(quota, R, FF // reps),
            shape(3, quota, R, D // reps),
            shape(2, quota, R, KV // reps),
            shape(2, quota, R, FF // reps),
        ],
        in_specs=[VMEM] * 2,
        out_specs=[VMEM] * 5,
        scratch_shapes=[
            pltpu.VMEM((quota, R, feed_lanes(reps)), f32),
            pltpu.VMEM((quota, R, qkv_lanes(reps)), f32),
        ],
        compiler_params=pltpu.CompilerParams(vmem_limit_bytes=8 << 20),
        cost_estimate=pl.CostEstimate(flops=10**6, bytes_accessed=1 << 20, transcendentals=0),
        name="deliver",
    )(keep, other)


def per_device(
    tokens,
    cotangent,
    segment_ids,
    adapter_ids,
    norm_gains,
    frozen_qkv,
    frozen_out,
    frozen_gate_up,
    frozen_down,
    lower_mats,
    lower_down,
    upper_width,
    upper_keys,
    upper_hidden,
):
    reps = lax.axis_size("rep")
    chosen = adapter_ids[0]
    first = lax.axis_index("grp") == 0
    swap = lambda value: lax.ppermute(value, "grp", SWAP)

    tok_own = tokens[0]
    tok_oth = swap(tok_own)
    qkv_oth = swap(frozen_qkv)
    gains_oth = swap(norm_gains)
    a_down = jnp.pad(
        lax.dynamic_index_in_dim(lower_down, chosen, 0, keepdims=False), ((0, 0), (0, 128 - R))
    )
    tok_oth, qkv_oth, gains_oth, a_down, wo, wgu, wd = lax.optimization_barrier(
        (tok_oth, qkv_oth, gains_oth, a_down, frozen_out, frozen_gate_up, frozen_down)
    )
    wo_oth = swap(wo)
    wgu_oth = swap(wgu)
    wd_oth = swap(wd)

    lower_t = lower_mats.transpose(0, 1, 3, 2)
    gains = (norm_gains, gains_oth)

    (o_own, o_send, query, key_t, value_t, mixed_t, normed, zt, scales, cosine, sine, *chances) = (
        attend(
            adapter_ids,
            tok_own,
            tok_oth,
            frozen_qkv,
            qkv_oth,
            lower_t,
            upper_width,
            upper_keys,
            *gains,
            segment_ids,
        )
    )
    o_oth = swap(o_send)
    layer_out, grad_middle, do_own, do_send, pack_own, pack_send = feed(
        reps,
        adapter_ids,
        o_own,
        o_oth,
        tok_own,
        cotangent[0],
        frozen_out,
        wo_oth,
        frozen_gate_up,
        wgu_oth,
        frozen_down,
        wd_oth,
        a_down,
        lower_t,
        upper_width,
        upper_hidden,
        *gains,
    )
    do_oth = swap(do_send)
    pack_oth = swap(pack_send)
    dy, dy_send, exchange = attend_back(
        reps,
        adapter_ids,
        do_own,
        do_oth,
        mixed_t,
        normed,
        upper_width,
        upper_keys,
        query,
        key_t,
        value_t,
        zt,
        scales,
        cosine,
        sine,
        pack_own,
        pack_oth,
        *chances,
    )
    received = lax.all_to_all(exchange, "rep", 0, 0, tiled=True)
    input_grad = finish(
        adapter_ids,
        dy,
        frozen_qkv,
        qkv_oth,
        lower_t,
        tok_own,
        *gains,
        swap(dy_send),
        grad_middle,
    )
    received, input_grad = lax.optimization_barrier((received, input_grad))
    keep, send = collect(received)
    lower, down, width, keys, hidden = deliver(reps, keep, swap(send))
    return (
        layer_out[None],
        input_grad[None],
        lower.transpose(0, 1, 3, 2),
        down.transpose(0, 2, 1),
        width,
        keys,
        hidden,
    )


def solution(mesh):
    return jax.shard_map(
        per_device,
        mesh=mesh,
        in_specs=(
            P("rep", "grp", None),
            P("rep", "grp", None),
            P("rep", None),
            P("rep"),
            P(None, "grp"),
            P("grp", None),
            P("grp", None),
            P("grp", None),
            P("grp", None),
            P(),
            P(),
            P(),
            P(),
            P(),
        ),
        out_specs=(
            P("rep", "grp", None),
            P("rep", "grp", None),
            P(None, "grp", "rep", None),
            P("grp", "rep", None),
            P(None, "grp", None, "rep"),
            P(None, "grp", None, "rep"),
            P(None, "grp", None, "rep"),
        ),
        check_vma=False,
    )
```

```python
import functools

import jax
import jax.numpy as jnp
import numpy as np
from jax import lax
from jax.experimental import pallas as pl
from jax.experimental.pallas import tpu as pltpu
from jax.sharding import PartitionSpec as P

D = 1152
H = 18
KVH = 6
HD = 64
FF = 3072
R = 16
NAD = 8
KV = 384

HALF = D // 2
HEADS = H // 2
GROUP = H // KVH
QW = 640
KW = 256
SPAN = QW + 2 * KW
AUG = D + 128
TILE = 768
BLOCK = 256
BLOCKS = 1024 // BLOCK
DOCS = 4
KEYS = HEADS // GROUP
VMEM_BYTES = 61900 * 1024

epsilon = 1e-05
theta_base = 10000.0
masked_value = -1e30
f32 = jnp.float32
bf16 = jnp.bfloat16
SWAP = [(0, 1), (1, 0)]

HBM = pl.BlockSpec(memory_space=pltpu.MemorySpace.HBM)
ANY = pl.BlockSpec(memory_space=pl.ANY)
VMEM = pl.BlockSpec(memory_space=pltpu.VMEM)
SMEM = pl.BlockSpec(memory_space=pltpu.SMEM)


def nn(left, right):
    return jnp.dot(left, right, preferred_element_type=f32)


def nt(left, right):
    return lax.dot_general(left, right, (((1,), (1,)), ((), ())), preferred_element_type=f32)


def tn(left, right):
    return lax.dot_general(left, right, (((0,), (0,)), ((), ())), preferred_element_type=f32)


def lanes(shape):
    return lax.broadcasted_iota(jnp.int32, shape, len(shape) - 1)


def gain_row(g, own, other, row):
    mine = own[row : row + 1, :].astype(f32)
    theirs = other[row : row + 1, :].astype(f32)
    return jnp.where(
        g == 0,
        jnp.concatenate([mine, theirs], axis=1),
        jnp.concatenate([theirs, mine], axis=1),
    )


def copied(source, target, sem):
    return pltpu.make_async_copy(source, target, sem)


def doc_starts(segments):
    return [
        jnp.sum(jnp.where(segments < doc, 1.0, 0.0), axis=-1, keepdims=True)
        for doc in range(1, DOCS)
    ]


def start_at(place, starts):
    found = jnp.zeros_like(place)
    for start in starts:
        found = jnp.where(place >= start, start, found)
    return found


def fill_angles(starts, cosine, sine):
    def both(angle):
        return jnp.cos(angle), jnp.sin(angle)

    powers = np.float32(theta_base) ** (-np.arange(HD // 2, dtype=np.float32) * 2.0 / HD)
    row = lax.broadcasted_iota(jnp.int32, (HD // 2, 128), 0)
    freqs = jnp.zeros(row.shape, f32)
    for index, power in enumerate(powers):
        freqs = jnp.where(row == index, np.float32(power), freqs)

    fine_cos, fine_sin = both(lanes(freqs.shape).astype(f32) * freqs)
    docs = [both(start * freqs) for start in starts]
    for at in range(0, cosine.shape[1], 128):
        wide_cos, wide_sin = both(float(at) * freqs)
        cos_p = wide_cos * fine_cos - wide_sin * fine_sin
        sin_p = wide_sin * fine_cos + wide_cos * fine_sin
        place = (lanes(freqs.shape) + at).astype(f32)
        cos_d, sin_d = jnp.ones_like(cos_p), jnp.zeros_like(cos_p)
        for start, (cos_s, sin_s) in zip(starts, docs):
            inside = place >= start
            cos_d = jnp.where(inside, cos_s, cos_d)
            sin_d = jnp.where(inside, sin_s, sin_d)
        cosine[:, at : at + 128] = cos_p * cos_d + sin_p * sin_d
        sine[:, at : at + 128] = sin_p * cos_d - cos_p * sin_d


def turned(block, cosine, sine):
    first, second = block[: HD // 2], block[HD // 2 :]
    return jnp.concatenate(
        [first * cosine - second * sine, second * cosine + first * sine], axis=0
    )


def head_rows(slot):
    return pl.ds(pl.multiple_of(slot * HD, HD), HD)


def fill_mask(bias, starts, low, high):
    place = lanes((1, BLOCK)).astype(f32) + low
    begin = start_at(place, starts)
    for first in range(0, high, BLOCK):
        key_place = lax.broadcasted_iota(jnp.int32, (BLOCK, BLOCK), 0).astype(f32) + first
        allowed = key_place >= begin
        if first == low:
            allowed = allowed & (key_place <= place)
        bias[first : first + BLOCK, :] = jnp.where(allowed, 0.0, masked_value)


def qkv_loads(g, side, own, oth, weight, sems):
    w_here = pl.ds(pl.multiple_of(g * HALF, 64), HALF)
    w_there = pl.ds(pl.multiple_of((1 - g) * HALF, 64), HALF)
    windows = (
        (pl.multiple_of(side * 512, 128), QW, 0),
        (pl.multiple_of(D + side * 128, 128), KW, QW),
        (pl.multiple_of(D + KV + side * 128, 128), KW, QW + KW),
    )
    loads = []
    for index, (at, width, to) in enumerate(windows):
        for part, (source, rows) in enumerate(((own, w_here), (oth, w_there))):
            loads.append(
                copied(
                    source.at[:, pl.ds(at, width)],
                    weight.at[rows, pl.ds(to, width)],
                    sems.at[2 * index + part],
                )
            )
    return loads


def upper_loads(g, chosen, upper_width, upper_keys, weight, base, sems):
    loads = []
    loads.append(
        copied(
            upper_width.at[0, chosen, :, pl.ds(pl.multiple_of(g * 512, 128), QW)],
            weight.at[pl.ds(base, R), pl.ds(0, QW)],
            sems.at[6],
        )
    )
    for index in range(2):
        loads.append(
            copied(
                upper_keys.at[index, chosen, :, pl.ds(pl.multiple_of(g * 128, 128), KW)],
                weight.at[pl.ds(base + (index + 1) * R, R), pl.ds(QW + index * KW, KW)],
                sems.at[7 + index],
            )
        )
    return loads


def attend_kernel(
    adapter,
    tok_own,
    tok_oth,
    qkv_own,
    qkv_oth,
    lower_t,
    upper_width,
    upper_keys,
    gains_own,
    gains_oth,
    segments,
    o_own,
    o_send,
    q_out,
    k_out,
    v_out,
    o_out,
    n_out,
    zt_out,
    scale_out,
    cos_out,
    sin_out,
    *refs,
):
    attend_body(
        adapter,
        tok_own,
        tok_oth,
        qkv_own,
        qkv_oth,
        lower_t,
        upper_width,
        upper_keys,
        gains_own,
        gains_oth,
        segments,
        o_own,
        o_send,
        q_out,
        k_out,
        v_out,
        o_out,
        n_out,
        zt_out,
        scale_out,
        cos_out,
        sin_out,
        refs[:BLOCKS],
        refs[BLOCKS : 2 * BLOCKS],
        *refs[2 * BLOCKS :],
    )


def attend_body(
    adapter,
    tok_own,
    tok_oth,
    qkv_own,
    qkv_oth,
    lower_t,
    upper_width,
    upper_keys,
    gains_own,
    gains_oth,
    segments,
    o_own,
    o_send,
    q_out,
    k_out,
    v_out,
    o_out,
    n_out,
    zt_out,
    scale_out,
    cos_out,
    sin_out,
    chances_out,
    chances,
    tok,
    normed,
    weight,
    maps,
    query,
    key_t,
    value_t,
    key_rows,
    value_aug,
    mixed_t,
    mixed,
    scores,
    bias,
    cosine,
    sine,
    inner_t,
    scales,
    sems,
    w_sems,
    out_sems,
    keep_sem,
):
    g = lax.axis_index("grp")
    chosen = adapter[0]
    rows = tok_own.shape[0]
    here = pl.ds(pl.multiple_of(g * rows, 128), rows)
    there = pl.ds(pl.multiple_of((1 - g) * rows, 128), rows)
    maps[...] = jnp.zeros_like(maps)
    weight[D:, :] = jnp.zeros((128, SPAN), bf16)
    loads = [
        copied(tok_own, tok.at[here], sems.at[0]),
        copied(tok_oth, tok.at[there], sems.at[1]),
    ] + [
        copied(lower_t.at[index, chosen], maps.at[pl.ds(index * R, R)], sems.at[2 + index])
        for index in range(3)
    ]
    w_loads = qkv_loads(g, g, qkv_own, qkv_oth, weight, w_sems)
    w_loads += upper_loads(g, chosen, upper_width, upper_keys, weight, D, w_sems)
    for load in loads:
        load.start()
    starts = doc_starts(segments[...])
    fill_angles(starts, cosine, sine)
    gain = gain_row(g, gains_own, gains_oth, 0)
    for load in loads:
        load.wait()
    for load in w_loads:
        load.start()

    def norm_part(part, carry):
        span = pl.ds(pl.multiple_of(part * rows, 128), rows)
        wide = tok[span, :].astype(f32)
        scale = lax.rsqrt(jnp.mean(wide * wide, axis=-1, keepdims=True) + epsilon)
        normed[span, :D] = (wide * scale * gain).astype(bf16)
        inner = nt(normed[span, :D], maps[...])
        normed[span, D:] = inner.astype(bf16)
        inner_t[:, span] = inner.T[: 3 * R, :].astype(bf16)
        return carry

    lax.fori_loop(0, 2, norm_part, 0)
    for load in w_loads:
        load.wait()

    def project(part, carry):
        span = pl.ds(pl.multiple_of(part * rows, 128), rows)
        cos_cols = cosine[:, span]
        sin_cols = sine[:, span]
        for target, base, count, turn, scale in (
            (query, 0, QW, True, HD**-0.5),
            (key_t, QW, KW, True, 1.0),
            (value_t, QW + KW, KW, False, 1.0),
        ):
            for at in range(0, count, 256):
                width = min(256, count - at)
                made = nn(normed[span, :], weight[:, base + at : base + at + width]).T
                for to in range(0, width, HD):
                    block = made[to : to + HD]
                    if turn:
                        block = turned(block, cos_cols, sin_cols) * scale
                    target[at + to : at + to + HD, span] = block.astype(bf16)
        return carry

    lax.fori_loop(0, 2, project, 0)
    stores = [
        copied(query, q_out, out_sems.at[0]),
        copied(key_t, k_out, out_sems.at[1]),
        copied(value_t, v_out, out_sems.at[2]),
        copied(normed.at[:, pl.ds(0, D)], n_out, out_sems.at[3]),
        copied(cosine, cos_out, out_sems.at[4]),
        copied(sine, sin_out, out_sems.at[5]),
        copied(inner_t, zt_out, out_sems.at[6]),
    ]
    for store in stores:
        store.start()
    for j in range(KEYS):
        key_rows[j] = key_t[head_rows(j + g), :].T
        value_aug[j, :HD, :] = value_t[head_rows(j + g), :]
        value_aug[j, HD:, :] = jnp.ones((R, 2 * rows), bf16)
    mixed_t[:HD, :] = jnp.zeros((HD, 2 * rows), bf16)
    mixed_t[(HEADS + 1) * HD :, :] = jnp.zeros((HD, 2 * rows), bf16)

    for block in reversed(range(BLOCKS)):
        low, high = block * BLOCK, (block + 1) * BLOCK
        kept = chances[block]
        fill_mask(bias, starts, low, high)

        def score(h, side, low=low, high=high):
            top = None
            for first in range(0, high, BLOCK):
                span = slice(first, first + BLOCK)
                made = (
                    nn(key_rows[h // GROUP, span, :], query[head_rows(h + g), low:high])
                    + bias[span, :]
                )
                scores[side, span, :] = made
                best = jnp.max(made.reshape(BLOCK // 8, 8, BLOCK), axis=0)
                top = best if top is None else jnp.maximum(top, best)
            return jnp.max(top, axis=0, keepdims=True)

        def blend(h, side, top, low=low, high=high, kept=kept):
            for first in range(0, high, BLOCK):
                span = slice(first, first + BLOCK)
                kept[h, span, :] = jnp.exp(scores[side, span, :] - top).astype(bf16)
            made = nn(value_aug[h // GROUP, :, :high], kept[h])
            scale = 1.0 / made[HD : HD + 1]
            mixed_t[head_rows(h + 1), low:high] = (made[:HD] * scale).astype(bf16)
            scales[pl.ds(h, 1), low:high] = scale

        def group(j, top, score=score, blend=blend):
            for member in range(GROUP):
                h = j * GROUP + member
                later = score(jnp.minimum(h + 1, HEADS - 1), (member + 1) % GROUP)
                blend(h, member, top)
                top = later
            return top

        if block < BLOCKS - 1:
            lax.fori_loop(0, KEYS, group, score(0, 0))
        else:
            top = score(0, 0)
            for h in range(HEADS):
                later = score(h + 1, (h + 1) % GROUP) if h + 1 < HEADS else None
                blend(h, h % GROUP, top)
                top = later
        stores.append(copied(kept, chances_out[block], keep_sem.at[block]))
        stores[-1].start()
        for pair in range(QW // 128):
            side = pl.ds(pl.multiple_of((2 * pair + 1 - g) * HD, HD), 128)
            mixed[low:high, pair * 128 : pair * 128 + 128] = mixed_t[side, low:high].T
    last = [
        copied(mixed.at[here], o_own, out_sems.at[7]),
        copied(mixed.at[there], o_send, out_sems.at[8]),
        copied(mixed_t, o_out, out_sems.at[9]),
        copied(scales, scale_out, out_sems.at[10]),
    ]
    for store in last:
        store.start()
    for store in stores + last:
        store.wait()


def attend(adapter, tok_own, *rest):
    rows = tok_own.shape[0]
    length = 2 * rows
    shape = jax.ShapeDtypeStruct
    return pl.pallas_call(
        attend_kernel,
        out_shape=[
            shape((rows, QW), bf16),
            shape((rows, QW), bf16),
            shape((QW, length), bf16),
            shape((KW, length), bf16),
            shape((KW, length), bf16),
            shape(((HEADS + 2) * HD, length), bf16),
            shape((length, D), bf16),
            shape((3 * R, length), bf16),
            shape((R, length), f32),
            shape((HD // 2, length), f32),
            shape((HD // 2, length), f32),
        ]
        + [shape((HEADS, (block + 1) * BLOCK, BLOCK), bf16) for block in range(BLOCKS)],
        in_specs=[SMEM, HBM, ANY, HBM, ANY] + [HBM] * 3 + [VMEM] * 3,
        out_specs=[HBM] * (11 + BLOCKS),
        scratch_shapes=[
            pltpu.VMEM((HEADS, (block + 1) * BLOCK, BLOCK), bf16) for block in range(BLOCKS)
        ]
        + [
            pltpu.VMEM((length, D), bf16),
            pltpu.VMEM((length, AUG), bf16),
            pltpu.VMEM((AUG, SPAN), bf16),
            pltpu.VMEM((128, D), bf16),
            pltpu.VMEM((QW, length), bf16),
            pltpu.VMEM((KW, length), bf16),
            pltpu.VMEM((KW, length), bf16),
            pltpu.VMEM((KEYS, length, HD), bf16),
            pltpu.VMEM((KEYS, HD + R, length), bf16),
            pltpu.VMEM(((HEADS + 2) * HD, length), bf16),
            pltpu.VMEM((length, QW), bf16),
            pltpu.VMEM((GROUP, length, BLOCK), f32),
            pltpu.VMEM((length, BLOCK), f32),
            pltpu.VMEM((HD // 2, length), f32),
            pltpu.VMEM((HD // 2, length), f32),
            pltpu.VMEM((3 * R, length), bf16),
            pltpu.VMEM((R, length), f32),
            pltpu.SemaphoreType.DMA((5,)),
            pltpu.SemaphoreType.DMA((9,)),
            pltpu.SemaphoreType.DMA((11,)),
            pltpu.SemaphoreType.DMA((BLOCKS,)),
        ],
        compiler_params=pltpu.CompilerParams(vmem_limit_bytes=50 << 20),
        cost_estimate=pl.CostEstimate(
            flops=16 * 10**9, bytes_accessed=16 << 20, transcendentals=6 * 10**6
        ),
        name="attend",
    )(adapter, tok_own, *rest)


def normed_back(rows, gain_row, grad):
    scale = lax.rsqrt(jnp.mean(rows * rows, axis=-1, keepdims=True) + epsilon)
    scaled = grad * gain_row
    inside = jnp.mean(rows * scaled, axis=-1, keepdims=True)
    return scale * (scaled - rows * (scale * scale * inside))


def rounded_up(count, unit):
    return -(-count // unit) * unit


def feed_lanes(reps):
    return rounded_up((5 * D + 3 * FF) // reps, 256)


def qkv_lanes(reps):
    return rounded_up((4 * D + 2 * KV) // reps + 1, 128)


def packed(grads, reps, target):
    for rep in range(reps):
        at = 0
        for grad in grads:
            piece = grad.shape[-1] // reps
            share = grad[:, rep * piece : (rep + 1) * piece]
            target[rep * R : (rep + 1) * R, at : at + piece] = share.astype(target.dtype)
            at += piece


def feed_kernel(
    reps,
    adapter,
    o_own_in,
    o_oth_in,
    tok_in,
    cot_in,
    wo_own,
    wo_oth,
    wgu_own,
    wgu_oth,
    wd_own,
    wd_oth,
    a_down,
    lower_t,
    upper_width,
    upper_hidden,
    gains_own,
    gains_oth,
    layer_out,
    grad_middle,
    do_own_out,
    do_oth_out,
    pack_own_out,
    pack_send_out,
    o_own,
    o_oth,
    tok,
    cot,
    do_own,
    do_oth,
    wout,
    wg,
    wu,
    wd,
    at_out,
    at_gu,
    b_out,
    b_down,
    middle,
    normed,
    cot_aug,
    total,
    back,
    result,
    z_gu_t,
    dz_down_t,
    ga_out,
    pack,
    sems,
    o_sems,
    out_sems,
):
    g = lax.axis_index("grp")
    chosen = adapter[0]
    gain = gain_row(g, gains_own, gains_oth, 1)
    steps = FF // TILE
    each = steps // 2
    w_here = pl.ds(pl.multiple_of(g * HALF, 64), HALF)
    w_there = pl.ds(pl.multiple_of((1 - g) * HALF, 64), HALF)

    def column(step):
        owner = jnp.where(step < each, g, 1 - g)
        return owner * (FF // 2) + (step % each) * TILE

    def copies(step, slot):
        at = pl.multiple_of(column(step), TILE)
        gate_at = pl.ds(at, TILE)
        up_at = pl.ds(pl.multiple_of(FF + at, TILE), TILE)
        sem = lambda k: sems.at[slot, k]
        return [
            copied(wgu_own.at[:, gate_at], wg.at[slot, w_here], sem(0)),
            copied(wgu_oth.at[:, gate_at], wg.at[slot, w_there], sem(1)),
            copied(wgu_own.at[:, up_at], wu.at[slot, w_here], sem(2)),
            copied(wgu_oth.at[:, up_at], wu.at[slot, w_there], sem(3)),
            copied(upper_hidden.at[0, chosen, :, gate_at], wg.at[slot, pl.ds(D, R)], sem(4)),
            copied(upper_hidden.at[1, chosen, :, gate_at], wu.at[slot, pl.ds(D + R, R)], sem(5)),
            copied(a_down.at[gate_at], wd.at[slot, :, pl.ds(D, 128)], sem(6)),
        ]

    def down_copy(source, step, slot):
        local = pl.ds(pl.multiple_of((step % each) * TILE, TILE), TILE)
        return copied(source.at[local], wd.at[slot, :, pl.ds(0, D)], sems.at[slot, 7])

    def start(step, slot):
        for copy in copies(step, slot):
            copy.start()

        @pl.when(step < each)
        def _():
            down_copy(wd_own, step, slot).start()

        @pl.when(step >= each)
        def _():
            down_copy(wd_oth, step, slot).start()

    def wait(step, slot):
        for copy in copies(step, slot):
            copy.wait()
        down_copy(wd_own, step, slot).wait()

    for slot in range(2):
        wg[slot, D:, :] = jnp.zeros((128, TILE), bf16)
        wu[slot, D:, :] = jnp.zeros((128, TILE), bf16)
        at_out[slot] = jnp.zeros((128, QW), bf16)
        wout[slot, :HD, :D] = jnp.zeros((HD, D), bf16)
        wout[slot, HALF:, :D] = jnp.zeros((HD, D), bf16)
    for ref in (at_gu, b_out, b_down):
        ref[...] = jnp.zeros_like(ref)
    own_at = pl.multiple_of(g * 512, 128)
    oth_at = pl.multiple_of((1 - g) * 512, 128)
    loads = [
        copied(
            wo_own, wout.at[0, pl.ds(pl.multiple_of(g * HD, HD), HALF), pl.ds(0, D)], o_sems.at[0]
        ),
        copied(
            wo_oth,
            wout.at[1, pl.ds(pl.multiple_of((1 - g) * HD, HD), HALF), pl.ds(0, D)],
            o_sems.at[1],
        ),
        copied(lower_t.at[3, chosen, :, pl.ds(own_at, QW)], at_out.at[0, pl.ds(0, R)], o_sems.at[2]),
        copied(lower_t.at[3, chosen, :, pl.ds(oth_at, QW)], at_out.at[1, pl.ds(0, R)], o_sems.at[3]),
        copied(lower_t.at[4, chosen], at_gu.at[pl.ds(0, R)], o_sems.at[4]),
        copied(lower_t.at[5, chosen], at_gu.at[pl.ds(R, R)], o_sems.at[5]),
        copied(upper_width.at[1, chosen], b_out.at[pl.ds(0, R)], o_sems.at[6]),
        copied(upper_width.at[2, chosen], b_down.at[pl.ds(0, R)], o_sems.at[7]),
        copied(o_own_in, o_own, o_sems.at[8]),
        copied(o_oth_in, o_oth, o_sems.at[9]),
        copied(tok_in, tok, o_sems.at[10]),
        copied(cot_in, cot, o_sems.at[11]),
    ]
    first, second, third = loads[11:] + loads[2:4] + loads[7:8], loads[:2] + loads[8:10], loads[4:7] + loads[10:11]
    for load in first + second + third:
        load.start()
    pack[...] = jnp.zeros_like(pack)
    total[...] = jnp.zeros_like(total)
    back[...] = jnp.zeros_like(back)
    for load in first:
        load.wait()
    cot_aug[:, :D] = cot[...]
    dz_down = nt(cot[...], b_down[...])
    cot_aug[:, D:] = dz_down.astype(bf16)
    dz_down_t[...] = dz_down.T[:R, :].astype(bf16)
    for slot in range(2):
        wout[slot, :, D:] = at_out[slot].T
    for load in second + third:
        load.wait()
    start(0, 0)
    made = nn(o_own[...], wout[0]) + nn(o_oth[...], wout[1])
    inner_out = made[:, D:].astype(bf16)
    middle[...] = tok[...].astype(f32) + made[:, :D] + nn(inner_out, b_out[...])
    scale = lax.rsqrt(jnp.mean(middle[...] * middle[...], axis=-1, keepdims=True) + epsilon)
    normed[:, :D] = (middle[...] * scale * gain).astype(bf16)
    inner_gu = nt(normed[:, :D], at_gu[...])
    normed[:, D:] = inner_gu.astype(bf16)
    z_gu_t[...] = inner_gu.T[: 2 * R, :].astype(bf16)

    def step_body(step, carry):
        slot = step % 2

        @pl.when(step + 1 < steps)
        def _():
            start(step + 1, 1 - slot)

        wait(step, slot)
        parts = []
        for at in range(0, TILE, 256):
            cols = slice(at, at + 256)
            parts.append(
                (
                    nn(normed[...], wg[slot, :, cols]),
                    nn(normed[...], wu[slot, :, cols]),
                    nt(cot_aug[...], wd[slot, cols, :]),
                )
            )
        acts, gates, ups = [], [], []
        for gate, up, grad_active in parts:
            sigmoid = 1.0 / (1.0 + jnp.exp(-gate))
            silu = gate * sigmoid
            acts.append((silu * up).astype(bf16))
            gates.append(
                (grad_active * up * (sigmoid * (1.0 + gate * (1.0 - sigmoid)))).astype(bf16)
            )
            ups.append((grad_active * silu).astype(bf16))
        active = jnp.concatenate(acts, axis=1)
        grad_gate = jnp.concatenate(gates, axis=1)
        grad_up = jnp.concatenate(ups, axis=1)
        total[...] += nn(active, wd[slot])
        back[...] += nt(grad_gate, wg[slot]) + nt(grad_up, wu[slot])
        shares = (
            nn(dz_down_t[...], active),
            nn(z_gu_t[...], grad_gate)[:R],
            nn(z_gu_t[...], grad_up)[R:],
        )
        piece = FF // reps
        base = column(step) // piece
        for index, share in enumerate(shares):
            at = 5 * (D // reps) + index * piece
            for rep in range(TILE // piece):
                target = pl.ds(pl.multiple_of((base + rep) * R, R), R)
                pack[target, at : at + piece] = share[:, rep * piece : (rep + 1) * piece].astype(bf16)
        return carry

    lax.fori_loop(0, steps, step_body, 0)

    inner_down = total[:, D:].astype(bf16)
    result[...] = (middle[...] + total[:, :D] + nn(inner_down, b_down[...])).astype(bf16)
    stores = [copied(result, layer_out, out_sems.at[0])]
    stores[0].start()
    gb_down = nn(total[:, D:].T[:R, :].astype(bf16), cot[...])
    dz_gu = back[:, D:].astype(bf16)
    grad_normed = back[:, :D] + nn(dz_gu, at_gu[...])
    grad = cot[...].astype(f32) + normed_back(middle[...], gain, grad_normed)
    total[:, :D] = grad
    stores.append(copied(total.at[:, pl.ds(0, D)], grad_middle, out_sems.at[1]))
    stores[1].start()
    branch = normed
    ga_gu = nn(back[:, D:].T[: 2 * R, :].astype(bf16), normed[:, :D])
    branch[:, :D] = grad.astype(bf16)
    dz_out = nt(branch[:, :D], b_out[...])
    branch[:, D:] = dz_out.astype(bf16)
    dz_out_t = dz_out.T[:R, :].astype(bf16)
    do_oth[...] = nt(wout[1], branch[...]).astype(bf16)
    stores.append(copied(do_oth, do_oth_out, out_sems.at[2]))
    stores[-1].start()
    do_own[...] = nt(wout[0], branch[...]).astype(bf16)
    stores.append(copied(do_own, do_own_out, out_sems.at[3]))
    stores[-1].start()
    gb_out = nn(inner_out.astype(f32).T[:R, :].astype(bf16), branch[:, :D])
    ga_out[...] = jnp.zeros_like(ga_out)
    ga_out[:, pl.ds(own_at, QW)] += nn(dz_out_t, o_own[...])
    ga_out[:, pl.ds(oth_at, QW)] += nn(dz_out_t, o_oth[...])
    packed([ga_out[...], ga_gu[:R], ga_gu[R:], gb_out, gb_down], reps, pack)
    half = pack.shape[1] // 2
    for index, (side, target) in enumerate(((g, pack_own_out), (1 - g, pack_send_out))):
        source = pack.at[:, pl.ds(pl.multiple_of(side * half, 128), half)]
        stores.append(copied(source, target, out_sems.at[4 + index]))
        stores[-1].start()
    for store in stores:
        store.wait()


def feed(reps, *args):
    rows = args[3].shape[0]
    half = feed_lanes(reps) // 2
    shape = jax.ShapeDtypeStruct
    return pl.pallas_call(
        functools.partial(feed_kernel, reps),
        out_shape=[
            shape((rows, D), bf16),
            shape((rows, D), f32),
            shape((QW, rows), bf16),
            shape((QW, rows), bf16),
            shape((reps * R, half), bf16),
            shape((reps * R, half), bf16),
        ],
        in_specs=[SMEM, HBM, ANY] + [HBM] * 12 + [VMEM] * 2,
        out_specs=[HBM] * 6,
        scratch_shapes=[
            pltpu.VMEM((rows, QW), bf16),
            pltpu.VMEM((rows, QW), bf16),
            pltpu.VMEM((rows, D), bf16),
            pltpu.VMEM((rows, D), bf16),
            pltpu.VMEM((QW, rows), bf16),
            pltpu.VMEM((QW, rows), bf16),
            pltpu.VMEM((2, QW, AUG), bf16),
            pltpu.VMEM((2, AUG, TILE), bf16),
            pltpu.VMEM((2, AUG, TILE), bf16),
            pltpu.VMEM((2, TILE, AUG), bf16),
            pltpu.VMEM((2, 128, QW), bf16),
            pltpu.VMEM((128, D), bf16),
            pltpu.VMEM((128, D), bf16),
            pltpu.VMEM((128, D), bf16),
            pltpu.VMEM((rows, D), f32),
            pltpu.VMEM((rows, AUG), bf16),
            pltpu.VMEM((rows, AUG), bf16),
            pltpu.VMEM((rows, AUG), f32),
            pltpu.VMEM((rows, AUG), f32),
            pltpu.VMEM((rows, D), bf16),
            pltpu.VMEM((2 * R, rows), bf16),
            pltpu.VMEM((R, rows), bf16),
            pltpu.VMEM((R, D), f32),
            pltpu.VMEM((reps * R, 2 * half), bf16),
            pltpu.SemaphoreType.DMA((2, 8)),
            pltpu.SemaphoreType.DMA((12,)),
            pltpu.SemaphoreType.DMA((6,)),
        ],
        compiler_params=pltpu.CompilerParams(vmem_limit_bytes=44 << 20),
        cost_estimate=pl.CostEstimate(
            flops=30 * 10**9, bytes_accessed=36 << 20, transcendentals=2 * 10**6
        ),
        name="feed",
    )(*args)


def attend_back_kernel(
    reps,
    adapter,
    do_own,
    do_oth,
    o_in,
    normed,
    upper_width,
    upper_keys,
    query_in,
    k_in,
    v_in,
    zt_in,
    scale_in,
    cos_in,
    sin_in,
    pack_own_in,
    pack_oth_in,
    *refs,
):
    attend_back_body(
        reps,
        adapter,
        do_own,
        do_oth,
        o_in,
        normed,
        upper_width,
        upper_keys,
        query_in,
        k_in,
        v_in,
        zt_in,
        scale_in,
        cos_in,
        sin_in,
        pack_own_in,
        pack_oth_in,
        refs[:BLOCKS],
        refs[BLOCKS + 3 : 2 * BLOCKS + 3],
        *refs[BLOCKS : BLOCKS + 3],
        *refs[2 * BLOCKS + 3 :],
    )


def attend_back_body(
    reps,
    adapter,
    do_own,
    do_oth,
    o_in,
    normed,
    upper_width,
    upper_keys,
    query_in,
    k_in,
    v_in,
    zt_in,
    scale_in,
    cos_in,
    sin_in,
    pack_own_in,
    pack_oth_in,
    chances_in,
    chances,
    dy_out,
    part_out,
    exchange_out,
    query,
    key_t,
    value_t,
    zt,
    scales,
    cosine,
    sine,
    pack_own,
    pack_oth,
    exchange,
    grad_o,
    mixed_t,
    n_rows,
    weight,
    value_rows,
    delta,
    dq,
    dk,
    dv,
    dy_t,
    dy,
    grad_scores,
    gb_q,
    gb_kv,
    pack,
    sems,
    b_sems,
    out_sem,
    keep_sem,
):
    g = lax.axis_index("grp")
    chosen = adapter[0]
    length = query.shape[1]
    rows = length // 2
    here = pl.ds(pl.multiple_of(g * rows, 128), rows)
    there = pl.ds(pl.multiple_of((1 - g) * rows, 128), rows)
    weight[...] = jnp.zeros_like(weight)
    early = [
        copied(k_in, key_t, sems.at[0]),
        copied(v_in, value_t, sems.at[1]),
    ]
    loads = [
        copied(do_own, grad_o.at[:, here], sems.at[2]),
        copied(do_oth, grad_o.at[:, there], sems.at[3]),
        copied(o_in, mixed_t, sems.at[4]),
        copied(query_in, query, sems.at[5]),
        copied(scale_in, scales, sems.at[6]),
    ]
    late = [
        copied(cos_in, cosine, sems.at[7]),
        copied(sin_in, sine, sems.at[8]),
        copied(normed, n_rows, sems.at[9]),
        copied(zt_in, zt, sems.at[10]),
        copied(pack_own_in, pack_own, sems.at[11]),
        copied(pack_oth_in, pack_oth, sems.at[12]),
    ] + upper_loads(g, chosen, upper_width, upper_keys, weight, 0, b_sems)
    kept = [
        copied(chances_in[block], chances[block], keep_sem.at[block]) for block in range(BLOCKS)
    ]
    for load in early + loads:
        load.start()
    kept[0].start()
    dk[...] = jnp.zeros_like(dk)
    dv[...] = jnp.zeros_like(dv)
    dy_t[...] = jnp.zeros_like(dy_t)
    for load in early:
        load.wait()
    for j in range(KEYS):
        value_rows[j] = value_t[head_rows(j + g), :].T
    for load in loads:
        load.wait()
    for load in kept[1:] + late:
        load.start()
    for h in range(HEADS):
        scaled = grad_o[head_rows(h + g), :].astype(f32) * scales[h : h + 1, :]
        product = scaled * mixed_t[(h + 1) * HD : (h + 2) * HD, :].astype(f32)
        delta[h : h + 1, :] = jnp.sum(product, axis=0, keepdims=True)
        grad_o[head_rows(h + g), :] = scaled.astype(bf16)

    for block in range(length // BLOCK):
        low, high = block * BLOCK, (block + 1) * BLOCK
        found = chances[block]
        kept[block].wait()

        def score(h, side, low=low, high=high, found=found):
            deltas = delta[pl.ds(h, 1), low:high]
            for first in range(0, high, BLOCK):
                span = slice(first, first + BLOCK)
                grad = nn(value_rows[h // GROUP, span, :], grad_o[head_rows(h + g), low:high])
                chance = found[h, span, :].astype(f32)
                grad_scores[side, span, :] = (chance * (grad - deltas)).astype(bf16)

        def spread(h, side, low=low, high=high, found=found):
            dq[h, :, low:high] = nn(
                key_t[head_rows(h // GROUP + g), :high], grad_scores[side, :high, :]
            )
            return (
                nt(grad_o[head_rows(h + g), low:high], found[h]),
                nt(query[head_rows(h + g), low:high], grad_scores[side, :high, :]),
            )

        def group(j, carry, high=high, score=score, spread=spread):
            sums = []
            for member in range(GROUP):
                h = j * GROUP + member
                score(jnp.minimum(h + 1, HEADS - 1), (member + 1) % GROUP)
                sums.append(spread(h, member))
            dv[j, :, :high] += sums[0][0] + sums[1][0] + sums[2][0]
            dk[j, :, :high] += sums[0][1] + sums[1][1] + sums[2][1]
            return carry

        score(0, 0)
        lax.fori_loop(0, KEYS, group, 0)

    for load in late:
        load.wait()
    back_sine = -sine[...]
    for h in range(HEADS):
        dy_t[(h + 1) * HD : (h + 2) * HD, :] = (
            turned(dq[h], cosine[...], back_sine) * HD**-0.5
        ).astype(bf16)
    key_base = (HEADS + 2) * HD
    value_base = key_base + (KEYS + 2) * HD
    for j in range(KEYS):
        at = key_base + (j + 1) * HD
        dy_t[at : at + HD, :] = turned(dk[j], cosine[...], back_sine).astype(bf16)
        at = value_base + (j + 1) * HD
        dy_t[at : at + HD, :] = dv[j].astype(bf16)
    for base, count, to in ((0, QW, 0), (key_base, KW, QW), (value_base, KW, QW + KW)):
        for at in range(0, count, 128):
            side = pl.ds(pl.multiple_of(base + at + (1 - g) * HD, HD), 128)
            dy[:, to + at : to + at + 128] = dy_t[side, :].T
    inner = nt(dy[:, :SPAN], weight[...])
    dy[:, SPAN:] = inner.astype(bf16)
    dy_stores = [
        copied(dy.at[place], target, out_sem.at[index])
        for place, target, index in ((there, part_out, 0), (here, dy_out, 1))
    ]
    for copy in dy_stores:
        copy.start()
    gb = nn(zt[...], dy[:, :SPAN])
    gb_q[...] = jnp.zeros_like(gb_q)
    gb_kv[...] = jnp.zeros_like(gb_kv)
    gb_q[:, pl.ds(pl.multiple_of(g * 512, 128), QW)] = gb[:R, :QW]
    for index in range(2):
        gb_kv[index, :, pl.ds(pl.multiple_of(g * 128, 128), KW)] = gb[
            (index + 1) * R : (index + 2) * R, QW + index * KW : QW + (index + 1) * KW
        ]
    ga = nn(inner.T[: 3 * R, :].astype(bf16), n_rows[...])
    pack[...] = jnp.zeros_like(pack)
    packed(
        [ga[:R], ga[R : 2 * R], ga[2 * R :], gb_q[...], gb_kv[0], gb_kv[1]],
        reps,
        pack,
    )
    half = pack_own.shape[1]
    width = pack.shape[1]
    exchange[:, :half] = (pack_own[...].astype(f32) + pack_oth[...].astype(f32)).astype(bf16)
    exchange[:, half:] = jnp.where(
        lanes(pack.shape) == width - 1, chosen.astype(f32), pack[...].astype(f32)
    ).astype(bf16)
    last = copied(exchange, exchange_out, out_sem.at[2])
    last.start()
    for copy in (*dy_stores, last):
        copy.wait()


def attend_back(reps, *args):
    rows = args[1].shape[1]
    length = 2 * rows
    half = feed_lanes(reps) // 2
    width = qkv_lanes(reps)
    shape = jax.ShapeDtypeStruct
    return pl.pallas_call(
        functools.partial(attend_back_kernel, reps),
        out_shape=[
            shape((rows, AUG), bf16),
            shape((rows, AUG), bf16),
            shape((reps * R, half + width), bf16),
        ],
        in_specs=[SMEM, HBM, ANY] + [HBM] * 12 + [ANY] + [HBM] * BLOCKS,
        out_specs=[HBM] * 3,
        scratch_shapes=[
            pltpu.VMEM((HEADS, (block + 1) * BLOCK, BLOCK), bf16) for block in range(BLOCKS)
        ]
        + [
            pltpu.VMEM((QW, length), bf16),
            pltpu.VMEM((KW, length), bf16),
            pltpu.VMEM((KW, length), bf16),
            pltpu.VMEM((3 * R, length), bf16),
            pltpu.VMEM((R, length), f32),
            pltpu.VMEM((HD // 2, length), f32),
            pltpu.VMEM((HD // 2, length), f32),
            pltpu.VMEM((reps * R, half), bf16),
            pltpu.VMEM((reps * R, half), bf16),
            pltpu.VMEM((reps * R, half + width), bf16),
            pltpu.VMEM((QW, length), bf16),
            pltpu.VMEM(((HEADS + 2) * HD, length), bf16),
            pltpu.VMEM((length, D), bf16),
            pltpu.VMEM((128, SPAN), bf16),
            pltpu.VMEM((KEYS, length, HD), bf16),
            pltpu.VMEM((R, length), f32),
            pltpu.VMEM((HEADS, HD, length), f32),
            pltpu.VMEM((KEYS, HD, length), f32),
            pltpu.VMEM((KEYS, HD, length), f32),
            pltpu.VMEM(((HEADS + 2 * KEYS + 6) * HD, length), bf16),
            pltpu.VMEM((length, AUG), bf16),
            pltpu.VMEM((GROUP, length, BLOCK), bf16),
            pltpu.VMEM((R, D), f32),
            pltpu.VMEM((2, R, KV), f32),
            pltpu.VMEM((reps * R, width), bf16),
            pltpu.SemaphoreType.DMA((16,)),
            pltpu.SemaphoreType.DMA((9,)),
            pltpu.SemaphoreType.DMA((4,)),
            pltpu.SemaphoreType.DMA((BLOCKS,)),
        ],
        compiler_params=pltpu.CompilerParams(vmem_limit_bytes=50 << 20),
        cost_estimate=pl.CostEstimate(
            flops=24 * 10**9, bytes_accessed=20 << 20, transcendentals=6 * 10**6
        ),
        name="attend_back",
    )(*args)


def finish_kernel(
    adapter,
    dy_in,
    qkv_own,
    qkv_oth,
    lower_t,
    tok_in,
    gains_own,
    gains_oth,
    part_in,
    middle_in,
    out,
    dy,
    part,
    tok,
    grad_middle,
    weight,
    weight_oth,
    maps,
    result,
    sems,
    w_sems,
    out_sem,
):
    g = lax.axis_index("grp")
    chosen = adapter[0]
    maps[...] = jnp.zeros_like(maps)
    loads = qkv_loads(g, g, qkv_own, qkv_oth, weight, w_sems.at[0])
    loads += qkv_loads(g, 1 - g, qkv_own, qkv_oth, weight_oth, w_sems.at[1])
    for index, (source, target) in enumerate(
        ((dy_in, dy), (part_in, part), (tok_in, tok), (middle_in, grad_middle))
    ):
        loads.append(copied(source, target, sems.at[index]))
    for index in range(3):
        loads.append(
            copied(lower_t.at[index, chosen], maps.at[pl.ds(index * R, R)], sems.at[5 + index])
        )
    for load in loads:
        load.start()
    gain = gain_row(g, gains_own, gains_oth, 0)
    for load in loads:
        load.wait()

    def half(index, carry):
        count = tok.shape[0] // 2
        span = pl.ds(pl.multiple_of(index * count, 128), count)
        inner = dy[span, SPAN:].astype(f32) + part[span, SPAN:].astype(f32)
        grad = (
            nt(dy[span, :SPAN], weight[...])
            + nt(part[span, :SPAN], weight_oth[...])
            + nn(inner.astype(bf16), maps[...])
        )
        result[span, :] = (
            grad_middle[span, :] + normed_back(tok[span, :].astype(f32), gain, grad)
        ).astype(bf16)
        return carry

    lax.fori_loop(0, 2, half, 0)
    store = copied(result, out, out_sem.at[0])
    store.start()
    store.wait()


def finish(*args):
    rows = args[1].shape[0]
    return pl.pallas_call(
        finish_kernel,
        out_shape=jax.ShapeDtypeStruct((rows, D), bf16),
        in_specs=[SMEM] + [HBM] * 5 + [VMEM] * 2 + [ANY, HBM],
        out_specs=HBM,
        scratch_shapes=[
            pltpu.VMEM((rows, AUG), bf16),
            pltpu.VMEM((rows, AUG), bf16),
            pltpu.VMEM((rows, D), bf16),
            pltpu.VMEM((rows, D), f32),
            pltpu.VMEM((D, SPAN), bf16),
            pltpu.VMEM((D, SPAN), bf16),
            pltpu.VMEM((128, D), bf16),
            pltpu.VMEM((rows, D), bf16),
            pltpu.SemaphoreType.DMA((8,)),
            pltpu.SemaphoreType.DMA((2, 6)),
            pltpu.SemaphoreType.DMA((1,)),
        ],
        compiler_params=pltpu.CompilerParams(vmem_limit_bytes=50 << 20),
        cost_estimate=pl.CostEstimate(
            flops=4 * 10**9, bytes_accessed=10 << 20, transcendentals=0
        ),
        name="finish",
    )(*args)


def collect_kernel(source, keep, send, received, sem):
    load = copied(source, received, sem.at[0])
    load.start()
    load.wait()
    g = lax.axis_index("grp")
    count, width = received.shape
    quota = NAD // 2
    label = received[:, width - 1 :].astype(f32)
    lane = lanes((count, NAD * R))
    row = lax.broadcasted_iota(jnp.int32, (count, NAD * R), 0)
    picks = ((lane // R).astype(f32) == label) & (lane % R == row % R)
    sums = tn(picks.astype(f32).astype(bf16), received[...])
    first = g == 0
    for adapter in range(quota):
        low = sums[adapter * R : (adapter + 1) * R]
        high = sums[(quota + adapter) * R : (quota + adapter + 1) * R]
        keep[adapter] = jnp.where(first, low, high)
        send[adapter] = jnp.where(first, high, low)


def collect(received):
    shape = jax.ShapeDtypeStruct((NAD // 2, R, received.shape[1]), f32)
    return pl.pallas_call(
        collect_kernel,
        out_shape=[shape, shape],
        in_specs=[ANY],
        out_specs=[VMEM] * 2,
        scratch_shapes=[
            pltpu.VMEM(received.shape, bf16),
            pltpu.SemaphoreType.DMA((1,)),
        ],
        compiler_params=pltpu.CompilerParams(vmem_limit_bytes=8 << 20),
        cost_estimate=pl.CostEstimate(flops=10**8, bytes_accessed=2 << 20, transcendentals=0),
        name="collect",
    )(received)


def deliver_kernel(reps, keep, other, lower, down, width, keys, hidden, feeds, qkvs):
    g = lax.axis_index("grp")
    half = feeds.shape[-1] // 2
    feeds[:, :, pl.ds(pl.multiple_of(g * half, 128), half)] = keep[:, :, :half]
    feeds[:, :, pl.ds(pl.multiple_of((1 - g) * half, 128), half)] = other[:, :, :half]
    qkvs[...] = keep[:, :, half:] + other[:, :, half:]
    piece, tall, short = D // reps, FF // reps, KV // reps
    for index in range(3):
        lower[index] = qkvs[:, :, index * piece : (index + 1) * piece]
        lower[3 + index] = feeds[:, :, index * piece : (index + 1) * piece]
    width[0] = qkvs[:, :, 3 * piece : 4 * piece]
    width[1] = feeds[:, :, 3 * piece : 4 * piece]
    width[2] = feeds[:, :, 4 * piece : 5 * piece]
    for index in range(2):
        at = 4 * piece + index * short
        keys[index] = qkvs[:, :, at : at + short]
        at = 5 * piece + (1 + index) * tall
        hidden[index] = feeds[:, :, at : at + tall]
    down[...] = feeds[:, :, 5 * piece : 5 * piece + tall]


def deliver(reps, keep, other):
    quota = NAD // 2
    shape = lambda *dims: jax.ShapeDtypeStruct(dims, f32)
    return pl.pallas_call(
        functools.partial(deliver_kernel, reps),
        out_shape=[
            shape(6, quota, R, D // reps),
            shape(quota, R, FF // reps),
            shape(3, quota, R, D // reps),
            shape(2, quota, R, KV // reps),
            shape(2, quota, R, FF // reps),
        ],
        in_specs=[VMEM] * 2,
        out_specs=[VMEM] * 5,
        scratch_shapes=[
            pltpu.VMEM((quota, R, feed_lanes(reps)), f32),
            pltpu.VMEM((quota, R, qkv_lanes(reps)), f32),
        ],
        compiler_params=pltpu.CompilerParams(vmem_limit_bytes=8 << 20),
        cost_estimate=pl.CostEstimate(flops=10**6, bytes_accessed=1 << 20, transcendentals=0),
        name="deliver",
    )(keep, other)


def per_device(
    tokens,
    cotangent,
    segment_ids,
    adapter_ids,
    norm_gains,
    frozen_qkv,
    frozen_out,
    frozen_gate_up,
    frozen_down,
    lower_mats,
    lower_down,
    upper_width,
    upper_keys,
    upper_hidden,
):
    reps = lax.axis_size("rep")
    chosen = adapter_ids[0]
    first = lax.axis_index("grp") == 0
    swap = lambda value: lax.ppermute(value, "grp", SWAP)

    tok_own = tokens[0]
    tok_oth = swap(tok_own)
    qkv_oth = swap(frozen_qkv)
    gains_oth = swap(norm_gains)
    a_down = jnp.pad(
        lax.dynamic_index_in_dim(lower_down, chosen, 0, keepdims=False), ((0, 0), (0, 128 - R))
    )
    tok_oth, qkv_oth, gains_oth, a_down, wo, wgu, wd = lax.optimization_barrier(
        (tok_oth, qkv_oth, gains_oth, a_down, frozen_out, frozen_gate_up, frozen_down)
    )
    wo_oth = swap(wo)
    wgu_oth = swap(wgu)
    wd_oth = swap(wd)

    lower_t = lower_mats.transpose(0, 1, 3, 2)
    gains = (norm_gains, gains_oth)

    (o_own, o_send, query, key_t, value_t, mixed_t, normed, zt, scales, cosine, sine, *chances) = (
        attend(
            adapter_ids,
            tok_own,
            tok_oth,
            frozen_qkv,
            qkv_oth,
            lower_t,
            upper_width,
            upper_keys,
            *gains,
            segment_ids,
        )
    )
    o_oth = swap(o_send)
    layer_out, grad_middle, do_own, do_send, pack_own, pack_send = feed(
        reps,
        adapter_ids,
        o_own,
        o_oth,
        tok_own,
        cotangent[0],
        frozen_out,
        wo_oth,
        frozen_gate_up,
        wgu_oth,
        frozen_down,
        wd_oth,
        a_down,
        lower_t,
        upper_width,
        upper_hidden,
        *gains,
    )
    do_oth = swap(do_send)
    pack_oth = swap(pack_send)
    dy, dy_send, exchange = attend_back(
        reps,
        adapter_ids,
        do_own,
        do_oth,
        mixed_t,
        normed,
        upper_width,
        upper_keys,
        query,
        key_t,
        value_t,
        zt,
        scales,
        cosine,
        sine,
        pack_own,
        pack_oth,
        *chances,
    )
    received = lax.all_to_all(exchange, "rep", 0, 0, tiled=True)
    input_grad = finish(
        adapter_ids,
        dy,
        frozen_qkv,
        qkv_oth,
        lower_t,
        tok_own,
        *gains,
        swap(dy_send),
        grad_middle,
    )
    received, input_grad = lax.optimization_barrier((received, input_grad))
    keep, send = collect(received)
    lower, down, width, keys, hidden = deliver(reps, keep, swap(send))
    return (
        layer_out[None],
        input_grad[None],
        lower.transpose(0, 1, 3, 2),
        down.transpose(0, 2, 1),
        width,
        keys,
        hidden,
    )


def solution(mesh):
    return jax.shard_map(
        per_device,
        mesh=mesh,
        in_specs=(
            P("rep", "grp", None),
            P("rep", "grp", None),
            P("rep", None),
            P("rep"),
            P(None, "grp"),
            P("grp", None),
            P("grp", None),
            P("grp", None),
            P("grp", None),
            P(),
            P(),
            P(),
            P(),
            P(),
        ),
        out_specs=(
            P("rep", "grp", None),
            P("rep", "grp", None),
            P(None, "grp", "rep", None),
            P("grp", "rep", None),
            P(None, "grp", None, "rep"),
            P(None, "grp", None, "rep"),
            P(None, "grp", None, "rep"),
        ),
        check_vma=False,
    )
```

```python
import functools

import jax
import jax.numpy as jnp
import numpy as np
from jax import lax
from jax.experimental import pallas as pl
from jax.experimental.pallas import tpu as pltpu
from jax.sharding import PartitionSpec as P

D = 1152
H = 18
KVH = 6
HD = 64
FF = 3072
R = 16
NAD = 8
KV = 384

HALF = D // 2
HEADS = H // 2
GROUP = H // KVH
QW = 640
KW = 256
SPAN = QW + 2 * KW
AUG = D + 128
TILE = 768
BLOCK = 256
BLOCKS = 1024 // BLOCK
DOCS = 4
KEYS = HEADS // GROUP
VMEM_BYTES = 61900 * 1024

epsilon = 1e-05
theta_base = 10000.0
masked_value = -1e30
f32 = jnp.float32
bf16 = jnp.bfloat16
SWAP = [(0, 1), (1, 0)]

HBM = pl.BlockSpec(memory_space=pltpu.MemorySpace.HBM)
ANY = pl.BlockSpec(memory_space=pl.ANY)
VMEM = pl.BlockSpec(memory_space=pltpu.VMEM)
SMEM = pl.BlockSpec(memory_space=pltpu.SMEM)


def nn(left, right):
    return jnp.dot(left, right, preferred_element_type=f32)


def nt(left, right):
    return lax.dot_general(left, right, (((1,), (1,)), ((), ())), preferred_element_type=f32)


def tn(left, right):
    return lax.dot_general(left, right, (((0,), (0,)), ((), ())), preferred_element_type=f32)


def lanes(shape):
    return lax.broadcasted_iota(jnp.int32, shape, len(shape) - 1)


def gain_row(g, own, other, row):
    mine = own[row : row + 1, :].astype(f32)
    theirs = other[row : row + 1, :].astype(f32)
    return jnp.where(
        g == 0,
        jnp.concatenate([mine, theirs], axis=1),
        jnp.concatenate([theirs, mine], axis=1),
    )


def copied(source, target, sem):
    return pltpu.make_async_copy(source, target, sem)


def doc_starts(segments):
    return [
        jnp.sum(jnp.where(segments < doc, 1.0, 0.0), axis=-1, keepdims=True)
        for doc in range(1, DOCS)
    ]


def start_at(place, starts):
    found = jnp.zeros_like(place)
    for start in starts:
        found = jnp.where(place >= start, start, found)
    return found


def fill_angles(starts, cosine, sine):
    def both(angle):
        return jnp.cos(angle), jnp.sin(angle)

    powers = np.float32(theta_base) ** (-np.arange(HD // 2, dtype=np.float32) * 2.0 / HD)
    row = lax.broadcasted_iota(jnp.int32, (HD // 2, 128), 0)
    freqs = jnp.zeros(row.shape, f32)
    for index, power in enumerate(powers):
        freqs = jnp.where(row == index, np.float32(power), freqs)

    fine_cos, fine_sin = both(lanes(freqs.shape).astype(f32) * freqs)
    docs = [both(start * freqs) for start in starts]
    for at in range(0, cosine.shape[1], 128):
        wide_cos, wide_sin = both(float(at) * freqs)
        cos_p = wide_cos * fine_cos - wide_sin * fine_sin
        sin_p = wide_sin * fine_cos + wide_cos * fine_sin
        place = (lanes(freqs.shape) + at).astype(f32)
        cos_d, sin_d = jnp.ones_like(cos_p), jnp.zeros_like(cos_p)
        for start, (cos_s, sin_s) in zip(starts, docs):
            inside = place >= start
            cos_d = jnp.where(inside, cos_s, cos_d)
            sin_d = jnp.where(inside, sin_s, sin_d)
        cosine[:, at : at + 128] = cos_p * cos_d + sin_p * sin_d
        sine[:, at : at + 128] = sin_p * cos_d - cos_p * sin_d


def turned(block, cosine, sine):
    first, second = block[: HD // 2], block[HD // 2 :]
    return jnp.concatenate(
        [first * cosine - second * sine, second * cosine + first * sine], axis=0
    )


def head_rows(slot):
    return pl.ds(pl.multiple_of(slot * HD, HD), HD)


def fill_mask(bias, starts, low, high):
    place = lanes((1, BLOCK)).astype(f32) + low
    begin = start_at(place, starts)
    for first in range(0, high, BLOCK):
        key_place = lax.broadcasted_iota(jnp.int32, (BLOCK, BLOCK), 0).astype(f32) + first
        allowed = key_place >= begin
        if first == low:
            allowed = allowed & (key_place <= place)
        bias[first : first + BLOCK, :] = jnp.where(allowed, 0.0, masked_value)


def qkv_loads(g, side, own, oth, weight, sems):
    w_here = pl.ds(pl.multiple_of(g * HALF, 64), HALF)
    w_there = pl.ds(pl.multiple_of((1 - g) * HALF, 64), HALF)
    windows = (
        (pl.multiple_of(side * 512, 128), QW, 0),
        (pl.multiple_of(D + side * 128, 128), KW, QW),
        (pl.multiple_of(D + KV + side * 128, 128), KW, QW + KW),
    )
    loads = []
    for index, (at, width, to) in enumerate(windows):
        for part, (source, rows) in enumerate(((own, w_here), (oth, w_there))):
            loads.append(
                copied(
                    source.at[:, pl.ds(at, width)],
                    weight.at[rows, pl.ds(to, width)],
                    sems.at[2 * index + part],
                )
            )
    return loads


def upper_loads(g, chosen, upper_width, upper_keys, weight, base, sems):
    loads = []
    loads.append(
        copied(
            upper_width.at[0, chosen, :, pl.ds(pl.multiple_of(g * 512, 128), QW)],
            weight.at[pl.ds(base, R), pl.ds(0, QW)],
            sems.at[6],
        )
    )
    for index in range(2):
        loads.append(
            copied(
                upper_keys.at[index, chosen, :, pl.ds(pl.multiple_of(g * 128, 128), KW)],
                weight.at[pl.ds(base + (index + 1) * R, R), pl.ds(QW + index * KW, KW)],
                sems.at[7 + index],
            )
        )
    return loads


def attend_kernel(
    adapter,
    tok_own,
    tok_oth,
    qkv_own,
    qkv_oth,
    lower_t,
    upper_width,
    upper_keys,
    gains_own,
    gains_oth,
    segments,
    o_own,
    o_send,
    q_out,
    k_out,
    v_out,
    o_out,
    n_out,
    zt_out,
    scale_out,
    cos_out,
    sin_out,
    *refs,
):
    attend_body(
        adapter,
        tok_own,
        tok_oth,
        qkv_own,
        qkv_oth,
        lower_t,
        upper_width,
        upper_keys,
        gains_own,
        gains_oth,
        segments,
        o_own,
        o_send,
        q_out,
        k_out,
        v_out,
        o_out,
        n_out,
        zt_out,
        scale_out,
        cos_out,
        sin_out,
        refs[:BLOCKS],
        refs[BLOCKS : 2 * BLOCKS],
        *refs[2 * BLOCKS :],
    )


def attend_body(
    adapter,
    tok_own,
    tok_oth,
    qkv_own,
    qkv_oth,
    lower_t,
    upper_width,
    upper_keys,
    gains_own,
    gains_oth,
    segments,
    o_own,
    o_send,
    q_out,
    k_out,
    v_out,
    o_out,
    n_out,
    zt_out,
    scale_out,
    cos_out,
    sin_out,
    chances_out,
    chances,
    tok,
    normed,
    weight,
    maps,
    query,
    key_t,
    value_t,
    key_rows,
    value_aug,
    mixed_t,
    mixed,
    scores,
    bias,
    cosine,
    sine,
    inner_t,
    scales,
    sems,
    w_sems,
    out_sems,
    keep_sem,
):
    g = lax.axis_index("grp")
    chosen = adapter[0]
    rows = tok_own.shape[0]
    here = pl.ds(pl.multiple_of(g * rows, 128), rows)
    there = pl.ds(pl.multiple_of((1 - g) * rows, 128), rows)
    maps[...] = jnp.zeros_like(maps)
    weight[D:, :] = jnp.zeros((128, SPAN), bf16)
    loads = [
        copied(tok_own, tok.at[here], sems.at[0]),
        copied(tok_oth, tok.at[there], sems.at[1]),
    ] + [
        copied(lower_t.at[index, chosen], maps.at[pl.ds(index * R, R)], sems.at[2 + index])
        for index in range(3)
    ]
    w_loads = qkv_loads(g, g, qkv_own, qkv_oth, weight, w_sems)
    w_loads += upper_loads(g, chosen, upper_width, upper_keys, weight, D, w_sems)
    for load in loads:
        load.start()
    starts = doc_starts(segments[...])
    fill_angles(starts, cosine, sine)
    gain = gain_row(g, gains_own, gains_oth, 0)
    for load in loads:
        load.wait()
    for load in w_loads:
        load.start()

    def norm_part(part, carry):
        span = pl.ds(pl.multiple_of(part * rows, 128), rows)
        wide = tok[span, :].astype(f32)
        scale = lax.rsqrt(jnp.mean(wide * wide, axis=-1, keepdims=True) + epsilon)
        normed[span, :D] = (wide * scale * gain).astype(bf16)
        inner = nt(normed[span, :D], maps[...])
        normed[span, D:] = inner.astype(bf16)
        inner_t[:, span] = inner.T[: 3 * R, :].astype(bf16)
        return carry

    lax.fori_loop(0, 2, norm_part, 0)
    for load in w_loads:
        load.wait()

    def project(part, carry):
        span = pl.ds(pl.multiple_of(part * rows, 128), rows)
        cos_cols = cosine[:, span]
        sin_cols = sine[:, span]
        for target, base, count, turn, scale in (
            (query, 0, QW, True, HD**-0.5),
            (key_t, QW, KW, True, 1.0),
            (value_t, QW + KW, KW, False, 1.0),
        ):
            for at in range(0, count, 256):
                width = min(256, count - at)
                made = nn(normed[span, :], weight[:, base + at : base + at + width]).T
                for to in range(0, width, HD):
                    block = made[to : to + HD]
                    if turn:
                        block = turned(block, cos_cols, sin_cols) * scale
                    target[at + to : at + to + HD, span] = block.astype(bf16)
        return carry

    lax.fori_loop(0, 2, project, 0)
    stores = [
        copied(query, q_out, out_sems.at[0]),
        copied(key_t, k_out, out_sems.at[1]),
        copied(value_t, v_out, out_sems.at[2]),
        copied(normed.at[:, pl.ds(0, D)], n_out, out_sems.at[3]),
        copied(cosine, cos_out, out_sems.at[4]),
        copied(sine, sin_out, out_sems.at[5]),
        copied(inner_t, zt_out, out_sems.at[6]),
    ]
    for store in stores:
        store.start()
    for j in range(KEYS):
        key_rows[j] = key_t[head_rows(j + g), :].T
        value_aug[j, :HD, :] = value_t[head_rows(j + g), :]
        value_aug[j, HD:, :] = jnp.ones((R, 2 * rows), bf16)
    mixed_t[:HD, :] = jnp.zeros((HD, 2 * rows), bf16)
    mixed_t[(HEADS + 1) * HD :, :] = jnp.zeros((HD, 2 * rows), bf16)

    for block in reversed(range(BLOCKS)):
        low, high = block * BLOCK, (block + 1) * BLOCK
        kept = chances[block]
        fill_mask(bias, starts, low, high)

        def score(h, side, low=low, high=high):
            top = None
            for first in range(0, high, BLOCK):
                span = slice(first, first + BLOCK)
                made = (
                    nn(key_rows[h // GROUP, span, :], query[head_rows(h + g), low:high])
                    + bias[span, :]
                )
                scores[side, span, :] = made
                best = jnp.max(made.reshape(BLOCK // 8, 8, BLOCK), axis=0)
                top = best if top is None else jnp.maximum(top, best)
            return jnp.max(top, axis=0, keepdims=True)

        def blend(h, side, top, low=low, high=high, kept=kept):
            for first in range(0, high, BLOCK):
                span = slice(first, first + BLOCK)
                kept[h, span, :] = jnp.exp(scores[side, span, :] - top).astype(bf16)
            made = nn(value_aug[h // GROUP, :, :high], kept[h])
            scale = 1.0 / made[HD : HD + 1]
            mixed_t[head_rows(h + 1), low:high] = (made[:HD] * scale).astype(bf16)
            scales[pl.ds(h, 1), low:high] = scale

        def group(j, top, score=score, blend=blend):
            for member in range(GROUP):
                h = j * GROUP + member
                later = score(jnp.minimum(h + 1, HEADS - 1), (member + 1) % GROUP)
                blend(h, member, top)
                top = later
            return top

        if block < BLOCKS - 1:
            lax.fori_loop(0, KEYS, group, score(0, 0))
        else:
            top = score(0, 0)
            for h in range(HEADS):
                later = score(h + 1, (h + 1) % GROUP) if h + 1 < HEADS else None
                blend(h, h % GROUP, top)
                top = later
        stores.append(copied(kept, chances_out[block], keep_sem.at[block]))
        stores[-1].start()
        for pair in range(QW // 128):
            side = pl.ds(pl.multiple_of((2 * pair + 1 - g) * HD, HD), 128)
            mixed[low:high, pair * 128 : pair * 128 + 128] = mixed_t[side, low:high].T
    last = [
        copied(mixed.at[here], o_own, out_sems.at[7]),
        copied(mixed.at[there], o_send, out_sems.at[8]),
        copied(mixed_t, o_out, out_sems.at[9]),
        copied(scales, scale_out, out_sems.at[10]),
    ]
    for store in last:
        store.start()
    for store in stores + last:
        store.wait()


def attend(adapter, tok_own, *rest):
    rows = tok_own.shape[0]
    length = 2 * rows
    shape = jax.ShapeDtypeStruct
    return pl.pallas_call(
        attend_kernel,
        out_shape=[
            shape((rows, QW), bf16),
            shape((rows, QW), bf16),
            shape((QW, length), bf16),
            shape((KW, length), bf16),
            shape((KW, length), bf16),
            shape(((HEADS + 2) * HD, length), bf16),
            shape((length, D), bf16),
            shape((3 * R, length), bf16),
            shape((R, length), f32),
            shape((HD // 2, length), f32),
            shape((HD // 2, length), f32),
        ]
        + [shape((HEADS, (block + 1) * BLOCK, BLOCK), bf16) for block in range(BLOCKS)],
        in_specs=[SMEM, HBM, ANY, HBM, ANY] + [HBM] * 3 + [VMEM] * 3,
        out_specs=[HBM] * (11 + BLOCKS),
        scratch_shapes=[
            pltpu.VMEM((HEADS, (block + 1) * BLOCK, BLOCK), bf16) for block in range(BLOCKS)
        ]
        + [
            pltpu.VMEM((length, D), bf16),
            pltpu.VMEM((length, AUG), bf16),
            pltpu.VMEM((AUG, SPAN), bf16),
            pltpu.VMEM((128, D), bf16),
            pltpu.VMEM((QW, length), bf16),
            pltpu.VMEM((KW, length), bf16),
            pltpu.VMEM((KW, length), bf16),
            pltpu.VMEM((KEYS, length, HD), bf16),
            pltpu.VMEM((KEYS, HD + R, length), bf16),
            pltpu.VMEM(((HEADS + 2) * HD, length), bf16),
            pltpu.VMEM((length, QW), bf16),
            pltpu.VMEM((GROUP, length, BLOCK), f32),
            pltpu.VMEM((length, BLOCK), f32),
            pltpu.VMEM((HD // 2, length), f32),
            pltpu.VMEM((HD // 2, length), f32),
            pltpu.VMEM((3 * R, length), bf16),
            pltpu.VMEM((R, length), f32),
            pltpu.SemaphoreType.DMA((5,)),
            pltpu.SemaphoreType.DMA((9,)),
            pltpu.SemaphoreType.DMA((11,)),
            pltpu.SemaphoreType.DMA((BLOCKS,)),
        ],
        compiler_params=pltpu.CompilerParams(vmem_limit_bytes=50 << 20),
        cost_estimate=pl.CostEstimate(
            flops=16 * 10**9, bytes_accessed=16 << 20, transcendentals=6 * 10**6
        ),
        name="attend",
    )(adapter, tok_own, *rest)


def normed_back(rows, gain_row, grad):
    scale = lax.rsqrt(jnp.mean(rows * rows, axis=-1, keepdims=True) + epsilon)
    scaled = grad * gain_row
    inside = jnp.mean(rows * scaled, axis=-1, keepdims=True)
    return scale * (scaled - rows * (scale * scale * inside))


def rounded_up(count, unit):
    return -(-count // unit) * unit


def feed_lanes(reps):
    return rounded_up((5 * D + 3 * FF) // reps, 256)


def qkv_lanes(reps):
    return rounded_up((4 * D + 2 * KV) // reps + 1, 128)


def packed(grads, reps, target):
    for rep in range(reps):
        at = 0
        for grad in grads:
            piece = grad.shape[-1] // reps
            share = grad[:, rep * piece : (rep + 1) * piece]
            target[rep * R : (rep + 1) * R, at : at + piece] = share.astype(target.dtype)
            at += piece


def feed_kernel(
    reps,
    adapter,
    o_own_in,
    o_oth_in,
    tok_in,
    cot_in,
    wo_own,
    wo_oth,
    wgu_own,
    wgu_oth,
    wd_own,
    wd_oth,
    a_down,
    lower_t,
    upper_width,
    upper_hidden,
    gains_own,
    gains_oth,
    layer_out,
    grad_middle,
    do_own_out,
    do_oth_out,
    pack_own_out,
    pack_send_out,
    o_own,
    o_oth,
    tok,
    cot,
    do_own,
    do_oth,
    wout,
    wg,
    wu,
    wd,
    at_out,
    at_gu,
    b_out,
    b_down,
    middle,
    normed,
    cot_aug,
    total,
    back,
    result,
    z_gu_t,
    dz_down_t,
    ga_out,
    pack,
    sems,
    o_sems,
    out_sems,
):
    g = lax.axis_index("grp")
    chosen = adapter[0]
    gain = gain_row(g, gains_own, gains_oth, 1)
    steps = FF // TILE
    each = steps // 2
    w_here = pl.ds(pl.multiple_of(g * HALF, 64), HALF)
    w_there = pl.ds(pl.multiple_of((1 - g) * HALF, 64), HALF)

    def column(step):
        owner = jnp.where(step < each, g, 1 - g)
        return owner * (FF // 2) + (step % each) * TILE

    def copies(step, slot):
        at = pl.multiple_of(column(step), TILE)
        gate_at = pl.ds(at, TILE)
        up_at = pl.ds(pl.multiple_of(FF + at, TILE), TILE)
        sem = lambda k: sems.at[slot, k]
        return [
            copied(wgu_own.at[:, gate_at], wg.at[slot, w_here], sem(0)),
            copied(wgu_oth.at[:, gate_at], wg.at[slot, w_there], sem(1)),
            copied(wgu_own.at[:, up_at], wu.at[slot, w_here], sem(2)),
            copied(wgu_oth.at[:, up_at], wu.at[slot, w_there], sem(3)),
            copied(upper_hidden.at[0, chosen, :, gate_at], wg.at[slot, pl.ds(D, R)], sem(4)),
            copied(upper_hidden.at[1, chosen, :, gate_at], wu.at[slot, pl.ds(D + R, R)], sem(5)),
            copied(a_down.at[gate_at], wd.at[slot, :, pl.ds(D, 128)], sem(6)),
        ]

    def down_copy(source, step, slot):
        local = pl.ds(pl.multiple_of((step % each) * TILE, TILE), TILE)
        return copied(source.at[local], wd.at[slot, :, pl.ds(0, D)], sems.at[slot, 7])

    def start(step, slot):
        for copy in copies(step, slot):
            copy.start()

        @pl.when(step < each)
        def _():
            down_copy(wd_own, step, slot).start()

        @pl.when(step >= each)
        def _():
            down_copy(wd_oth, step, slot).start()

    def wait(step, slot):
        for copy in copies(step, slot):
            copy.wait()
        down_copy(wd_own, step, slot).wait()

    for slot in range(2):
        wg[slot, D:, :] = jnp.zeros((128, TILE), bf16)
        wu[slot, D:, :] = jnp.zeros((128, TILE), bf16)
        at_out[slot] = jnp.zeros((128, QW), bf16)
        wout[slot, :HD, :D] = jnp.zeros((HD, D), bf16)
        wout[slot, HALF:, :D] = jnp.zeros((HD, D), bf16)
    for ref in (at_gu, b_out, b_down):
        ref[...] = jnp.zeros_like(ref)
    own_at = pl.multiple_of(g * 512, 128)
    oth_at = pl.multiple_of((1 - g) * 512, 128)
    loads = [
        copied(
            wo_own, wout.at[0, pl.ds(pl.multiple_of(g * HD, HD), HALF), pl.ds(0, D)], o_sems.at[0]
        ),
        copied(
            wo_oth,
            wout.at[1, pl.ds(pl.multiple_of((1 - g) * HD, HD), HALF), pl.ds(0, D)],
            o_sems.at[1],
        ),
        copied(lower_t.at[3, chosen, :, pl.ds(own_at, QW)], at_out.at[0, pl.ds(0, R)], o_sems.at[2]),
        copied(lower_t.at[3, chosen, :, pl.ds(oth_at, QW)], at_out.at[1, pl.ds(0, R)], o_sems.at[3]),
        copied(lower_t.at[4, chosen], at_gu.at[pl.ds(0, R)], o_sems.at[4]),
        copied(lower_t.at[5, chosen], at_gu.at[pl.ds(R, R)], o_sems.at[5]),
        copied(upper_width.at[1, chosen], b_out.at[pl.ds(0, R)], o_sems.at[6]),
        copied(upper_width.at[2, chosen], b_down.at[pl.ds(0, R)], o_sems.at[7]),
        copied(o_own_in, o_own, o_sems.at[8]),
        copied(o_oth_in, o_oth, o_sems.at[9]),
        copied(tok_in, tok, o_sems.at[10]),
        copied(cot_in, cot, o_sems.at[11]),
    ]
    first, second, third = loads[11:] + loads[2:4] + loads[7:8], loads[:2] + loads[8:10], loads[4:7] + loads[10:11]
    for load in first + second + third:
        load.start()
    pack[...] = jnp.zeros_like(pack)
    total[...] = jnp.zeros_like(total)
    back[...] = jnp.zeros_like(back)
    for load in first:
        load.wait()
    cot_aug[:, :D] = cot[...]
    dz_down = nt(cot[...], b_down[...])
    cot_aug[:, D:] = dz_down.astype(bf16)
    dz_down_t[...] = dz_down.T[:R, :].astype(bf16)
    for slot in range(2):
        wout[slot, :, D:] = at_out[slot].T
    for load in second + third:
        load.wait()
    start(0, 0)
    count = tok.shape[0] // 2
    spans = [slice(0, count), slice(count, 2 * count)]
    mades = [nn(o_own[span, :], wout[0]) + nn(o_oth[span, :], wout[1]) for span in spans]
    inner_out = jnp.concatenate([made[:, D:].astype(bf16) for made in mades], axis=0)
    for span, made in zip(spans, mades):
        rows_mid = tok[span, :].astype(f32) + made[:, :D] + nn(inner_out[span, :], b_out[...])
        middle[span, :] = rows_mid
        scale = lax.rsqrt(jnp.mean(rows_mid * rows_mid, axis=-1, keepdims=True) + epsilon)
        normed[span, :D] = (rows_mid * scale * gain).astype(bf16)
    inner_gu = nt(normed[:, :D], at_gu[...])
    normed[:, D:] = inner_gu.astype(bf16)
    z_gu_t[...] = inner_gu.T[: 2 * R, :].astype(bf16)

    def step_body(step, carry):
        slot = step % 2

        @pl.when(step + 1 < steps)
        def _():
            start(step + 1, 1 - slot)

        wait(step, slot)
        parts = []
        for at in range(0, TILE, 256):
            cols = slice(at, at + 256)
            parts.append(
                (
                    nn(normed[...], wg[slot, :, cols]),
                    nn(normed[...], wu[slot, :, cols]),
                    nt(cot_aug[...], wd[slot, cols, :]),
                )
            )
        acts, gates, ups = [], [], []
        for gate, up, grad_active in parts:
            sigmoid = 1.0 / (1.0 + jnp.exp(-gate))
            silu = gate * sigmoid
            acts.append((silu * up).astype(bf16))
            gates.append(
                (grad_active * up * (sigmoid * (1.0 + gate * (1.0 - sigmoid)))).astype(bf16)
            )
            ups.append((grad_active * silu).astype(bf16))
        active = jnp.concatenate(acts, axis=1)
        grad_gate = jnp.concatenate(gates, axis=1)
        grad_up = jnp.concatenate(ups, axis=1)
        total[...] += nn(active, wd[slot])
        back[...] += nt(grad_gate, wg[slot]) + nt(grad_up, wu[slot])
        shares = (
            nn(dz_down_t[...], active),
            nn(z_gu_t[...], grad_gate)[:R],
            nn(z_gu_t[...], grad_up)[R:],
        )
        piece = FF // reps
        base = column(step) // piece
        for index, share in enumerate(shares):
            at = 5 * (D // reps) + index * piece
            for rep in range(TILE // piece):
                target = pl.ds(pl.multiple_of((base + rep) * R, R), R)
                pack[target, at : at + piece] = share[:, rep * piece : (rep + 1) * piece].astype(bf16)
        return carry

    lax.fori_loop(0, steps, step_body, 0)

    inner_down = total[:, D:].astype(bf16)
    result[...] = (middle[...] + total[:, :D] + nn(inner_down, b_down[...])).astype(bf16)
    stores = [copied(result, layer_out, out_sems.at[0])]
    stores[0].start()
    gb_down = nn(total[:, D:].T[:R, :].astype(bf16), cot[...])
    dz_gu = back[:, D:].astype(bf16)
    grad_normed = back[:, :D] + nn(dz_gu, at_gu[...])
    grad = cot[...].astype(f32) + normed_back(middle[...], gain, grad_normed)
    total[:, :D] = grad
    stores.append(copied(total.at[:, pl.ds(0, D)], grad_middle, out_sems.at[1]))
    stores[1].start()
    branch = normed
    ga_gu = nn(back[:, D:].T[: 2 * R, :].astype(bf16), normed[:, :D])
    branch[:, :D] = grad.astype(bf16)
    dz_out = nt(branch[:, :D], b_out[...])
    branch[:, D:] = dz_out.astype(bf16)
    dz_out_t = dz_out.T[:R, :].astype(bf16)
    do_oth[...] = nt(wout[1], branch[...]).astype(bf16)
    stores.append(copied(do_oth, do_oth_out, out_sems.at[2]))
    stores[-1].start()
    do_own[...] = nt(wout[0], branch[...]).astype(bf16)
    stores.append(copied(do_own, do_own_out, out_sems.at[3]))
    stores[-1].start()
    gb_out = nn(inner_out.astype(f32).T[:R, :].astype(bf16), branch[:, :D])
    ga_out[...] = jnp.zeros_like(ga_out)
    ga_out[:, pl.ds(own_at, QW)] += nn(dz_out_t, o_own[...])
    ga_out[:, pl.ds(oth_at, QW)] += nn(dz_out_t, o_oth[...])
    packed([ga_out[...], ga_gu[:R], ga_gu[R:], gb_out, gb_down], reps, pack)
    half = pack.shape[1] // 2
    for index, (side, target) in enumerate(((g, pack_own_out), (1 - g, pack_send_out))):
        source = pack.at[:, pl.ds(pl.multiple_of(side * half, 128), half)]
        stores.append(copied(source, target, out_sems.at[4 + index]))
        stores[-1].start()
    for store in stores:
        store.wait()


def feed(reps, *args):
    rows = args[3].shape[0]
    half = feed_lanes(reps) // 2
    shape = jax.ShapeDtypeStruct
    return pl.pallas_call(
        functools.partial(feed_kernel, reps),
        out_shape=[
            shape((rows, D), bf16),
            shape((rows, D), f32),
            shape((QW, rows), bf16),
            shape((QW, rows), bf16),
            shape((reps * R, half), bf16),
            shape((reps * R, half), bf16),
        ],
        in_specs=[SMEM, HBM, ANY] + [HBM] * 12 + [VMEM] * 2,
        out_specs=[HBM] * 6,
        scratch_shapes=[
            pltpu.VMEM((rows, QW), bf16),
            pltpu.VMEM((rows, QW), bf16),
            pltpu.VMEM((rows, D), bf16),
            pltpu.VMEM((rows, D), bf16),
            pltpu.VMEM((QW, rows), bf16),
            pltpu.VMEM((QW, rows), bf16),
            pltpu.VMEM((2, QW, AUG), bf16),
            pltpu.VMEM((2, AUG, TILE), bf16),
            pltpu.VMEM((2, AUG, TILE), bf16),
            pltpu.VMEM((2, TILE, AUG), bf16),
            pltpu.VMEM((2, 128, QW), bf16),
            pltpu.VMEM((128, D), bf16),
            pltpu.VMEM((128, D), bf16),
            pltpu.VMEM((128, D), bf16),
            pltpu.VMEM((rows, D), f32),
            pltpu.VMEM((rows, AUG), bf16),
            pltpu.VMEM((rows, AUG), bf16),
            pltpu.VMEM((rows, AUG), f32),
            pltpu.VMEM((rows, AUG), f32),
            pltpu.VMEM((rows, D), bf16),
            pltpu.VMEM((2 * R, rows), bf16),
            pltpu.VMEM((R, rows), bf16),
            pltpu.VMEM((R, D), f32),
            pltpu.VMEM((reps * R, 2 * half), bf16),
            pltpu.SemaphoreType.DMA((2, 8)),
            pltpu.SemaphoreType.DMA((12,)),
            pltpu.SemaphoreType.DMA((6,)),
        ],
        compiler_params=pltpu.CompilerParams(vmem_limit_bytes=44 << 20),
        cost_estimate=pl.CostEstimate(
            flops=30 * 10**9, bytes_accessed=36 << 20, transcendentals=2 * 10**6
        ),
        name="feed",
    )(*args)


def attend_back_kernel(
    reps,
    adapter,
    do_own,
    do_oth,
    o_in,
    normed,
    upper_width,
    upper_keys,
    query_in,
    k_in,
    v_in,
    zt_in,
    scale_in,
    cos_in,
    sin_in,
    pack_own_in,
    pack_oth_in,
    *refs,
):
    attend_back_body(
        reps,
        adapter,
        do_own,
        do_oth,
        o_in,
        normed,
        upper_width,
        upper_keys,
        query_in,
        k_in,
        v_in,
        zt_in,
        scale_in,
        cos_in,
        sin_in,
        pack_own_in,
        pack_oth_in,
        refs[:BLOCKS],
        refs[BLOCKS + 3 : 2 * BLOCKS + 3],
        *refs[BLOCKS : BLOCKS + 3],
        *refs[2 * BLOCKS + 3 :],
    )


def attend_back_body(
    reps,
    adapter,
    do_own,
    do_oth,
    o_in,
    normed,
    upper_width,
    upper_keys,
    query_in,
    k_in,
    v_in,
    zt_in,
    scale_in,
    cos_in,
    sin_in,
    pack_own_in,
    pack_oth_in,
    chances_in,
    chances,
    dy_out,
    part_out,
    exchange_out,
    query,
    key_t,
    value_t,
    zt,
    scales,
    cosine,
    sine,
    pack_own,
    pack_oth,
    exchange,
    grad_o,
    mixed_t,
    n_rows,
    weight,
    value_rows,
    delta,
    dq,
    dk,
    dv,
    dy_t,
    dy,
    grad_scores,
    gb_q,
    gb_kv,
    pack,
    sems,
    b_sems,
    out_sem,
    keep_sem,
):
    g = lax.axis_index("grp")
    chosen = adapter[0]
    length = query.shape[1]
    rows = length // 2
    here = pl.ds(pl.multiple_of(g * rows, 128), rows)
    there = pl.ds(pl.multiple_of((1 - g) * rows, 128), rows)
    weight[...] = jnp.zeros_like(weight)
    early = [
        copied(k_in, key_t, sems.at[0]),
        copied(v_in, value_t, sems.at[1]),
    ]
    loads = [
        copied(do_own, grad_o.at[:, here], sems.at[2]),
        copied(do_oth, grad_o.at[:, there], sems.at[3]),
        copied(o_in, mixed_t, sems.at[4]),
        copied(query_in, query, sems.at[5]),
        copied(scale_in, scales, sems.at[6]),
    ]
    late = [
        copied(cos_in, cosine, sems.at[7]),
        copied(sin_in, sine, sems.at[8]),
        copied(normed, n_rows, sems.at[9]),
        copied(zt_in, zt, sems.at[10]),
        copied(pack_own_in, pack_own, sems.at[11]),
        copied(pack_oth_in, pack_oth, sems.at[12]),
    ] + upper_loads(g, chosen, upper_width, upper_keys, weight, 0, b_sems)
    kept = [
        copied(chances_in[block], chances[block], keep_sem.at[block]) for block in range(BLOCKS)
    ]
    for load in early + loads:
        load.start()
    kept[0].start()
    dk[...] = jnp.zeros_like(dk)
    dv[...] = jnp.zeros_like(dv)
    dy_t[...] = jnp.zeros_like(dy_t)
    for load in early:
        load.wait()
    for j in range(KEYS):
        value_rows[j] = value_t[head_rows(j + g), :].T
    for load in loads:
        load.wait()
    for load in kept[1:] + late:
        load.start()
    for h in range(HEADS):
        scaled = grad_o[head_rows(h + g), :].astype(f32) * scales[h : h + 1, :]
        product = scaled * mixed_t[(h + 1) * HD : (h + 2) * HD, :].astype(f32)
        delta[h : h + 1, :] = jnp.sum(product, axis=0, keepdims=True)
        grad_o[head_rows(h + g), :] = scaled.astype(bf16)

    for block in range(length // BLOCK):
        low, high = block * BLOCK, (block + 1) * BLOCK
        found = chances[block]
        kept[block].wait()

        def score(h, side, low=low, high=high, found=found):
            deltas = delta[pl.ds(h, 1), low:high]
            for first in range(0, high, BLOCK):
                span = slice(first, first + BLOCK)
                grad = nn(value_rows[h // GROUP, span, :], grad_o[head_rows(h + g), low:high])
                chance = found[h, span, :].astype(f32)
                grad_scores[side, span, :] = (chance * (grad - deltas)).astype(bf16)

        def spread(h, side, low=low, high=high, found=found):
            dq[h, :, low:high] = nn(
                key_t[head_rows(h // GROUP + g), :high], grad_scores[side, :high, :]
            )
            return (
                nt(grad_o[head_rows(h + g), low:high], found[h]),
                nt(query[head_rows(h + g), low:high], grad_scores[side, :high, :]),
            )

        def group(j, carry, high=high, score=score, spread=spread):
            sums = []
            for member in range(GROUP):
                h = j * GROUP + member
                score(jnp.minimum(h + 1, HEADS - 1), (member + 1) % GROUP)
                sums.append(spread(h, member))
            dv[j, :, :high] += sums[0][0] + sums[1][0] + sums[2][0]
            dk[j, :, :high] += sums[0][1] + sums[1][1] + sums[2][1]
            return carry

        score(0, 0)
        lax.fori_loop(0, KEYS, group, 0)

    for load in late:
        load.wait()
    back_sine = -sine[...]
    for h in range(HEADS):
        dy_t[(h + 1) * HD : (h + 2) * HD, :] = (
            turned(dq[h], cosine[...], back_sine) * HD**-0.5
        ).astype(bf16)
    key_base = (HEADS + 2) * HD
    value_base = key_base + (KEYS + 2) * HD
    for j in range(KEYS):
        at = key_base + (j + 1) * HD
        dy_t[at : at + HD, :] = turned(dk[j], cosine[...], back_sine).astype(bf16)
        at = value_base + (j + 1) * HD
        dy_t[at : at + HD, :] = dv[j].astype(bf16)
    for base, count, to in ((0, QW, 0), (key_base, KW, QW), (value_base, KW, QW + KW)):
        for at in range(0, count, 128):
            side = pl.ds(pl.multiple_of(base + at + (1 - g) * HD, HD), 128)
            dy[:, to + at : to + at + 128] = dy_t[side, :].T
    inner = nt(dy[:, :SPAN], weight[...])
    dy[:, SPAN:] = inner.astype(bf16)
    dy_stores = [
        copied(dy.at[place], target, out_sem.at[index])
        for place, target, index in ((there, part_out, 0), (here, dy_out, 1))
    ]
    for copy in dy_stores:
        copy.start()
    gb = nn(zt[...], dy[:, :SPAN])
    gb_q[...] = jnp.zeros_like(gb_q)
    gb_kv[...] = jnp.zeros_like(gb_kv)
    gb_q[:, pl.ds(pl.multiple_of(g * 512, 128), QW)] = gb[:R, :QW]
    for index in range(2):
        gb_kv[index, :, pl.ds(pl.multiple_of(g * 128, 128), KW)] = gb[
            (index + 1) * R : (index + 2) * R, QW + index * KW : QW + (index + 1) * KW
        ]
    ga = nn(inner.T[: 3 * R, :].astype(bf16), n_rows[...])
    pack[...] = jnp.zeros_like(pack)
    packed(
        [ga[:R], ga[R : 2 * R], ga[2 * R :], gb_q[...], gb_kv[0], gb_kv[1]],
        reps,
        pack,
    )
    half = pack_own.shape[1]
    width = pack.shape[1]
    exchange[:, :half] = (pack_own[...].astype(f32) + pack_oth[...].astype(f32)).astype(bf16)
    exchange[:, half:] = jnp.where(
        lanes(pack.shape) == width - 1, chosen.astype(f32), pack[...].astype(f32)
    ).astype(bf16)
    last = copied(exchange, exchange_out, out_sem.at[2])
    last.start()
    for copy in (*dy_stores, last):
        copy.wait()


def attend_back(reps, *args):
    rows = args[1].shape[1]
    length = 2 * rows
    half = feed_lanes(reps) // 2
    width = qkv_lanes(reps)
    shape = jax.ShapeDtypeStruct
    return pl.pallas_call(
        functools.partial(attend_back_kernel, reps),
        out_shape=[
            shape((rows, AUG), bf16),
            shape((rows, AUG), bf16),
            shape((reps * R, half + width), bf16),
        ],
        in_specs=[SMEM, HBM, ANY] + [HBM] * 12 + [ANY] + [HBM] * BLOCKS,
        out_specs=[HBM] * 3,
        scratch_shapes=[
            pltpu.VMEM((HEADS, (block + 1) * BLOCK, BLOCK), bf16) for block in range(BLOCKS)
        ]
        + [
            pltpu.VMEM((QW, length), bf16),
            pltpu.VMEM((KW, length), bf16),
            pltpu.VMEM((KW, length), bf16),
            pltpu.VMEM((3 * R, length), bf16),
            pltpu.VMEM((R, length), f32),
            pltpu.VMEM((HD // 2, length), f32),
            pltpu.VMEM((HD // 2, length), f32),
            pltpu.VMEM((reps * R, half), bf16),
            pltpu.VMEM((reps * R, half), bf16),
            pltpu.VMEM((reps * R, half + width), bf16),
            pltpu.VMEM((QW, length), bf16),
            pltpu.VMEM(((HEADS + 2) * HD, length), bf16),
            pltpu.VMEM((length, D), bf16),
            pltpu.VMEM((128, SPAN), bf16),
            pltpu.VMEM((KEYS, length, HD), bf16),
            pltpu.VMEM((R, length), f32),
            pltpu.VMEM((HEADS, HD, length), f32),
            pltpu.VMEM((KEYS, HD, length), f32),
            pltpu.VMEM((KEYS, HD, length), f32),
            pltpu.VMEM(((HEADS + 2 * KEYS + 6) * HD, length), bf16),
            pltpu.VMEM((length, AUG), bf16),
            pltpu.VMEM((GROUP, length, BLOCK), bf16),
            pltpu.VMEM((R, D), f32),
            pltpu.VMEM((2, R, KV), f32),
            pltpu.VMEM((reps * R, width), bf16),
            pltpu.SemaphoreType.DMA((16,)),
            pltpu.SemaphoreType.DMA((9,)),
            pltpu.SemaphoreType.DMA((4,)),
            pltpu.SemaphoreType.DMA((BLOCKS,)),
        ],
        compiler_params=pltpu.CompilerParams(vmem_limit_bytes=50 << 20),
        cost_estimate=pl.CostEstimate(
            flops=24 * 10**9, bytes_accessed=20 << 20, transcendentals=6 * 10**6
        ),
        name="attend_back",
    )(*args)


def finish_kernel(
    adapter,
    dy_in,
    qkv_own,
    qkv_oth,
    lower_t,
    tok_in,
    gains_own,
    gains_oth,
    part_in,
    middle_in,
    out,
    dy,
    part,
    tok,
    grad_middle,
    weight,
    weight_oth,
    maps,
    result,
    sems,
    w_sems,
    out_sem,
):
    g = lax.axis_index("grp")
    chosen = adapter[0]
    maps[...] = jnp.zeros_like(maps)
    loads = qkv_loads(g, g, qkv_own, qkv_oth, weight, w_sems.at[0])
    loads += qkv_loads(g, 1 - g, qkv_own, qkv_oth, weight_oth, w_sems.at[1])
    for index, (source, target) in enumerate(
        ((dy_in, dy), (part_in, part), (tok_in, tok), (middle_in, grad_middle))
    ):
        loads.append(copied(source, target, sems.at[index]))
    for index in range(3):
        loads.append(
            copied(lower_t.at[index, chosen], maps.at[pl.ds(index * R, R)], sems.at[5 + index])
        )
    for load in loads:
        load.start()
    gain = gain_row(g, gains_own, gains_oth, 0)
    for load in loads:
        load.wait()

    def half(index, carry):
        count = tok.shape[0] // 2
        span = pl.ds(pl.multiple_of(index * count, 128), count)
        inner = dy[span, SPAN:].astype(f32) + part[span, SPAN:].astype(f32)
        grad = (
            nt(dy[span, :SPAN], weight[...])
            + nt(part[span, :SPAN], weight_oth[...])
            + nn(inner.astype(bf16), maps[...])
        )
        result[span, :] = (
            grad_middle[span, :] + normed_back(tok[span, :].astype(f32), gain, grad)
        ).astype(bf16)
        return carry

    lax.fori_loop(0, 2, half, 0)
    store = copied(result, out, out_sem.at[0])
    store.start()
    store.wait()


def finish(*args):
    rows = args[1].shape[0]
    return pl.pallas_call(
        finish_kernel,
        out_shape=jax.ShapeDtypeStruct((rows, D), bf16),
        in_specs=[SMEM] + [HBM] * 5 + [VMEM] * 2 + [ANY, HBM],
        out_specs=HBM,
        scratch_shapes=[
            pltpu.VMEM((rows, AUG), bf16),
            pltpu.VMEM((rows, AUG), bf16),
            pltpu.VMEM((rows, D), bf16),
            pltpu.VMEM((rows, D), f32),
            pltpu.VMEM((D, SPAN), bf16),
            pltpu.VMEM((D, SPAN), bf16),
            pltpu.VMEM((128, D), bf16),
            pltpu.VMEM((rows, D), bf16),
            pltpu.SemaphoreType.DMA((8,)),
            pltpu.SemaphoreType.DMA((2, 6)),
            pltpu.SemaphoreType.DMA((1,)),
        ],
        compiler_params=pltpu.CompilerParams(vmem_limit_bytes=50 << 20),
        cost_estimate=pl.CostEstimate(
            flops=4 * 10**9, bytes_accessed=10 << 20, transcendentals=0
        ),
        name="finish",
    )(*args)


def collect_kernel(source, keep, send, received, sem):
    load = copied(source, received, sem.at[0])
    load.start()
    load.wait()
    g = lax.axis_index("grp")
    count, width = received.shape
    quota = NAD // 2
    label = received[:, width - 1 :].astype(f32)
    lane = lanes((count, NAD * R))
    row = lax.broadcasted_iota(jnp.int32, (count, NAD * R), 0)
    picks = ((lane // R).astype(f32) == label) & (lane % R == row % R)
    sums = tn(picks.astype(f32).astype(bf16), received[...])
    first = g == 0
    for adapter in range(quota):
        low = sums[adapter * R : (adapter + 1) * R]
        high = sums[(quota + adapter) * R : (quota + adapter + 1) * R]
        keep[adapter] = jnp.where(first, low, high)
        send[adapter] = jnp.where(first, high, low)


def collect(received):
    shape = jax.ShapeDtypeStruct((NAD // 2, R, received.shape[1]), f32)
    return pl.pallas_call(
        collect_kernel,
        out_shape=[shape, shape],
        in_specs=[ANY],
        out_specs=[VMEM] * 2,
        scratch_shapes=[
            pltpu.VMEM(received.shape, bf16),
            pltpu.SemaphoreType.DMA((1,)),
        ],
        compiler_params=pltpu.CompilerParams(vmem_limit_bytes=8 << 20),
        cost_estimate=pl.CostEstimate(flops=10**8, bytes_accessed=2 << 20, transcendentals=0),
        name="collect",
    )(received)


def deliver_kernel(reps, keep, other, lower, down, width, keys, hidden, feeds, qkvs):
    g = lax.axis_index("grp")
    half = feeds.shape[-1] // 2
    feeds[:, :, pl.ds(pl.multiple_of(g * half, 128), half)] = keep[:, :, :half]
    feeds[:, :, pl.ds(pl.multiple_of((1 - g) * half, 128), half)] = other[:, :, :half]
    qkvs[...] = keep[:, :, half:] + other[:, :, half:]
    piece, tall, short = D // reps, FF // reps, KV // reps
    for index in range(3):
        lower[index] = qkvs[:, :, index * piece : (index + 1) * piece]
        lower[3 + index] = feeds[:, :, index * piece : (index + 1) * piece]
    width[0] = qkvs[:, :, 3 * piece : 4 * piece]
    width[1] = feeds[:, :, 3 * piece : 4 * piece]
    width[2] = feeds[:, :, 4 * piece : 5 * piece]
    for index in range(2):
        at = 4 * piece + index * short
        keys[index] = qkvs[:, :, at : at + short]
        at = 5 * piece + (1 + index) * tall
        hidden[index] = feeds[:, :, at : at + tall]
    down[...] = feeds[:, :, 5 * piece : 5 * piece + tall]


def deliver(reps, keep, other):
    quota = NAD // 2
    shape = lambda *dims: jax.ShapeDtypeStruct(dims, f32)
    return pl.pallas_call(
        functools.partial(deliver_kernel, reps),
        out_shape=[
            shape(6, quota, R, D // reps),
            shape(quota, R, FF // reps),
            shape(3, quota, R, D // reps),
            shape(2, quota, R, KV // reps),
            shape(2, quota, R, FF // reps),
        ],
        in_specs=[VMEM] * 2,
        out_specs=[VMEM] * 5,
        scratch_shapes=[
            pltpu.VMEM((quota, R, feed_lanes(reps)), f32),
            pltpu.VMEM((quota, R, qkv_lanes(reps)), f32),
        ],
        compiler_params=pltpu.CompilerParams(vmem_limit_bytes=8 << 20),
        cost_estimate=pl.CostEstimate(flops=10**6, bytes_accessed=1 << 20, transcendentals=0),
        name="deliver",
    )(keep, other)


def per_device(
    tokens,
    cotangent,
    segment_ids,
    adapter_ids,
    norm_gains,
    frozen_qkv,
    frozen_out,
    frozen_gate_up,
    frozen_down,
    lower_mats,
    lower_down,
    upper_width,
    upper_keys,
    upper_hidden,
):
    reps = lax.axis_size("rep")
    chosen = adapter_ids[0]
    first = lax.axis_index("grp") == 0
    swap = lambda value: lax.ppermute(value, "grp", SWAP)

    tok_own = tokens[0]
    tok_oth = swap(tok_own)
    qkv_oth = swap(frozen_qkv)
    gains_oth = swap(norm_gains)
    a_down = jnp.pad(
        lax.dynamic_index_in_dim(lower_down, chosen, 0, keepdims=False), ((0, 0), (0, 128 - R))
    )
    tok_oth, qkv_oth, gains_oth, a_down, wo, wgu, wd = lax.optimization_barrier(
        (tok_oth, qkv_oth, gains_oth, a_down, frozen_out, frozen_gate_up, frozen_down)
    )
    wo_oth = swap(wo)
    wgu_oth = swap(wgu)
    wd_oth = swap(wd)

    lower_t = lower_mats.transpose(0, 1, 3, 2)
    gains = (norm_gains, gains_oth)

    (o_own, o_send, query, key_t, value_t, mixed_t, normed, zt, scales, cosine, sine, *chances) = (
        attend(
            adapter_ids,
            tok_own,
            tok_oth,
            frozen_qkv,
            qkv_oth,
            lower_t,
            upper_width,
            upper_keys,
            *gains,
            segment_ids,
        )
    )
    o_oth = swap(o_send)
    layer_out, grad_middle, do_own, do_send, pack_own, pack_send = feed(
        reps,
        adapter_ids,
        o_own,
        o_oth,
        tok_own,
        cotangent[0],
        frozen_out,
        wo_oth,
        frozen_gate_up,
        wgu_oth,
        frozen_down,
        wd_oth,
        a_down,
        lower_t,
        upper_width,
        upper_hidden,
        *gains,
    )
    do_oth = swap(do_send)
    pack_oth = swap(pack_send)
    dy, dy_send, exchange = attend_back(
        reps,
        adapter_ids,
        do_own,
        do_oth,
        mixed_t,
        normed,
        upper_width,
        upper_keys,
        query,
        key_t,
        value_t,
        zt,
        scales,
        cosine,
        sine,
        pack_own,
        pack_oth,
        *chances,
    )
    received = lax.all_to_all(exchange, "rep", 0, 0, tiled=True)
    input_grad = finish(
        adapter_ids,
        dy,
        frozen_qkv,
        qkv_oth,
        lower_t,
        tok_own,
        *gains,
        swap(dy_send),
        grad_middle,
    )
    received, input_grad = lax.optimization_barrier((received, input_grad))
    keep, send = collect(received)
    lower, down, width, keys, hidden = deliver(reps, keep, swap(send))
    return (
        layer_out[None],
        input_grad[None],
        lower.transpose(0, 1, 3, 2),
        down.transpose(0, 2, 1),
        width,
        keys,
        hidden,
    )


def solution(mesh):
    return jax.shard_map(
        per_device,
        mesh=mesh,
        in_specs=(
            P("rep", "grp", None),
            P("rep", "grp", None),
            P("rep", None),
            P("rep"),
            P(None, "grp"),
            P("grp", None),
            P("grp", None),
            P("grp", None),
            P("grp", None),
            P(),
            P(),
            P(),
            P(),
            P(),
        ),
        out_specs=(
            P("rep", "grp", None),
            P("rep", "grp", None),
            P(None, "grp", "rep", None),
            P("grp", "rep", None),
            P(None, "grp", None, "rep"),
            P(None, "grp", None, "rep"),
            P(None, "grp", None, "rep"),
        ),
        check_vma=False,
    )
```
